32 devices in a mesh: dp: 8 (over z, x), seq: 4 (over y, core).
Axes of the slice: x: 2, y: 2, z: 4, core: 2. Of those that a mesh axis runs over, the one named last changes fastest.
Arguments:
- inputs: bfloat16 [16, 2048, 768], P('dp', 'seq'), may hold values from -6 to 6
- lengths: int32 [16], P('dp'), may hold values from 256 to 2048
- first_gain: float32 [768], replicated, may hold values from 0.5 to 1.5
- first_shift: float32 [768], replicated, may hold values from -2 to 2
- query_weight: bfloat16 [768, 768], replicated, may hold values from -0.21875 to 0.21875
- query_bias: float32 [768], replicated, may hold values from -1.5 to 1.5
- key_weight: bfloat16 [768, 768], replicated, may hold values from -0.21875 to 0.21875
- value_weight: bfloat16 [768, 768], replicated, may hold values from -0.21875 to 0.21875
- value_bias: float32 [768], replicated, may hold values from -0.25 to 0.25
- output_weight: bfloat16 [768, 768], replicated, may hold values from -4 to 4
- output_bias: float32 [768], replicated, may hold values from -2 to 2
- second_gain: float32 [768], replicated, may hold values from 0.5 to 1.5
- second_shift: float32 [768], replicated, may hold values from -2 to 2
- inner_weight: bfloat16 [768, 3072], replicated, may hold values from -0.21875 to 0.21875
- inner_bias: float32 [3072], replicated, may hold values from -2 to 2
- outer_weight: bfloat16 [3072, 768], replicated, may hold values from -0.109375 to 0.109375
- outer_bias: float32 [768], replicated, may hold values from -2 to 2
- cotangent: bfloat16 [16, 2048, 768], P('dp', 'seq'), may hold values from -6 to 6
Outputs:
- result: bfloat16 [16, 2048, 768], P('dp', 'seq')
- grad_inputs: bfloat16 [16, 2048, 768], P('dp', 'seq')
- grad_first_gain: float32 [768], replicated
- grad_first_shift: float32 [768], replicated
- grad_query_weight: float32 [768, 768], P('dp')
- grad_query_bias: float32 [768], replicated
- grad_key_weight: float32 [768, 768], P('dp')
- grad_value_weight: float32 [768, 768], P('dp')
- grad_value_bias: float32 [768], replicated
- grad_output_weight: float32 [768, 768], P('dp')
- grad_output_bias: float32 [768], replicated
- grad_second_gain: float32 [768], replicated
- grad_second_shift: float32 [768], replicated
- grad_inner_weight: float32 [768, 3072], P('dp')
- grad_inner_bias: float32 [3072], replicated
- grad_outer_weight: float32 [3072, 768], P('dp')
- grad_outer_bias: float32 [768], replicated
- stream_scale: float32 [], replicated
- attention_scale: float32 [], replicated
- feedforward_scale: float32 [], replicated
The draws below stay inside these ranges and needn't reach their ends.
All inputs are finite; a program needn't handle non-finite values.
Results may differ from the reference program's by a relative error of at most 0.012.
Values may be sent and summed in bfloat16 or wider, within the bound.
A program may use at most 256 MiB of HBM per device.

```python
import math
import jax
import jax.numpy as jnp
from jax import lax

D = 768
FF = 3072
HEADS = 12
HEAD_DIM = 64
LEN = 2048
ROWS = 16


def draw_lengths(key, part):
    row_ids = jnp.arange(ROWS, dtype=jnp.int32)
    floor_len = LEN // 8
    lowest = LEN // 4
    ramp = LEN - (LEN - lowest) * row_ids // max(ROWS - 1, 1)
    jitter = jax.random.randint(key, (ROWS,), 0, floor_len + 1, dtype=jnp.int32)
    drawn = jnp.clip(ramp - jitter, floor_len, LEN)
    drawn = jnp.where(row_ids == ROWS - 1, floor_len, drawn)
    return jnp.where(row_ids == 0, LEN, drawn).astype(jnp.int32)


def block_scale(stream_key, dims, split, low, largest):
    def one(axis_at, shards_of):
        draws = jax.random.uniform(jax.random.fold_in(jax.random.fold_in(stream_key, 6), axis_at), (shards_of,), jnp.float32, low / len(split), largest / len(split))
        return jnp.repeat(jnp.exp(draws), dims[axis_at] // shards_of).reshape((-1,) + (1,) * (len(dims) - axis_at - 1))

    factor_of = one(*split[0])
    for cut in split[1:]:
        factor_of = factor_of * one(*cut)
    return factor_of


def bell_draw(key, shape, scale, most, cuts=(), kind=jnp.bfloat16):
    factor_of = block_scale(key, shape, cuts, -0.22, 0.18) if cuts else 1.0
    array = jax.random.normal(key, shape, jnp.float32) * scale * factor_of
    return jnp.minimum(jnp.maximum(array, -most), most).astype(kind)


def setup_inputs(seed: int = 0) -> dict:
    keys = jax.random.split(jax.random.key(seed), 19)
    inputs = bell_draw(keys[0], (ROWS, LEN, D), 1.0, 6.0, ((0, 8), (1, 4)))
    lengths = draw_lengths(jax.random.fold_in(keys[18], 71), 0)
    first_gain = jnp.clip(1.0 + 0.1 * jax.random.normal(keys[2], (D,), jnp.float32), 0.5, 1.5)
    first_shift = bell_draw(keys[3], (D,), 0.3, 2.0, (), jnp.float32)
    query_weight = bell_draw(keys[4], (D, D), D ** -0.5, 0.21875)
    query_bias = bell_draw(keys[5], (D,), 0.2, 1.5, (), jnp.float32)
    key_weight = bell_draw(keys[6], (D, D), D ** -0.5, 0.21875)
    value_weight = bell_draw(keys[7], (D, D), D ** -0.5, 0.21875)
    value_bias = bell_draw(keys[8], (D,), 0.03, 0.25, (), jnp.float32)
    output_weight = bell_draw(keys[9], (D, D), (max(1, D // 384)) ** -0.5, 4.0)
    output_bias = bell_draw(keys[10], (D,), 0.3, 2.0, (), jnp.float32)
    second_gain = jnp.clip(1.0 + 0.1 * jax.random.normal(keys[11], (D,), jnp.float32), 0.5, 1.5)
    second_shift = bell_draw(keys[12], (D,), 0.3, 2.0, (), jnp.float32)
    inner_weight = bell_draw(keys[13], (D, FF), D ** -0.5, 0.21875)
    inner_bias = bell_draw(keys[14], (FF,), 0.3, 2.0, (), jnp.float32)
    outer_weight = bell_draw(keys[15], (FF, D), FF ** -0.5, 0.109375)
    outer_bias = bell_draw(keys[16], (D,), 0.3, 2.0, (), jnp.float32)
    cotangent = bell_draw(keys[17], (ROWS, LEN, D), 1.0, 6.0, ((0, 8), (1, 4)))
    return {"inputs": inputs, "lengths": lengths, "first_gain": first_gain, "first_shift": first_shift, "query_weight": query_weight, "query_bias": query_bias, "key_weight": key_weight, "value_weight": value_weight, "value_bias": value_bias, "output_weight": output_weight, "output_bias": output_bias, "second_gain": second_gain, "second_shift": second_shift, "inner_weight": inner_weight, "inner_bias": inner_bias, "outer_weight": outer_weight, "outer_bias": outer_bias, "cotangent": cotangent}


EPSILON = 1e-12
NEGATIVE = -1e+30

@jax.custom_vjp
def low(v):
    return lax.optimization_barrier(v.astype(jnp.bfloat16)).astype(jnp.float32)

@jax.custom_vjp
def low_back(v):
    return v

def low_keep(v):
    return (low(v), None)

def low_pass(kept, grad):
    return (grad,)

def back_keep(v):
    return (v, None)

def back_low(kept, grad):
    return (low(grad),)
low.defvjp(low_keep, low_pass)
low_back.defvjp(back_keep, back_low)

def norm_apply(values, gain_vec, shift_vec):
    average = lax.optimization_barrier(jnp.mean(values, axis=-1, keepdims=True))
    centered = values - average
    spread = lax.optimization_barrier(jnp.mean(centered * centered, axis=-1, keepdims=True))
    return centered * lax.rsqrt(spread + EPSILON) * gain_vec + shift_vec

def exact_gelu(values):
    return jax.nn.gelu(values, approximate=False)

def product(left_side, right_side):
    return jnp.dot(left_side, right_side, precision=lax.Precision.HIGHEST)

def layer(params, rows_in, key_valid):
    first_gain, first_shift, query_weight, query_bias, key_weight, value_weight, value_bias, output_weight, output_bias, second_gain, second_shift, inner_weight, inner_bias, outer_weight, outer_bias = params
    batch_rows = rows_in.shape[0]
    keep_rows = key_valid[..., None].astype(rows_in.dtype)
    normed_one = low(norm_apply(rows_in, first_gain, first_shift))
    queries = low(low_back(product(normed_one, query_weight) + query_bias))
    keys_all = low(low_back(product(normed_one, key_weight)))
    values_all = low(low_back(product(normed_one, value_weight) + value_bias))
    head_shape = (batch_rows, LEN, HEADS, HEAD_DIM)
    query_heads = queries.reshape(head_shape)
    key_heads = keys_all.reshape(head_shape)
    value_heads = values_all.reshape(head_shape)
    block_rows = min(512, LEN)
    block_count = LEN // block_rows
    score_scale = HEAD_DIM ** (-0.5)
    query_blocks = jnp.moveaxis(query_heads.reshape(batch_rows, block_count, block_rows, HEADS, HEAD_DIM), 1, 0)

    @jax.checkpoint
    def attend(query_blk):
        raw_scores = low_back(jnp.einsum('gqhd,gkhd->ghqk', query_blk, key_heads, precision=lax.Precision.HIGHEST) * score_scale)
        logits = jnp.where(key_valid[:, None, None, :], raw_scores, NEGATIVE)
        probability = low(jax.nn.softmax(logits, axis=-1))
        return jnp.einsum('ghqk,gkhd->gqhd', probability, value_heads, precision=lax.Precision.HIGHEST)
    mixed_blocks = lax.map(attend, query_blocks)
    attended = jnp.moveaxis(mixed_blocks, 0, 1).reshape(batch_rows, LEN, D)
    attended = low(low_back(attended))
    branch_attn = low_back(product(attended, output_weight) + output_bias)
    hidden = rows_in + branch_attn
    normed_two = low(norm_apply(hidden, second_gain, second_shift))
    inner = low_back(product(normed_two, inner_weight) + inner_bias)
    activated = low(exact_gelu(inner))
    branch_ffn = low_back(product(activated, outer_weight) + outer_bias)
    stream = keep_rows * (hidden + branch_ffn)
    stats = (jnp.sum(stream * stream), jnp.sum(keep_rows * branch_attn * branch_attn), jnp.sum(keep_rows * branch_ffn * branch_ffn))
    return (stream, stats)

def reference(inputs, lengths, first_gain, first_shift, query_weight, query_bias, key_weight, value_weight, value_bias, output_weight, output_bias, second_gain, second_shift, inner_weight, inner_bias, outer_weight, outer_bias, cotangent):
    params = (first_gain, first_shift, query_weight.astype(jnp.float32), query_bias, key_weight.astype(jnp.float32), value_weight.astype(jnp.float32), value_bias, output_weight.astype(jnp.float32), output_bias, second_gain, second_shift, inner_weight.astype(jnp.float32), inner_bias, outer_weight.astype(jnp.float32), outer_bias)
    group_rows = math.gcd(ROWS, max(1, 4096 // LEN))
    step_count = ROWS // group_rows
    rows_all = inputs.astype(jnp.float32).reshape(step_count, group_rows, LEN, D)
    cot_all = cotangent.astype(jnp.float32).reshape(step_count, group_rows, LEN, D)
    len_all = lengths.astype(jnp.int32).reshape(step_count, group_rows)
    grads_zero = jax.tree.map(jnp.zeros_like, params)
    stats_zero = jnp.zeros((4,), jnp.float32)

    def scan_step(carry, items):
        grads_acc, stats_acc = carry
        rows_in, cot_rows, row_lens = items
        key_valid = jnp.arange(LEN, dtype=jnp.int32)[None, :] < row_lens[:, None]

        def forward(param_set, rows_x):
            return layer(param_set, rows_x, key_valid)
        stream, back_fn, stats = jax.vjp(forward, params, rows_in, has_aux=True)
        grad_params, grad_rows = back_fn(cot_rows)
        grads_acc = jax.tree.map(jnp.add, grads_acc, grad_params)
        counted = jnp.sum(key_valid.astype(jnp.float32))
        stats_acc = stats_acc + jnp.stack([stats[0], stats[1], stats[2], counted])
        return ((grads_acc, stats_acc), (stream.astype(jnp.bfloat16), grad_rows.astype(jnp.bfloat16)))
    (grads_sum, stats_sum), (streams, grad_rows_all) = lax.scan(scan_step, (grads_zero, stats_zero), (rows_all, cot_all, len_all))
    result = streams.reshape(ROWS, LEN, D)
    grad_inputs = grad_rows_all.reshape(ROWS, LEN, D)
    denominator = stats_sum[3] * D
    stream_scale = jnp.sqrt(stats_sum[0] / denominator)
    attention_scale = jnp.sqrt(stats_sum[1] / denominator)
    feedforward_scale = jnp.sqrt(stats_sum[2] / denominator)
    return (result, grad_inputs, grads_sum[0], grads_sum[1], grads_sum[2], grads_sum[3], grads_sum[4], grads_sum[5], grads_sum[6], grads_sum[7], grads_sum[8], grads_sum[9], grads_sum[10], grads_sum[11], grads_sum[12], grads_sum[13], grads_sum[14], stream_scale, attention_scale, feedforward_scale)
```

```python
import functools

import jax
import jax.numpy as jnp
from jax import lax
from jax.experimental import pallas as pl
from jax.experimental.pallas import tpu as pltpu
from jax.sharding import PartitionSpec as P

HEADS = 12
HEAD_DIM = 64
EPSILON = 1e-12
NEGATIVE = -1e30
PAIR = 2 * HEAD_DIM
NT = ((1,), (1,))
NN = ((1,), (0,))
TN = ((0,), (0,))


def norm_apply(values, gain_vec, shift_vec):
    average = jnp.mean(values, axis=-1, keepdims=True)
    centered = values - average
    spread = jnp.mean(centered * centered, axis=-1, keepdims=True)
    return centered * lax.rsqrt(spread + EPSILON) * gain_vec + shift_vec


def exact_gelu(values):
    return jax.nn.gelu(values, approximate=False)


def dot(left, right, dims):
    return lax.dot_general(left, right, (dims, ((), ())), preferred_element_type=jnp.float32)


def key_valid(info_ref, keys_total):
    spots = lax.broadcasted_iota(jnp.int32, (keys_total, 1), 0)
    blocks = info_ref.shape[0] - 1
    block_len = keys_total // blocks
    places = spots
    for index in range(blocks):
        inside = (spots >= index * block_len) & (spots < (index + 1) * block_len)
        places = jnp.where(inside, spots - index * block_len + info_ref[index + 1], places)
    return places < info_ref[0]


def attend_body(info_ref, q_ref, k_ref, v_ref, out_ref, lse_ref):
    lane = lax.broadcasted_iota(jnp.int32, (1, PAIR), 1)
    scale = jnp.bfloat16(HEAD_DIM ** (-0.5))
    queries = q_ref[...] * scale
    keys = k_ref[...]
    values_t = v_ref[...].T
    valid = key_valid(info_ref, keys.shape[0])
    outs = []
    for head in range(2):
        mine = (lane < HEAD_DIM) if head == 0 else (lane >= HEAD_DIM)
        scores = dot(keys, jnp.where(mine, queries, jnp.zeros_like(queries)), NT)
        scores = jnp.where(valid, scores, NEGATIVE)
        top = jnp.max(scores, axis=0, keepdims=True)
        weights = jnp.exp(scores - top)
        total = jnp.sum(weights, axis=0, keepdims=True)
        mixed = dot(
            values_t[HEAD_DIM * head : HEAD_DIM * (head + 1)], weights.astype(jnp.bfloat16), NN
        )
        outs.append(mixed * (1.0 / total))
        lse_ref[0, head : head + 1, :] = top + jnp.log(total)
    out_ref[...] = jnp.concatenate(outs, axis=0).T.astype(jnp.bfloat16)


def attend(info, queries, keys, values, block):
    tokens, width = queries.shape
    total = keys.shape[0]
    pairs = width // PAIR
    q_spec = pl.BlockSpec((block, PAIR), lambda h, i, n: (i, h))
    k_spec = pl.BlockSpec((total, PAIR), lambda h, i, n: (0, h))
    return pl.pallas_call(
        attend_body,
        grid_spec=pltpu.PrefetchScalarGridSpec(
            num_scalar_prefetch=1,
            grid=(pairs, tokens // block),
            in_specs=[q_spec, k_spec, k_spec],
            out_specs=[q_spec, pl.BlockSpec((1, 2, block), lambda h, i, n: (h, 0, i))],
        ),
        out_shape=[
            jax.ShapeDtypeStruct((tokens, width), jnp.bfloat16),
            jax.ShapeDtypeStruct((pairs, 2, tokens), jnp.float32),
        ],
        compiler_params=pltpu.CompilerParams(vmem_limit_bytes=48 << 20),
        cost_estimate=pl.CostEstimate(
            flops=16 * tokens * total * width, bytes_accessed=1 << 23, transcendentals=0
        ),
        name="attend",
    )(info, queries, keys, values)


def attend_back_body(
    info_ref, q_ref, k_ref, v_ref, do_ref, o_ref, lse_ref, dq_ref, dk_ref, dv_ref, dk_acc, dv_acc
):
    step = pl.program_id(1)
    lane = lax.broadcasted_iota(jnp.int32, (1, PAIR), 1)
    scale = jnp.bfloat16(HEAD_DIM ** (-0.5))
    grad_out = do_ref[...]
    queries = q_ref[...] * scale
    keys = k_ref[...]
    values = v_ref[...]
    product = grad_out.astype(jnp.float32) * o_ref[...].astype(jnp.float32)
    pick = (
        lax.broadcasted_iota(jnp.int32, (8, PAIR), 1) // HEAD_DIM
        == lax.broadcasted_iota(jnp.int32, (8, PAIR), 0)
    ).astype(jnp.float32)
    row_sums = lax.dot_general(
        pick,
        product,
        (NT, ((), ())),
        precision=lax.Precision.HIGHEST,
        preferred_element_type=jnp.float32,
    )
    valid = key_valid(info_ref, keys.shape[0])
    zero = jnp.zeros_like(queries)
    grad_k = 0
    grad_v = 0
    grad_q = 0
    for head in range(2):
        mine = (lane < HEAD_DIM) if head == 0 else (lane >= HEAD_DIM)
        query_h = jnp.where(mine, queries, zero)
        out_h = jnp.where(mine, grad_out, zero)
        scores = jnp.where(valid, dot(keys, query_h, NT), NEGATIVE)
        weights = jnp.exp(scores - lse_ref[0, head : head + 1, :])
        grad_w = dot(values, out_h, NT)
        grad_s = (weights * (grad_w - row_sums[head : head + 1])).astype(jnp.bfloat16)
        grad_v = grad_v + dot(weights.astype(jnp.bfloat16), out_h, NN)
        grad_k = grad_k + dot(grad_s, query_h, NN)
        grad_q_h = dot(grad_s, keys, TN)
        grad_q = grad_q_h if head == 0 else jnp.where(mine, grad_q_h, grad_q)
    dq_ref[...] = (grad_q * (HEAD_DIM ** (-0.5))).astype(jnp.bfloat16)

    @pl.when(step == 0)
    def _():
        dk_acc[...] = grad_k
        dv_acc[...] = grad_v

    @pl.when(step > 0)
    def _():
        dk_acc[...] += grad_k
        dv_acc[...] += grad_v

    @pl.when(step == pl.num_programs(1) - 1)
    def _():
        dk_ref[...] = dk_acc[...].astype(jnp.bfloat16)
        dv_ref[...] = dv_acc[...].astype(jnp.bfloat16)


def attend_back(info, queries, keys, values, grad_out, out, log_sums, block):
    tokens, width = queries.shape
    total = keys.shape[0]
    pairs = width // PAIR
    q_spec = pl.BlockSpec((block, PAIR), lambda h, i, n: (i, h))
    k_spec = pl.BlockSpec((total, PAIR), lambda h, i, n: (0, h))
    return pl.pallas_call(
        attend_back_body,
        grid_spec=pltpu.PrefetchScalarGridSpec(
            num_scalar_prefetch=1,
            grid=(pairs, tokens // block),
            in_specs=[
                q_spec,
                k_spec,
                k_spec,
                q_spec,
                q_spec,
                pl.BlockSpec((1, 2, block), lambda h, i, n: (h, 0, i)),
            ],
            out_specs=[q_spec, k_spec, k_spec],
            scratch_shapes=[pltpu.VMEM((total, PAIR), jnp.float32)] * 2,
        ),
        out_shape=[
            jax.ShapeDtypeStruct((tokens, width), jnp.bfloat16),
            jax.ShapeDtypeStruct((total, width), jnp.bfloat16),
            jax.ShapeDtypeStruct((total, width), jnp.bfloat16),
        ],
        compiler_params=pltpu.CompilerParams(vmem_limit_bytes=48 << 20),
        cost_estimate=pl.CostEstimate(
            flops=40 * tokens * total * width, bytes_accessed=1 << 24, transcendentals=0
        ),
        name="attend_back",
    )(info, queries, keys, values, grad_out, out, log_sums)


def local(
    inputs,
    lengths,
    first_gain,
    first_shift,
    query_weight,
    query_bias,
    key_weight,
    value_weight,
    value_bias,
    output_weight,
    output_bias,
    second_gain,
    second_shift,
    inner_weight,
    inner_bias,
    outer_weight,
    outer_bias,
    cotangent,
):
    groups = lax.axis_size("seq")
    seq_count, local_len, width = inputs.shape
    full_len = local_len * groups
    tokens_here = seq_count * local_len
    place = lax.axis_index("seq")
    half = groups // 2
    row = place // half
    across = [(i, (i + half) % groups) for i in range(groups)]
    beside = [(i, i ^ 1) for i in range(groups)]
    there = lax.rem(place + half, groups)
    near = place + 1 - 2 * lax.rem(place, 2)

    def mine_of(array):
        return lax.dynamic_index_in_dim(array, row, 0, keepdims=False)

    def swap(array):
        return lax.ppermute(
            lax.dynamic_index_in_dim(array, 1 - row, 0, keepdims=False), "seq", across
        )

    def give_back(array):
        own = array[:local_len]
        other = lax.ppermute(array[local_len:], "seq", across)
        return jnp.where(row == 0, jnp.stack([own, other]), jnp.stack([other, own]))

    length = lax.dynamic_index_in_dim(lengths, row, 0, keepdims=False)
    starts = jnp.stack(
        [place, there, near, lax.rem(near + half, groups)]
    ).astype(jnp.int32) * local_len
    info = jnp.concatenate([length[None], starts])
    spots = jnp.concatenate(
        [starts[0] + jnp.arange(local_len, dtype=jnp.int32), starts[1] + jnp.arange(local_len, dtype=jnp.int32)]
    )
    keep_rows = (spots < length).astype(jnp.float32)[:, None]
    own_in = mine_of(inputs)
    far_in = swap(inputs)
    cot = jnp.concatenate([mine_of(cotangent), swap(cotangent)], axis=0)

    def project(rows):
        normed = norm_apply(rows.astype(jnp.float32), first_gain, first_shift).astype(jnp.bfloat16)
        q = (
            jnp.dot(normed, query_weight, preferred_element_type=jnp.float32) + query_bias
        ).astype(jnp.bfloat16)
        k = jnp.dot(normed, key_weight, preferred_element_type=jnp.float32).astype(jnp.bfloat16)
        v = (
            jnp.dot(normed, value_weight, preferred_element_type=jnp.float32) + value_bias
        ).astype(jnp.bfloat16)
        return q, k, v

    parts = (project(own_in), project(far_in))
    queries = jnp.concatenate([parts[0][0], parts[1][0]], axis=0)

    def all_keys(index):
        sent = [lax.ppermute(part[index], "seq", beside) for part in parts]
        return jnp.concatenate([parts[0][index], parts[1][index], *sent], axis=0)

    keys = all_keys(1)
    values = all_keys(2)
    flat_in = jnp.concatenate([own_in, far_in], axis=0).astype(jnp.float32)
    normed_one, norm_one_back = jax.vjp(norm_apply, flat_in, first_gain, first_shift)
    normed_one_low = normed_one.astype(jnp.bfloat16)
    attended, log_sums = attend(info, queries, keys, values, 512)
    branch_attn = jnp.dot(attended, output_weight, preferred_element_type=jnp.float32) + output_bias
    hidden = flat_in + branch_attn
    normed_two, norm_two_back = jax.vjp(norm_apply, hidden, second_gain, second_shift)
    normed_two_low = normed_two.astype(jnp.bfloat16)
    inner = jnp.dot(normed_two_low, inner_weight, preferred_element_type=jnp.float32) + inner_bias
    activated_full, gelu_back = jax.vjp(exact_gelu, inner)
    activated = activated_full.astype(jnp.bfloat16)
    branch_ffn = jnp.dot(activated, outer_weight, preferred_element_type=jnp.float32) + outer_bias
    stream = keep_rows * (hidden + branch_ffn)
    result = give_back(stream.astype(jnp.bfloat16))
    grad_stream = keep_rows * cot.astype(jnp.float32)
    grad_ffn_low = grad_stream.astype(jnp.bfloat16)
    grad_outer_weight = jnp.einsum(
        "tf,td->fd", activated, grad_ffn_low, preferred_element_type=jnp.float32
    )
    grad_outer_bias = jnp.sum(grad_ffn_low, axis=0, dtype=jnp.float32)
    grad_activated = jnp.einsum(
        "td,fd->tf", grad_ffn_low, outer_weight, preferred_element_type=jnp.float32
    )
    grad_inner_low = gelu_back(grad_activated)[0].astype(jnp.bfloat16)
    grad_inner_weight = jnp.einsum(
        "td,tf->df", normed_two_low, grad_inner_low, preferred_element_type=jnp.float32
    )
    grad_inner_bias = jnp.sum(grad_inner_low, axis=0, dtype=jnp.float32)
    grad_normed_two = jnp.einsum(
        "tf,df->td", grad_inner_low, inner_weight, preferred_element_type=jnp.float32
    )
    grad_hidden_norm, grad_second_gain, grad_second_shift = norm_two_back(grad_normed_two)
    grad_hidden = grad_stream + grad_hidden_norm
    grad_attn_low = grad_hidden.astype(jnp.bfloat16)
    grad_output_weight = jnp.einsum(
        "tc,td->cd", attended, grad_attn_low, preferred_element_type=jnp.float32
    )
    grad_output_bias = jnp.sum(grad_attn_low, axis=0, dtype=jnp.float32)
    grad_attended = jnp.einsum(
        "td,cd->tc", grad_attn_low, output_weight, preferred_element_type=jnp.float32
    ).astype(jnp.bfloat16)
    grad_q_tok, grad_k_part, grad_v_part = attend_back(
        info, queries, keys, values, grad_attended, attended, log_sums, 256
    )

    def join(partial):
        far = lax.ppermute(partial[tokens_here:], "seq", beside)
        return (partial[:tokens_here].astype(jnp.float32) + far.astype(jnp.float32)).astype(
            jnp.bfloat16
        )

    grad_k_tok = join(grad_k_part)
    grad_v_tok = join(grad_v_part)
    grad_query_weight = jnp.einsum(
        "td,te->de", normed_one_low, grad_q_tok, preferred_element_type=jnp.float32
    )
    grad_key_weight = jnp.einsum(
        "td,te->de", normed_one_low, grad_k_tok, preferred_element_type=jnp.float32
    )
    grad_value_weight = jnp.einsum(
        "td,te->de", normed_one_low, grad_v_tok, preferred_element_type=jnp.float32
    )
    grad_query_bias = jnp.sum(grad_q_tok, axis=0, dtype=jnp.float32)
    grad_value_bias = jnp.sum(grad_v_tok, axis=0, dtype=jnp.float32)
    grad_normed_one = (
        jnp.einsum("te,de->td", grad_q_tok, query_weight, preferred_element_type=jnp.float32)
        + jnp.einsum("te,de->td", grad_k_tok, key_weight, preferred_element_type=jnp.float32)
        + jnp.einsum("te,de->td", grad_v_tok, value_weight, preferred_element_type=jnp.float32)
    )
    grad_in_norm, grad_first_gain, grad_first_shift = norm_one_back(grad_normed_one)
    grad_inputs = give_back((grad_hidden + grad_in_norm).astype(jnp.bfloat16))
    totals = lax.psum(
        (
            jnp.sum(stream * stream),
            jnp.sum(keep_rows * branch_attn * branch_attn),
            jnp.sum(keep_rows * branch_ffn * branch_ffn),
            jnp.sum(keep_rows),
            grad_first_gain,
            grad_first_shift,
            grad_query_bias,
            grad_value_bias,
            grad_output_bias,
            grad_second_gain,
            grad_second_shift,
            grad_inner_bias,
            grad_outer_bias,
        ),
        ("dp", "seq"),
    )
    denominator = totals[3] * width
    stream_scale = jnp.sqrt(totals[0] / denominator)
    attention_scale = jnp.sqrt(totals[1] / denominator)
    feedforward_scale = jnp.sqrt(totals[2] / denominator)
    data_groups = lax.axis_size("dp")

    def reduced(partial):
        piece = lax.psum_scatter(
            partial.astype(jnp.bfloat16), ("dp", "seq"), scatter_dimension=0, tiled=True
        )
        return lax.all_gather(piece, "seq", axis=0, tiled=True).astype(jnp.float32)

    summed_query = reduced(grad_query_weight)
    summed_key = reduced(grad_key_weight)
    summed_value = reduced(grad_value_weight)
    summed_output = reduced(grad_output_weight)
    summed_inner = reduced(grad_inner_weight)
    summed_outer = reduced(grad_outer_weight)
    return (
        result,
        grad_inputs,
        totals[4],
        totals[5],
        summed_query,
        totals[6],
        summed_key,
        summed_value,
        totals[7],
        summed_output,
        totals[8],
        totals[9],
        totals[10],
        summed_inner,
        totals[11],
        summed_outer,
        totals[12],
        stream_scale,
        attention_scale,
        feedforward_scale,
    )


def solution(mesh):
    return jax.shard_map(
        local,
        mesh=mesh,
        in_specs=(
            P("dp", "seq", None),
            P("dp"),
            P(),
            P(),
            P(),
            P(),
            P(),
            P(),
            P(),
            P(),
            P(),
            P(),
            P(),
            P(),
            P(),
            P(),
            P(),
            P("dp", "seq", None),
        ),
        out_specs=(
            P("dp", "seq", None),
            P("dp", "seq", None),
            P(),
            P(),
            P("dp", None),
            P(),
            P("dp", None),
            P("dp", None),
            P(),
            P("dp", None),
            P(),
            P(),
            P(),
            P("dp", None),
            P(),
            P("dp", None),
            P(),
            P(),
            P(),
            P(),
        ),
        check_vma=False,
    )
```

```python
import functools

import jax
import jax.numpy as jnp
from jax import lax
from jax.experimental import pallas as pl
from jax.experimental.pallas import tpu as pltpu
from jax.sharding import PartitionSpec as P

HEADS = 12
HEAD_DIM = 64
EPSILON = 1e-12
NEGATIVE = -1e30
PAIR = 2 * HEAD_DIM
NT = ((1,), (1,))
NN = ((1,), (0,))
TN = ((0,), (0,))


def norm_apply(values, gain_vec, shift_vec):
    average = jnp.mean(values, axis=-1, keepdims=True)
    centered = values - average
    spread = jnp.mean(centered * centered, axis=-1, keepdims=True)
    return centered * lax.rsqrt(spread + EPSILON) * gain_vec + shift_vec


def exact_gelu(values):
    return jax.nn.gelu(values, approximate=False)


def dot(left, right, dims):
    return lax.dot_general(left, right, (dims, ((), ())), preferred_element_type=jnp.float32)


def key_valid(info_ref, keys_total):
    spots = lax.broadcasted_iota(jnp.int32, (keys_total, 1), 0)
    blocks = info_ref.shape[0] - 1
    block_len = keys_total // blocks
    places = spots
    for index in range(blocks):
        inside = (spots >= index * block_len) & (spots < (index + 1) * block_len)
        places = jnp.where(inside, spots - index * block_len + info_ref[index + 1], places)
    return places < info_ref[0]


def attend_body(info_ref, q_ref, k_ref, v_ref, out_ref, lse_ref):
    lane = lax.broadcasted_iota(jnp.int32, (1, PAIR), 1)
    scale = jnp.bfloat16(HEAD_DIM ** (-0.5))
    queries = q_ref[...] * scale
    keys = k_ref[...]
    values_t = v_ref[...].T
    valid = key_valid(info_ref, keys.shape[0])
    outs = []
    for head in range(2):
        mine = (lane < HEAD_DIM) if head == 0 else (lane >= HEAD_DIM)
        scores = dot(keys, jnp.where(mine, queries, jnp.zeros_like(queries)), NT)
        scores = jnp.where(valid, scores, NEGATIVE)
        top = jnp.max(scores, axis=0, keepdims=True)
        weights = jnp.exp(scores - top)
        total = jnp.sum(weights, axis=0, keepdims=True)
        mixed = dot(
            values_t[HEAD_DIM * head : HEAD_DIM * (head + 1)], weights.astype(jnp.bfloat16), NN
        )
        outs.append(mixed * (1.0 / total))
        lse_ref[0, head : head + 1, :] = top + jnp.log(total)
    out_ref[...] = jnp.concatenate(outs, axis=0).T.astype(jnp.bfloat16)


def attend(info, queries, keys, values, block):
    tokens, width = queries.shape
    total = keys.shape[0]
    pairs = width // PAIR
    q_spec = pl.BlockSpec((block, PAIR), lambda h, i, n: (i, h))
    k_spec = pl.BlockSpec((total, PAIR), lambda h, i, n: (0, h))
    return pl.pallas_call(
        attend_body,
        grid_spec=pltpu.PrefetchScalarGridSpec(
            num_scalar_prefetch=1,
            grid=(pairs, tokens // block),
            in_specs=[q_spec, k_spec, k_spec],
            out_specs=[q_spec, pl.BlockSpec((1, 2, block), lambda h, i, n: (h, 0, i))],
        ),
        out_shape=[
            jax.ShapeDtypeStruct((tokens, width), jnp.bfloat16),
            jax.ShapeDtypeStruct((pairs, 2, tokens), jnp.float32),
        ],
        compiler_params=pltpu.CompilerParams(vmem_limit_bytes=48 << 20),
        cost_estimate=pl.CostEstimate(
            flops=16 * tokens * total * width, bytes_accessed=1 << 23, transcendentals=0
        ),
        name="attend",
    )(info, queries, keys, values)


def attend_back_body(
    info_ref, q_ref, k_ref, v_ref, do_ref, o_ref, lse_ref, dq_ref, dk_ref, dv_ref, dk_acc, dv_acc
):
    step = pl.program_id(1)
    lane = lax.broadcasted_iota(jnp.int32, (1, PAIR), 1)
    scale = jnp.bfloat16(HEAD_DIM ** (-0.5))
    grad_out = do_ref[...]
    queries = q_ref[...] * scale
    keys = k_ref[...]
    values = v_ref[...]
    product = grad_out.astype(jnp.float32) * o_ref[...].astype(jnp.float32)
    pick = (
        lax.broadcasted_iota(jnp.int32, (8, PAIR), 1) // HEAD_DIM
        == lax.broadcasted_iota(jnp.int32, (8, PAIR), 0)
    ).astype(jnp.float32)
    row_sums = lax.dot_general(
        pick,
        product,
        (NT, ((), ())),
        precision=lax.Precision.HIGHEST,
        preferred_element_type=jnp.float32,
    )
    valid = key_valid(info_ref, keys.shape[0])
    zero = jnp.zeros_like(queries)
    grad_k = 0
    grad_v = 0
    grad_q = 0
    for head in range(2):
        mine = (lane < HEAD_DIM) if head == 0 else (lane >= HEAD_DIM)
        query_h = jnp.where(mine, queries, zero)
        out_h = jnp.where(mine, grad_out, zero)
        scores = jnp.where(valid, dot(keys, query_h, NT), NEGATIVE)
        weights = jnp.exp(scores - lse_ref[0, head : head + 1, :])
        grad_w = dot(values, out_h, NT)
        grad_s = (weights * (grad_w - row_sums[head : head + 1])).astype(jnp.bfloat16)
        grad_v = grad_v + dot(weights.astype(jnp.bfloat16), out_h, NN)
        grad_k = grad_k + dot(grad_s, query_h, NN)
        grad_q_h = dot(grad_s, keys, TN)
        grad_q = grad_q_h if head == 0 else jnp.where(mine, grad_q_h, grad_q)
    dq_ref[...] = (grad_q * (HEAD_DIM ** (-0.5))).astype(jnp.bfloat16)

    @pl.when(step == 0)
    def _():
        dk_acc[...] = grad_k
        dv_acc[...] = grad_v

    @pl.when(step > 0)
    def _():
        dk_acc[...] += grad_k
        dv_acc[...] += grad_v

    @pl.when(step == pl.num_programs(1) - 1)
    def _():
        dk_ref[...] = dk_acc[...].astype(jnp.bfloat16)
        dv_ref[...] = dv_acc[...].astype(jnp.bfloat16)


def attend_back(info, queries, keys, values, grad_out, out, log_sums, block):
    tokens, width = queries.shape
    total = keys.shape[0]
    pairs = width // PAIR
    q_spec = pl.BlockSpec((block, PAIR), lambda h, i, n: (i, h))
    k_spec = pl.BlockSpec((total, PAIR), lambda h, i, n: (0, h))
    return pl.pallas_call(
        attend_back_body,
        grid_spec=pltpu.PrefetchScalarGridSpec(
            num_scalar_prefetch=1,
            grid=(pairs, tokens // block),
            in_specs=[
                q_spec,
                k_spec,
                k_spec,
                q_spec,
                q_spec,
                pl.BlockSpec((1, 2, block), lambda h, i, n: (h, 0, i)),
            ],
            out_specs=[q_spec, k_spec, k_spec],
            scratch_shapes=[pltpu.VMEM((total, PAIR), jnp.float32)] * 2,
        ),
        out_shape=[
            jax.ShapeDtypeStruct((tokens, width), jnp.bfloat16),
            jax.ShapeDtypeStruct((total, width), jnp.bfloat16),
            jax.ShapeDtypeStruct((total, width), jnp.bfloat16),
        ],
        compiler_params=pltpu.CompilerParams(vmem_limit_bytes=48 << 20),
        cost_estimate=pl.CostEstimate(
            flops=40 * tokens * total * width, bytes_accessed=1 << 24, transcendentals=0
        ),
        name="attend_back",
    )(info, queries, keys, values, grad_out, out, log_sums)


MESH_IDS = pl.DeviceIdType.MESH
AXES = ("zhi", "zlo", "x", "y")
COLORS = (("y", "x", "zlo", "zhi"), ("x", "y", "zlo", "zhi"), ("zlo", "zhi", "y", "x"))


def where_am_i():
    data = lax.axis_index("dp")
    seq = lax.axis_index("seq")
    bits = {
        "zhi": data // 4,
        "zlo": (data // 2) % 2,
        "x": data % 2,
        "y": seq // 2,
        "core": seq % 2,
    }

    def across(axis):
        if axis == "core":
            return (data, seq + 1 - 2 * bits["core"])
        if axis == "y":
            return (data, seq + 2 - 4 * bits["y"])
        step = {"zhi": 4, "zlo": 2, "x": 1}[axis]
        return (data + step - 2 * step * bits[axis], seq)

    return bits, across


def spot_of(piece, order):
    bits = {axis: (piece >> (3 - k)) & 1 for k, axis in enumerate(AXES)}
    return sum(bits[axis] << (3 - k) for k, axis in enumerate(order))


class Color:
    def __init__(self, source, acc, lands, gathers, sems, order):
        self.source, self.acc, self.lands, self.gathers = source, acc, lands, gathers
        self.sems, self.order = sems, order
        self.pieces, self.rows, self.cols = acc.shape
        self.bits, self.across = where_am_i()
        self.base = 0

    def remote(self, src, dst, slot, axis):
        return pltpu.make_async_remote_copy(
            src_ref=src,
            dst_ref=dst,
            send_sem=self.sems.at[0, slot],
            recv_sem=self.sems.at[1, slot],
            device_id=self.across(axis),
            device_id_type=MESH_IDS,
        )

    def begin(self):
        core = self.bits["core"]
        mine = pl.ds(pl.multiple_of(core * self.cols, 128), self.cols)
        theirs = pl.ds(pl.multiple_of((1 - core) * self.cols, 128), self.cols)
        for piece in range(self.pieces):
            spot = spot_of(piece, self.order)
            span = pl.ds(piece * self.rows, self.rows)
            self.remote(
                self.source.at[span, theirs], self.lands[0].at[spot], 0, "core"
            ).start()
            pltpu.make_async_copy(
                self.source.at[span, mine], self.acc.at[spot], self.sems.at[0, 7]
            ).start()

    def add(self, count, land):
        base = self.base

        @pl.loop(0, count)
        def _(index):
            total = self.acc[base + index].astype(jnp.float32) + land[index].astype(jnp.float32)
            self.acc[base + index] = total.astype(jnp.bfloat16)

    def send(self, stage):
        axis = self.order[stage]
        half = self.pieces >> (stage + 1)
        me = self.bits[axis]
        self.copy = self.remote(
            self.acc.at[pl.ds(self.base + (1 - me) * half, half)],
            self.lands[stage + 1],
            stage + 1,
            axis,
        )
        self.copy.start()
        self.base = self.base + me * half

    def step(self, stage):
        if stage == 0:
            whole = self.remote(self.lands[0], self.lands[0], 0, "core")
            pltpu.make_async_copy(self.acc, self.acc, self.sems.at[0, 7]).wait()
            whole.wait_send()
            whole.wait_recv()
            self.add(self.pieces, self.lands[0])
            self.send(0)
        elif stage <= 4:
            self.copy.wait()
            self.add(self.pieces >> stage, self.lands[stage])
            if stage < 4:
                self.send(stage)
            else:
                y = self.bits["y"]
                self.gathers[0][y] = self.acc[self.base]
                self.copy = self.remote(self.acc.at[self.base], self.gathers[0].at[y], 5, "y")
                self.copy.start()
        elif stage == 5:
            self.copy.wait()
            self.copy = self.remote(self.gathers[0], self.gathers[1], 6, "core")
            self.copy.start()
        else:
            self.copy.wait()


def vector_sum(source, held, lands, sems, bits_across):
    bits, across = bits_across
    held[...] = source[...]
    for slot, axis in enumerate(("core", "y", "x", "zlo", "zhi")):
        copy = pltpu.make_async_remote_copy(
            src_ref=held,
            dst_ref=lands.at[slot],
            send_sem=sems.at[0, slot],
            recv_sem=sems.at[1, slot],
            device_id=across(axis),
            device_id_type=MESH_IDS,
        )
        copy.start()
        yield
        copy.wait()
        held[...] = held[...] + lands[slot]


def reduce_body(count, orders, *refs):
    sources, vector = refs[:count], refs[count]
    outs = refs[count + 1 : count + 1 + 2 * count]
    vector_out = refs[3 * count + 1]
    scratch = refs[3 * count + 2 :]
    bits, across = where_am_i()
    barrier = pltpu.get_barrier_semaphore()
    for axis in ("core", *AXES):
        pl.semaphore_signal(barrier, inc=1, device_id=across(axis), device_id_type=MESH_IDS)
    pl.semaphore_wait(barrier, 5)
    colors = []
    for index in range(count):
        acc, *lands = scratch[7 * index : 7 * index + 6]
        colors.append(
            Color(
                sources[index],
                acc,
                lands,
                outs[2 * index : 2 * index + 2],
                scratch[7 * index + 6],
                orders[index],
            )
        )
    vector_lands, vector_sems = scratch[7 * count :]
    small = vector_sum(vector, vector_out, vector_lands, vector_sems, (bits, across))
    for color in colors:
        color.begin()
    next(small)
    for stage in range(7):
        for color in colors:
            color.step(stage)
        next(small, None)


def reduce_all(arrays, orders, vector, collective):
    scratch = []
    outs = []
    for array in arrays:
        rows, cols = array.shape[0] // 16, array.shape[1] // 2
        scratch.append(pltpu.VMEM((16, rows, cols), jnp.bfloat16))
        for size in (16, 8, 4, 2, 1):
            scratch.append(pltpu.VMEM((size, rows, cols), jnp.bfloat16))
        scratch.append(pltpu.SemaphoreType.DMA((2, 8)))
        outs += [jax.ShapeDtypeStruct((2, rows, cols), jnp.bfloat16)] * 2
    scratch.append(pltpu.VMEM((5, *vector.shape), jnp.float32))
    scratch.append(pltpu.SemaphoreType.DMA((2, 5)))
    outs.append(jax.ShapeDtypeStruct(vector.shape, jnp.float32))
    vmem = pl.BlockSpec(memory_space=pltpu.VMEM)
    got = pl.pallas_call(
        functools.partial(reduce_body, len(arrays), orders),
        out_shape=outs,
        in_specs=[pl.BlockSpec(memory_space=pl.ANY)] * len(arrays) + [vmem],
        out_specs=[vmem] * len(outs),
        scratch_shapes=scratch,
        compiler_params=pltpu.CompilerParams(
            collective_id=collective, has_side_effects=True, vmem_limit_bytes=60 << 20
        ),
        name="reduce_all",
    )(*arrays, vector)
    core = lax.axis_index("seq") % 2
    sums = []
    for index, array in enumerate(arrays):
        mine, other = got[2 * index], got[2 * index + 1]
        rows = array.shape[0] // 8
        left = jnp.where(core == 0, mine, other).reshape(rows, -1)
        right = jnp.where(core == 0, other, mine).reshape(rows, -1)
        sums.append(jnp.concatenate([left, right], axis=1).astype(jnp.float32))
    return sums, got[-1]


def local(
    inputs,
    lengths,
    first_gain,
    first_shift,
    query_weight,
    query_bias,
    key_weight,
    value_weight,
    value_bias,
    output_weight,
    output_bias,
    second_gain,
    second_shift,
    inner_weight,
    inner_bias,
    outer_weight,
    outer_bias,
    cotangent,
):
    groups = lax.axis_size("seq")
    seq_count, local_len, width = inputs.shape
    full_len = local_len * groups
    tokens_here = seq_count * local_len
    place = lax.axis_index("seq")
    half = groups // 2
    row = place // half
    across = [(i, (i + half) % groups) for i in range(groups)]
    beside = [(i, i ^ 1) for i in range(groups)]
    there = lax.rem(place + half, groups)
    near = place + 1 - 2 * lax.rem(place, 2)

    def mine_of(array):
        return lax.dynamic_index_in_dim(array, row, 0, keepdims=False)

    def swap(array):
        return lax.ppermute(
            lax.dynamic_index_in_dim(array, 1 - row, 0, keepdims=False), "seq", across
        )

    def give_back(array):
        own = array[:local_len]
        other = lax.ppermute(array[local_len:], "seq", across)
        return jnp.where(row == 0, jnp.stack([own, other]), jnp.stack([other, own]))

    length = lax.dynamic_index_in_dim(lengths, row, 0, keepdims=False)
    starts = jnp.stack(
        [place, there, near, lax.rem(near + half, groups)]
    ).astype(jnp.int32) * local_len
    info = jnp.concatenate([length[None], starts])
    spots = jnp.concatenate(
        [starts[0] + jnp.arange(local_len, dtype=jnp.int32), starts[1] + jnp.arange(local_len, dtype=jnp.int32)]
    )
    keep_rows = (spots < length).astype(jnp.float32)[:, None]
    own_in = mine_of(inputs)
    far_in = swap(inputs)
    cot = jnp.concatenate([mine_of(cotangent), swap(cotangent)], axis=0)

    def project(rows):
        normed = norm_apply(rows.astype(jnp.float32), first_gain, first_shift).astype(jnp.bfloat16)
        q = (
            jnp.dot(normed, query_weight, preferred_element_type=jnp.float32) + query_bias
        ).astype(jnp.bfloat16)
        k = jnp.dot(normed, key_weight, preferred_element_type=jnp.float32).astype(jnp.bfloat16)
        v = (
            jnp.dot(normed, value_weight, preferred_element_type=jnp.float32) + value_bias
        ).astype(jnp.bfloat16)
        return q, k, v

    parts = (project(own_in), project(far_in))
    queries = jnp.concatenate([parts[0][0], parts[1][0]], axis=0)

    def all_keys(index):
        sent = [lax.ppermute(part[index], "seq", beside) for part in parts]
        return jnp.concatenate([parts[0][index], parts[1][index], *sent], axis=0)

    keys = all_keys(1)
    values = all_keys(2)
    flat_in = jnp.concatenate([own_in, far_in], axis=0).astype(jnp.float32)
    normed_one, norm_one_back = jax.vjp(norm_apply, flat_in, first_gain, first_shift)
    normed_one_low = normed_one.astype(jnp.bfloat16)
    attended, log_sums = attend(info, queries, keys, values, 512)
    branch_attn = jnp.dot(attended, output_weight, preferred_element_type=jnp.float32) + output_bias
    hidden = flat_in + branch_attn
    normed_two, norm_two_back = jax.vjp(norm_apply, hidden, second_gain, second_shift)
    normed_two_low = normed_two.astype(jnp.bfloat16)
    inner = jnp.dot(normed_two_low, inner_weight, preferred_element_type=jnp.float32) + inner_bias
    activated_full, gelu_back = jax.vjp(exact_gelu, inner)
    activated = activated_full.astype(jnp.bfloat16)
    branch_ffn = jnp.dot(activated, outer_weight, preferred_element_type=jnp.float32) + outer_bias
    stream = keep_rows * (hidden + branch_ffn)
    result = give_back(stream.astype(jnp.bfloat16))
    grad_stream = keep_rows * cot.astype(jnp.float32)
    grad_ffn_low = grad_stream.astype(jnp.bfloat16)
    grad_outer_weight = jnp.einsum(
        "tf,td->fd", activated, grad_ffn_low, preferred_element_type=jnp.float32
    )
    grad_outer_bias = jnp.sum(grad_ffn_low, axis=0, dtype=jnp.float32)
    grad_activated = jnp.einsum(
        "td,fd->tf", grad_ffn_low, outer_weight, preferred_element_type=jnp.float32
    )
    grad_inner_low = gelu_back(grad_activated)[0].astype(jnp.bfloat16)
    grad_inner_weight = jnp.einsum(
        "td,tf->df", normed_two_low, grad_inner_low, preferred_element_type=jnp.float32
    )
    grad_inner_bias = jnp.sum(grad_inner_low, axis=0, dtype=jnp.float32)
    grad_normed_two = jnp.einsum(
        "tf,df->td", grad_inner_low, inner_weight, preferred_element_type=jnp.float32
    )
    grad_hidden_norm, grad_second_gain, grad_second_shift = norm_two_back(grad_normed_two)
    grad_hidden = grad_stream + grad_hidden_norm
    grad_attn_low = grad_hidden.astype(jnp.bfloat16)
    grad_output_weight = jnp.einsum(
        "tc,td->cd", attended, grad_attn_low, preferred_element_type=jnp.float32
    )
    grad_output_bias = jnp.sum(grad_attn_low, axis=0, dtype=jnp.float32)
    grad_attended = jnp.einsum(
        "td,cd->tc", grad_attn_low, output_weight, preferred_element_type=jnp.float32
    ).astype(jnp.bfloat16)
    grad_q_tok, grad_k_part, grad_v_part = attend_back(
        info, queries, keys, values, grad_attended, attended, log_sums, 256
    )

    def join(partial):
        far = lax.ppermute(partial[tokens_here:], "seq", beside)
        return (partial[:tokens_here].astype(jnp.float32) + far.astype(jnp.float32)).astype(
            jnp.bfloat16
        )

    grad_k_tok = join(grad_k_part)
    grad_v_tok = join(grad_v_part)
    grad_qkv = jnp.concatenate(
        [
            dot(normed_one_low, grad, TN).astype(jnp.bfloat16)
            for grad in (grad_q_tok, grad_k_tok, grad_v_tok)
        ],
        axis=1,
    )
    grad_query_bias = jnp.sum(grad_q_tok, axis=0, dtype=jnp.float32)
    grad_value_bias = jnp.sum(grad_v_tok, axis=0, dtype=jnp.float32)
    grad_normed_one = (
        jnp.einsum("te,de->td", grad_q_tok, query_weight, preferred_element_type=jnp.float32)
        + jnp.einsum("te,de->td", grad_k_tok, key_weight, preferred_element_type=jnp.float32)
        + jnp.einsum("te,de->td", grad_v_tok, value_weight, preferred_element_type=jnp.float32)
    )
    grad_in_norm, grad_first_gain, grad_first_shift = norm_one_back(grad_normed_one)
    grad_inputs = give_back((grad_hidden + grad_in_norm).astype(jnp.bfloat16))
    vectors = (
        jnp.stack(
            [
                jnp.sum(stream * stream),
                jnp.sum(keep_rows * branch_attn * branch_attn),
                jnp.sum(keep_rows * branch_ffn * branch_ffn),
                jnp.sum(keep_rows),
            ]
        ),
        grad_first_gain,
        grad_first_shift,
        grad_query_bias,
        grad_value_bias,
        grad_output_bias,
        grad_second_gain,
        grad_second_shift,
        grad_inner_bias,
        grad_outer_bias,
    )
    data_groups = lax.axis_size("dp")
    packed = jnp.concatenate([jnp.pad(vectors[0], (0, 124)), *vectors[1:]])
    size = packed.shape[0]
    packed = jnp.pad(packed, (0, -size % 1024)).reshape(-1, 128)
    low = jnp.bfloat16
    if data_groups == 8 and groups == 4:
        (summed_outer, summed_inner, qkv, summed_output), packed = reduce_all(
            (
                grad_outer_weight.astype(low),
                grad_inner_weight.astype(low),
                grad_qkv.astype(low),
                grad_output_weight.astype(low),
            ),
            (COLORS[0], COLORS[1], COLORS[2], COLORS[2]),
            packed,
            1,
        )
    else:

        def reduced(partial):
            piece = lax.psum_scatter(
                partial.astype(low), ("dp", "seq"), scatter_dimension=0, tiled=True
            )
            return lax.all_gather(piece, "seq", axis=0, tiled=True).astype(jnp.float32)

        summed_outer = reduced(grad_outer_weight)
        summed_inner = reduced(grad_inner_weight)
        summed_output = reduced(grad_output_weight)
        qkv = reduced(grad_qkv)
        packed = lax.psum(packed, ("dp", "seq"))
    summed_query, summed_key, summed_value = jnp.split(qkv, 3, axis=1)
    packed = packed.reshape(-1)
    totals = [packed[0], packed[1], packed[2], packed[3]]
    at = 128
    for item in vectors[1:]:
        totals.append(packed[at : at + item.shape[0]])
        at += item.shape[0]
    denominator = totals[3] * width
    stream_scale = jnp.sqrt(totals[0] / denominator)
    attention_scale = jnp.sqrt(totals[1] / denominator)
    feedforward_scale = jnp.sqrt(totals[2] / denominator)
    return (
        result,
        grad_inputs,
        totals[4],
        totals[5],
        summed_query,
        totals[6],
        summed_key,
        summed_value,
        totals[7],
        summed_output,
        totals[8],
        totals[9],
        totals[10],
        summed_inner,
        totals[11],
        summed_outer,
        totals[12],
        stream_scale,
        attention_scale,
        feedforward_scale,
    )


def solution(mesh):
    return jax.shard_map(
        local,
        mesh=mesh,
        in_specs=(
            P("dp", "seq", None),
            P("dp"),
            P(),
            P(),
            P(),
            P(),
            P(),
            P(),
            P(),
            P(),
            P(),
            P(),
            P(),
            P(),
            P(),
            P(),
            P(),
            P("dp", "seq", None),
        ),
        out_specs=(
            P("dp", "seq", None),
            P("dp", "seq", None),
            P(),
            P(),
            P("dp", None),
            P(),
            P("dp", None),
            P("dp", None),
            P(),
            P("dp", None),
            P(),
            P(),
            P(),
            P("dp", None),
            P(),
            P("dp", None),
            P(),
            P(),
            P(),
            P(),
        ),
        check_vma=False,
    )
```

```python
import functools

import jax
import jax.numpy as jnp
from jax import lax
from jax.experimental import pallas as pl
from jax.experimental.pallas import tpu as pltpu
from jax.sharding import PartitionSpec as P

HEADS = 12
HEAD_DIM = 64
EPSILON = 1e-12
NEGATIVE = -1e30
PAIR = 2 * HEAD_DIM
NT = ((1,), (1,))
NN = ((1,), (0,))
TN = ((0,), (0,))


def norm_apply(values, gain_vec, shift_vec):
    average = jnp.mean(values, axis=-1, keepdims=True)
    centered = values - average
    spread = jnp.mean(centered * centered, axis=-1, keepdims=True)
    return centered * lax.rsqrt(spread + EPSILON) * gain_vec + shift_vec


def dot(left, right, dims):
    return lax.dot_general(left, right, (dims, ((), ())), preferred_element_type=jnp.float32)


def key_valid(info_ref, keys_total):
    spots = lax.broadcasted_iota(jnp.int32, (keys_total, 1), 0)
    blocks = info_ref.shape[0] - 1
    block_len = keys_total // blocks
    places = spots
    for index in range(blocks):
        inside = (spots >= index * block_len) & (spots < (index + 1) * block_len)
        places = jnp.where(inside, spots - index * block_len + info_ref[index + 1], places)
    return places < info_ref[0]


def attend_body(info_ref, q_ref, k_ref, v_ref, out_ref, lse_ref):
    lane = lax.broadcasted_iota(jnp.int32, (1, PAIR), 1)
    scale = jnp.bfloat16(HEAD_DIM ** (-0.5))
    queries = q_ref[...] * scale
    keys = k_ref[...]
    values_t = v_ref[...].T
    valid = key_valid(info_ref, keys.shape[0])
    outs = []
    for head in range(2):
        mine = (lane < HEAD_DIM) if head == 0 else (lane >= HEAD_DIM)
        scores = dot(keys, jnp.where(mine, queries, jnp.zeros_like(queries)), NT)
        scores = jnp.where(valid, scores, NEGATIVE)
        top = jnp.max(scores, axis=0, keepdims=True)
        weights = jnp.exp(scores - top)
        total = jnp.sum(weights, axis=0, keepdims=True)
        mixed = dot(
            values_t[HEAD_DIM * head : HEAD_DIM * (head + 1)], weights.astype(jnp.bfloat16), NN
        )
        outs.append(mixed * (1.0 / total))
        lse_ref[0, head : head + 1, :] = top + jnp.log(total)
    out_ref[...] = jnp.concatenate(outs, axis=0).T.astype(jnp.bfloat16)


def attend(info, queries, keys, values, block):
    tokens, width = queries.shape
    total = keys.shape[0]
    pairs = width // PAIR
    q_spec = pl.BlockSpec((block, PAIR), lambda h, i, n: (i, h))
    k_spec = pl.BlockSpec((total, PAIR), lambda h, i, n: (0, h))
    return pl.pallas_call(
        attend_body,
        grid_spec=pltpu.PrefetchScalarGridSpec(
            num_scalar_prefetch=1,
            grid=(pairs, tokens // block),
            in_specs=[q_spec, k_spec, k_spec],
            out_specs=[q_spec, pl.BlockSpec((1, 2, block), lambda h, i, n: (h, 0, i))],
        ),
        out_shape=[
            jax.ShapeDtypeStruct((tokens, width), jnp.bfloat16),
            jax.ShapeDtypeStruct((pairs, 2, tokens), jnp.float32),
        ],
        compiler_params=pltpu.CompilerParams(vmem_limit_bytes=48 << 20),
        cost_estimate=pl.CostEstimate(
            flops=16 * tokens * total * width, bytes_accessed=1 << 23, transcendentals=0
        ),
        name="attend",
    )(info, queries, keys, values)


def attend_back_body(
    info_ref, q_ref, k_ref, v_ref, do_ref, o_ref, lse_ref, dq_ref, dk_ref, dv_ref, dk_acc, dv_acc
):
    step = pl.program_id(1)
    lane = lax.broadcasted_iota(jnp.int32, (1, PAIR), 1)
    scale = jnp.bfloat16(HEAD_DIM ** (-0.5))
    grad_out = do_ref[...]
    queries = q_ref[...] * scale
    keys = k_ref[...]
    values = v_ref[...]
    product = grad_out.astype(jnp.float32) * o_ref[...].astype(jnp.float32)
    pick = (
        lax.broadcasted_iota(jnp.int32, (8, PAIR), 1) // HEAD_DIM
        == lax.broadcasted_iota(jnp.int32, (8, PAIR), 0)
    ).astype(jnp.float32)
    row_sums = lax.dot_general(
        pick,
        product,
        (NT, ((), ())),
        precision=lax.Precision.HIGHEST,
        preferred_element_type=jnp.float32,
    )
    valid = key_valid(info_ref, keys.shape[0])
    zero = jnp.zeros_like(queries)
    grad_k = 0
    grad_v = 0
    grad_q = 0
    for head in range(2):
        mine = (lane < HEAD_DIM) if head == 0 else (lane >= HEAD_DIM)
        query_h = jnp.where(mine, queries, zero)
        out_h = jnp.where(mine, grad_out, zero)
        scores = jnp.where(valid, dot(keys, query_h, NT), NEGATIVE)
        weights = jnp.exp(scores - lse_ref[0, head : head + 1, :])
        grad_w = dot(values, out_h, NT)
        grad_s = (weights * (grad_w - row_sums[head : head + 1])).astype(jnp.bfloat16)
        grad_v = grad_v + dot(weights.astype(jnp.bfloat16), out_h, NN)
        grad_k = grad_k + dot(grad_s, query_h, NN)
        grad_q_h = dot(grad_s, keys, TN)
        grad_q = grad_q_h if head == 0 else jnp.where(mine, grad_q_h, grad_q)
    dq_ref[...] = (grad_q * (HEAD_DIM ** (-0.5))).astype(jnp.bfloat16)

    @pl.when(step == 0)
    def _():
        dk_acc[...] = grad_k
        dv_acc[...] = grad_v

    @pl.when(step > 0)
    def _():
        dk_acc[...] += grad_k
        dv_acc[...] += grad_v

    @pl.when(step == pl.num_programs(1) - 1)
    def _():
        dk_ref[...] = dk_acc[...].astype(jnp.bfloat16)
        dv_ref[...] = dv_acc[...].astype(jnp.bfloat16)


def attend_back(info, queries, keys, values, grad_out, out, log_sums, block):
    tokens, width = queries.shape
    total = keys.shape[0]
    pairs = width // PAIR
    q_spec = pl.BlockSpec((block, PAIR), lambda h, i, n: (i, h))
    k_spec = pl.BlockSpec((total, PAIR), lambda h, i, n: (0, h))
    return pl.pallas_call(
        attend_back_body,
        grid_spec=pltpu.PrefetchScalarGridSpec(
            num_scalar_prefetch=1,
            grid=(pairs, tokens // block),
            in_specs=[
                q_spec,
                k_spec,
                k_spec,
                q_spec,
                q_spec,
                pl.BlockSpec((1, 2, block), lambda h, i, n: (h, 0, i)),
            ],
            out_specs=[q_spec, k_spec, k_spec],
            scratch_shapes=[pltpu.VMEM((total, PAIR), jnp.float32)] * 2,
        ),
        out_shape=[
            jax.ShapeDtypeStruct((tokens, width), jnp.bfloat16),
            jax.ShapeDtypeStruct((total, width), jnp.bfloat16),
            jax.ShapeDtypeStruct((total, width), jnp.bfloat16),
        ],
        compiler_params=pltpu.CompilerParams(vmem_limit_bytes=48 << 20),
        cost_estimate=pl.CostEstimate(
            flops=40 * tokens * total * width, bytes_accessed=1 << 24, transcendentals=0
        ),
        name="attend_back",
    )(info, queries, keys, values, grad_out, out, log_sums)


MESH_IDS = pl.DeviceIdType.MESH
AXES = ("zhi", "zlo", "x", "y")
COLORS = (("y", "x", "zlo", "zhi"), ("x", "y", "zlo", "zhi"), ("zlo", "zhi", "y", "x"))


def where_am_i():
    data = lax.axis_index("dp")
    seq = lax.axis_index("seq")
    bits = {
        "zhi": data // 4,
        "zlo": (data // 2) % 2,
        "x": data % 2,
        "y": seq // 2,
        "core": seq % 2,
    }

    def across(axis):
        if axis == "core":
            return (data, seq + 1 - 2 * bits["core"])
        if axis == "y":
            return (data, seq + 2 - 4 * bits["y"])
        step = {"zhi": 4, "zlo": 2, "x": 1}[axis]
        return (data + step - 2 * step * bits[axis], seq)

    return bits, across


def spot_of(piece, order):
    bits = {axis: (piece >> (3 - k)) & 1 for k, axis in enumerate(AXES)}
    return sum(bits[axis] << (3 - k) for k, axis in enumerate(order))


class Color:
    def __init__(self, source, acc, lands, gathers, sems, order):
        self.source, self.acc, self.lands, self.gathers = source, acc, lands, gathers
        self.sems, self.order = sems, order
        self.pieces, self.rows, self.cols = acc.shape
        self.bits, self.across = where_am_i()

    def base(self, stage):
        return sum(self.bits[self.order[k]] * (self.pieces >> (k + 1)) for k in range(stage))

    def remote(self, src, dst, slot, axis):
        return pltpu.make_async_remote_copy(
            src_ref=src,
            dst_ref=dst,
            send_sem=self.sems.at[0, slot],
            recv_sem=self.sems.at[1, slot],
            device_id=self.across(axis),
            device_id_type=MESH_IDS,
        )

    def begin(self):
        core = self.bits["core"]
        mine = pl.ds(pl.multiple_of(core * self.cols, 128), self.cols)
        theirs = pl.ds(pl.multiple_of((1 - core) * self.cols, 128), self.cols)
        for piece in range(self.pieces):
            spot = spot_of(piece, self.order)
            span = pl.ds(piece * self.rows, self.rows)
            self.remote(
                self.source.at[span, theirs], self.lands[0].at[spot], 0, "core"
            ).start()
            pltpu.make_async_copy(
                self.source.at[span, mine], self.acc.at[spot], self.sems.at[0, 7]
            ).start()

    def add(self, base, count, land):
        @pl.loop(0, count)
        def _(index):
            total = self.acc[base + index].astype(jnp.float32) + land[index].astype(jnp.float32)
            self.acc[base + index] = total.astype(jnp.bfloat16)

    def transfer(self, stage):
        if stage < 4:
            axis = self.order[stage]
            half = self.pieces >> (stage + 1)
            start = self.base(stage) + (1 - self.bits[axis]) * half
            return self.remote(
                self.acc.at[pl.ds(start, half)], self.lands[stage + 1], stage + 1, axis
            )
        if stage == 4:
            there = self.gathers[0].at[self.bits["y"]]
            return self.remote(self.acc.at[self.base(4)], there, 5, "y")
        return self.remote(self.gathers[0], self.gathers[1], 6, "core")

    def step(self, stage):
        if stage == 0:
            whole = self.remote(self.lands[0], self.lands[0], 0, "core")
            pltpu.make_async_copy(self.acc, self.acc, self.sems.at[0, 7]).wait()
            whole.wait_send()
            whole.wait_recv()
        else:
            self.transfer(stage - 1).wait()
        if stage <= 4:
            self.add(self.base(stage), self.pieces >> stage, self.lands[stage])
        if stage == 4:
            self.gathers[0][self.bits["y"]] = self.acc[self.base(4)]
        if stage < 6:
            self.transfer(stage).start()


def greet(across):
    barrier = pltpu.get_barrier_semaphore()
    for axis in ("core", *AXES):
        pl.semaphore_signal(barrier, inc=1, device_id=across(axis), device_id_type=MESH_IDS)
    pl.semaphore_wait(barrier, 5)


def color_scratch(arrays):
    scratch = []
    outs = []
    for array in arrays:
        rows, cols = array.shape[0] // 16, array.shape[1] // 2
        scratch.append(pltpu.VMEM((16, rows, cols), jnp.bfloat16))
        for size in (16, 8, 4, 2, 1):
            scratch.append(pltpu.VMEM((size, rows, cols), jnp.bfloat16))
        scratch += [pltpu.VMEM((2, rows, cols), jnp.bfloat16)] * 2
        scratch.append(pltpu.SemaphoreType.DMA((2, 8)))
        outs += [jax.ShapeDtypeStruct((2, rows, cols), jnp.bfloat16)] * 2
    return scratch, outs


def colors_of(sources, scratch, orders):
    colors = []
    for index, source in enumerate(sources):
        acc, *lands = scratch[9 * index : 9 * index + 6]
        gathers = scratch[9 * index + 6 : 9 * index + 8]
        sems = scratch[9 * index + 8]
        colors.append(Color(source, acc, lands, gathers, sems, orders[index]))
    return colors


def hand_out(colors, outs):
    for index, color in enumerate(colors):
        outs[2 * index][...] = color.gathers[0][...]
        outs[2 * index + 1][...] = color.gathers[1][...]


def assemble(arrays, got):
    core = lax.axis_index("seq") % 2
    sums = []
    for index, array in enumerate(arrays):
        mine, other = got[2 * index], got[2 * index + 1]
        rows = array.shape[0] // 8
        left = jnp.where(core == 0, mine, other).reshape(rows, -1)
        right = jnp.where(core == 0, other, mine).reshape(rows, -1)
        sums.append(jnp.concatenate([left, right], axis=1).astype(jnp.float32))
    return sums


def vector_sum(source, held, lands, sems, bits_across):
    bits, across = bits_across
    held[...] = source[...]
    for slot, axis in enumerate(("core", "y", "x", "zlo", "zhi")):
        copy = pltpu.make_async_remote_copy(
            src_ref=held,
            dst_ref=lands.at[slot],
            send_sem=sems.at[0, slot],
            recv_sem=sems.at[1, slot],
            device_id=across(axis),
            device_id_type=MESH_IDS,
        )
        copy.start()
        yield
        copy.wait()
        held[...] = held[...] + lands[slot]


def reduce_body(count, orders, *refs):
    sources, vector = refs[:count], refs[count]
    outs = refs[count + 1 : count + 1 + 2 * count]
    vector_out = refs[3 * count + 1]
    scratch = refs[3 * count + 2 :]
    bits, across = where_am_i()
    greet(across)
    colors = colors_of(sources, scratch, orders)
    vector_lands, vector_sems = scratch[9 * count :]
    small = vector_sum(vector, vector_out, vector_lands, vector_sems, (bits, across))
    for color in colors:
        color.begin()
    next(small)
    for stage in range(7):
        for color in colors:
            color.step(stage)
        next(small, None)
    hand_out(colors, outs)


def reduce_all(arrays, orders, vector, collective):
    scratch, outs = color_scratch(arrays)
    scratch.append(pltpu.VMEM((5, *vector.shape), jnp.float32))
    scratch.append(pltpu.SemaphoreType.DMA((2, 5)))
    outs.append(jax.ShapeDtypeStruct(vector.shape, jnp.float32))
    vmem = pl.BlockSpec(memory_space=pltpu.VMEM)
    got = pl.pallas_call(
        functools.partial(reduce_body, len(arrays), orders),
        out_shape=outs,
        in_specs=[pl.BlockSpec(memory_space=pl.ANY)] * len(arrays) + [vmem],
        out_specs=[vmem] * len(outs),
        scratch_shapes=scratch,
        compiler_params=pltpu.CompilerParams(
            collective_id=collective, has_side_effects=True, vmem_limit_bytes=40 << 20
        ),
        cost_estimate=pl.CostEstimate(flops=1 << 34, bytes_accessed=1 << 24, transcendentals=0),
        name="reduce_all",
    )(*arrays, vector)
    return assemble(arrays, got), got[-1]


TIMES = ((3, 12, 16, 18, 20, 22, 23), (4, 12, 16, 18, 20, 22, 23), (5, 8, 11, 14, 17, 20, 23))


def attend_back_reduce_body(count, orders, *refs):
    info_ref, *blocks = refs[:7]
    sources = refs[7 : 7 + count]
    results = refs[7 + count : 10 + count]
    outs = refs[10 + count : 10 + 3 * count]
    dk_acc, dv_acc, *scratch = refs[10 + 3 * count :]
    now = pl.program_id(0) * pl.num_programs(1) + pl.program_id(1)
    bits, across = where_am_i()
    colors = colors_of(sources, scratch, orders)

    @pl.when(now == 0)
    def _():
        greet(across)
        for color in colors:
            color.begin()

    for when in sorted({when for times in TIMES for when in times}):

        @pl.when(now == when)
        def _(when=when):
            for color, times in zip(colors, TIMES):
                for stage in range(6):
                    if times[stage] == when:
                        color.step(stage)

    attend_back_body(info_ref, *blocks, *results, dk_acc, dv_acc)

    @pl.when(now == 23)
    def _():
        for color in colors:
            color.step(6)
        hand_out(colors, outs)


def attend_back_reduce(
    info, queries, keys, values, grad_out, out, log_sums, block, arrays, orders, collective
):
    tokens, width = queries.shape
    total = keys.shape[0]
    pairs = width // PAIR
    scratch, outs = color_scratch(arrays)
    q_spec = pl.BlockSpec((block, PAIR), lambda h, i, n: (i, h))
    k_spec = pl.BlockSpec((total, PAIR), lambda h, i, n: (0, h))
    whole = pl.BlockSpec(memory_space=pltpu.VMEM)
    got = pl.pallas_call(
        functools.partial(attend_back_reduce_body, len(arrays), orders),
        grid_spec=pltpu.PrefetchScalarGridSpec(
            num_scalar_prefetch=1,
            grid=(pairs, tokens // block),
            in_specs=[
                q_spec,
                k_spec,
                k_spec,
                q_spec,
                q_spec,
                pl.BlockSpec((1, 2, block), lambda h, i, n: (h, 0, i)),
                *[pl.BlockSpec(memory_space=pl.ANY)] * len(arrays),
            ],
            out_specs=[q_spec, k_spec, k_spec, *[whole] * len(outs)],
            scratch_shapes=[pltpu.VMEM((total, PAIR), jnp.float32)] * 2 + scratch,
        ),
        out_shape=[
            jax.ShapeDtypeStruct((tokens, width), jnp.bfloat16),
            jax.ShapeDtypeStruct((total, width), jnp.bfloat16),
            jax.ShapeDtypeStruct((total, width), jnp.bfloat16),
            *outs,
        ],
        compiler_params=pltpu.CompilerParams(
            collective_id=collective, has_side_effects=True, vmem_limit_bytes=60 << 20
        ),
        cost_estimate=pl.CostEstimate(
            flops=40 * tokens * total * width, bytes_accessed=1 << 25, transcendentals=0
        ),
        name="attend_back_reduce",
    )(info, queries, keys, values, grad_out, out, log_sums, *arrays)
    return got[:3], assemble(arrays, got[3:])


def feed_body(
    x_ref,
    att_ref,
    cot_ref,
    keep_ref,
    rows_ref,
    inner_bias_ref,
    wo_ref,
    wi_ref,
    wf_ref,
    result_ref,
    normed_ref,
    act_ref,
    g_inner_ref,
    g_ffn_ref,
    g_attn_ref,
    g_att_ref,
    g_hidden_ref,
    sums_ref,
):
    low = jnp.bfloat16
    width = x_ref.shape[1]
    inner_total = inner_bias_ref.shape[1]
    gain, shift = rows_ref[0:1], rows_ref[1:2]
    out_bias, outer_bias = rows_ref[2:3], rows_ref[3:4]
    keep = keep_ref[...]
    branch_attn = dot(att_ref[...], wo_ref[...], NN) + out_bias
    hidden = x_ref[...].astype(jnp.float32) + branch_attn
    centered = hidden - jnp.mean(hidden, axis=-1, keepdims=True)
    spread = lax.rsqrt(jnp.mean(centered * centered, axis=-1, keepdims=True) + EPSILON)
    normal = centered * spread
    normed = (normal * gain + shift).astype(low)
    normed_ref[...] = normed
    g_stream = keep * cot_ref[...].astype(jnp.float32)
    g_ffn = g_stream.astype(low)
    g_ffn_ref[...] = g_ffn
    branch = jnp.zeros_like(hidden) + outer_bias
    g_normed = jnp.zeros_like(hidden)
    sums = []
    for start in range(0, inner_total, width):
        span = slice(start, start + width)
        inner = dot(normed, wi_ref[:, span], NN) + inner_bias_ref[:, span]
        g_act = dot(g_ffn, wf_ref[span, :], NT)
        cdf = 0.5 + 0.5 * lax.erf(inner * (0.5**0.5))
        act = (inner * cdf).astype(low)
        slope = cdf + inner * (jnp.exp(-0.5 * inner * inner) * ((0.5 / jnp.pi) ** 0.5))
        g_inner = (g_act * slope).astype(low)
        act_ref[:, span] = act
        g_inner_ref[:, span] = g_inner
        branch = branch + dot(act, wf_ref[span, :], NN)
        g_normed = g_normed + dot(g_inner, wi_ref[:, span], NT)
        sums.append(jnp.sum(g_inner.astype(jnp.float32), axis=0, keepdims=True))
    stream = keep * (hidden + branch)
    result_ref[...] = stream.astype(low)
    e = g_normed * gain
    g_hidden = g_stream + spread * (
        e
        - jnp.mean(e, axis=-1, keepdims=True)
        - normal * jnp.mean(e * normal, axis=-1, keepdims=True)
    )
    g_hidden_ref[...] = g_hidden
    g_attn = g_hidden.astype(low)
    g_attn_ref[...] = g_attn
    g_att_ref[...] = dot(g_attn, wo_ref[...], NT).astype(low)
    for item in (
        stream * stream,
        keep * branch_attn * branch_attn,
        keep * branch * branch,
        jnp.broadcast_to(keep, hidden.shape),
        g_attn.astype(jnp.float32),
        g_normed * normal,
        g_normed,
        g_ffn.astype(jnp.float32),
    ):
        sums.append(jnp.sum(item, axis=0, keepdims=True))
    block = jnp.concatenate(sums, axis=0)

    @pl.when(pl.program_id(0) == 0)
    def _():
        sums_ref[...] = block

    @pl.when(pl.program_id(0) > 0)
    def _():
        sums_ref[...] += block


def feed(x, att, cot, keep, rows, inner_bias, wo, wi, wf, block):
    tokens, width = x.shape
    inner_total = wi.shape[1]
    low = jnp.bfloat16
    slot = pl.BlockSpec((block, width), lambda i: (i, 0))
    wide = pl.BlockSpec((block, inner_total), lambda i: (i, 0))

    def fixed(shape):
        return pl.BlockSpec(shape, lambda i: (0, 0), pipeline_mode=pl.Buffered(1))

    sums_rows = inner_total // width + 8
    return pl.pallas_call(
        feed_body,
        grid=(tokens // block,),
        in_specs=[
            slot,
            slot,
            slot,
            pl.BlockSpec((block, 1), lambda i: (i, 0)),
            fixed(rows.shape),
            fixed(inner_bias.shape),
            fixed(wo.shape),
            fixed(wi.shape),
            fixed(wf.shape),
        ],
        out_specs=[
            slot,
            slot,
            wide,
            wide,
            slot,
            slot,
            slot,
            slot,
            pl.BlockSpec((sums_rows, width), lambda i: (0, 0)),
        ],
        out_shape=[
            jax.ShapeDtypeStruct((tokens, width), low),
            jax.ShapeDtypeStruct((tokens, width), low),
            jax.ShapeDtypeStruct((tokens, inner_total), low),
            jax.ShapeDtypeStruct((tokens, inner_total), low),
            jax.ShapeDtypeStruct((tokens, width), low),
            jax.ShapeDtypeStruct((tokens, width), low),
            jax.ShapeDtypeStruct((tokens, width), low),
            jax.ShapeDtypeStruct((tokens, width), jnp.float32),
            jax.ShapeDtypeStruct((sums_rows, width), jnp.float32),
        ],
        compiler_params=pltpu.CompilerParams(vmem_limit_bytes=60 << 20),
        cost_estimate=pl.CostEstimate(
            flops=4 * tokens * width * (width + 2 * inner_total),
            bytes_accessed=1 << 25,
            transcendentals=0,
        ),
        name="feed",
    )(x, att, cot, keep, rows, inner_bias, wo, wi, wf)


def local(
    inputs,
    lengths,
    first_gain,
    first_shift,
    query_weight,
    query_bias,
    key_weight,
    value_weight,
    value_bias,
    output_weight,
    output_bias,
    second_gain,
    second_shift,
    inner_weight,
    inner_bias,
    outer_weight,
    outer_bias,
    cotangent,
):
    groups = lax.axis_size("seq")
    seq_count, local_len, width = inputs.shape
    full_len = local_len * groups
    tokens_here = seq_count * local_len
    place = lax.axis_index("seq")
    half = groups // 2
    row = place // half
    across = [(i, (i + half) % groups) for i in range(groups)]
    beside = [(i, i ^ 1) for i in range(groups)]
    there = lax.rem(place + half, groups)
    near = place + 1 - 2 * lax.rem(place, 2)

    def mine_of(array):
        return lax.dynamic_index_in_dim(array, row, 0, keepdims=False)

    def swap(array):
        return lax.ppermute(
            lax.dynamic_index_in_dim(array, 1 - row, 0, keepdims=False), "seq", across
        )

    def give_back(array):
        own = array[:local_len]
        other = lax.ppermute(array[local_len:], "seq", across)
        return jnp.where(row == 0, jnp.stack([own, other]), jnp.stack([other, own]))

    length = lax.dynamic_index_in_dim(lengths, row, 0, keepdims=False)
    starts = jnp.stack(
        [place, there, near, lax.rem(near + half, groups)]
    ).astype(jnp.int32) * local_len
    info = jnp.concatenate([length[None], starts])
    spots = jnp.concatenate(
        [starts[0] + jnp.arange(local_len, dtype=jnp.int32), starts[1] + jnp.arange(local_len, dtype=jnp.int32)]
    )
    keep_rows = (spots < length).astype(jnp.float32)[:, None]
    own_in = mine_of(inputs)
    far_in = swap(inputs)
    cot = jnp.concatenate([mine_of(cotangent), swap(cotangent)], axis=0)

    def project(rows):
        normed = norm_apply(rows.astype(jnp.float32), first_gain, first_shift).astype(jnp.bfloat16)
        q = (
            jnp.dot(normed, query_weight, preferred_element_type=jnp.float32) + query_bias
        ).astype(jnp.bfloat16)
        k = jnp.dot(normed, key_weight, preferred_element_type=jnp.float32).astype(jnp.bfloat16)
        v = (
            jnp.dot(normed, value_weight, preferred_element_type=jnp.float32) + value_bias
        ).astype(jnp.bfloat16)
        return q, k, v

    parts = (project(own_in), project(far_in))
    queries = jnp.concatenate([parts[0][0], parts[1][0]], axis=0)

    def all_keys(index):
        sent = [lax.ppermute(part[index], "seq", beside) for part in parts]
        return jnp.concatenate([parts[0][index], parts[1][index], *sent], axis=0)

    keys = all_keys(1)
    values = all_keys(2)
    both_in = jnp.concatenate([own_in, far_in], axis=0)
    flat_in = both_in.astype(jnp.float32)
    normed_one, norm_one_back = jax.vjp(norm_apply, flat_in, first_gain, first_shift)
    normed_one_low = normed_one.astype(jnp.bfloat16)
    attended, log_sums = attend(info, queries, keys, values, 512)
    (
        stream,
        normed_two,
        activated,
        grad_inner,
        grad_ffn,
        grad_attn,
        grad_attended,
        grad_hidden,
        sums,
    ) = feed(
        both_in,
        attended,
        cot,
        keep_rows,
        jnp.stack([second_gain, second_shift, output_bias, outer_bias]),
        inner_bias[None],
        output_weight,
        inner_weight,
        outer_weight,
        512,
    )
    result = give_back(stream)
    grad_outer_weight = dot(activated, grad_ffn, TN)
    grad_inner_weight = dot(normed_two, grad_inner, TN)
    grad_output_weight = dot(attended, grad_attn, TN)
    data_groups = lax.axis_size("dp")
    linked = data_groups == 8 and groups == 4
    low = jnp.bfloat16
    back_args = (info, queries, keys, values, grad_attended, attended, log_sums, 256)
    grads_early = (
        grad_outer_weight.astype(low),
        grad_inner_weight.astype(low),
        grad_output_weight.astype(low),
    )
    if linked:
        (grad_q_tok, grad_k_part, grad_v_part), sums_early = attend_back_reduce(
            *back_args, grads_early, COLORS, 2
        )
    else:
        grad_q_tok, grad_k_part, grad_v_part = attend_back(*back_args)

    def join(partial):
        far = lax.ppermute(partial[tokens_here:], "seq", beside)
        return (partial[:tokens_here].astype(jnp.float32) + far.astype(jnp.float32)).astype(
            jnp.bfloat16
        )

    grad_k_tok = join(grad_k_part)
    grad_v_tok = join(grad_v_part)
    grads_late = tuple(
        dot(normed_one_low, grad, TN).astype(low) for grad in (grad_q_tok, grad_k_tok, grad_v_tok)
    )
    grad_query_bias = jnp.sum(grad_q_tok, axis=0, dtype=jnp.float32)
    grad_value_bias = jnp.sum(grad_v_tok, axis=0, dtype=jnp.float32)
    grad_normed_one = (
        jnp.einsum("te,de->td", grad_q_tok, query_weight, preferred_element_type=jnp.float32)
        + jnp.einsum("te,de->td", grad_k_tok, key_weight, preferred_element_type=jnp.float32)
        + jnp.einsum("te,de->td", grad_v_tok, value_weight, preferred_element_type=jnp.float32)
    )
    grad_in_norm, grad_first_gain, grad_first_shift = norm_one_back(grad_normed_one)
    grad_inputs = give_back((grad_hidden + grad_in_norm).astype(jnp.bfloat16))
    packed = jnp.concatenate(
        [
            sums,
            jnp.stack([grad_first_gain, grad_first_shift, grad_query_bias, grad_value_bias]),
        ]
    )
    if linked:
        sums_late, packed = reduce_all(grads_late, COLORS, packed, 1)
    else:

        def reduced(partial):
            piece = lax.psum_scatter(partial, ("dp", "seq"), scatter_dimension=0, tiled=True)
            return lax.all_gather(piece, "seq", axis=0, tiled=True).astype(jnp.float32)

        sums_early = [reduced(item) for item in grads_early]
        sums_late = [reduced(item) for item in grads_late]
        packed = lax.psum(packed, ("dp", "seq"))
    summed_outer, summed_inner, summed_output = sums_early
    summed_query, summed_key, summed_value = sums_late
    inner_rows = inner_weight.shape[1] // width
    grad_inner_bias = packed[:inner_rows].reshape(-1)
    tail = packed[inner_rows:]
    denominator = tail[3, 0] * width
    stream_scale = jnp.sqrt(jnp.sum(tail[0]) / denominator)
    attention_scale = jnp.sqrt(jnp.sum(tail[1]) / denominator)
    feedforward_scale = jnp.sqrt(jnp.sum(tail[2]) / denominator)
    return (
        result,
        grad_inputs,
        tail[8],
        tail[9],
        summed_query,
        tail[10],
        summed_key,
        summed_value,
        tail[11],
        summed_output,
        tail[4],
        tail[5],
        tail[6],
        summed_inner,
        grad_inner_bias,
        summed_outer,
        tail[7],
        stream_scale,
        attention_scale,
        feedforward_scale,
    )


def solution(mesh):
    return jax.shard_map(
        local,
        mesh=mesh,
        in_specs=(
            P("dp", "seq", None),
            P("dp"),
            P(),
            P(),
            P(),
            P(),
            P(),
            P(),
            P(),
            P(),
            P(),
            P(),
            P(),
            P(),
            P(),
            P(),
            P(),
            P("dp", "seq", None),
        ),
        out_specs=(
            P("dp", "seq", None),
            P("dp", "seq", None),
            P(),
            P(),
            P("dp", None),
            P(),
            P("dp", None),
            P("dp", None),
            P(),
            P("dp", None),
            P(),
            P(),
            P(),
            P("dp", None),
            P(),
            P("dp", None),
            P(),
            P(),
            P(),
            P(),
        ),
        check_vma=False,
    )
```

```python
import functools

import jax
import jax.numpy as jnp
from jax import lax
from jax.experimental import pallas as pl
from jax.experimental.pallas import tpu as pltpu
from jax.sharding import PartitionSpec as P

HEADS = 12
HEAD_DIM = 64
EPSILON = 1e-12
NEGATIVE = -1e30
PAIR = 2 * HEAD_DIM
NT = ((1,), (1,))
NN = ((1,), (0,))
TN = ((0,), (0,))


def norm_apply(values, gain_vec, shift_vec):
    average = jnp.mean(values, axis=-1, keepdims=True)
    centered = values - average
    spread = jnp.mean(centered * centered, axis=-1, keepdims=True)
    return centered * lax.rsqrt(spread + EPSILON) * gain_vec + shift_vec


def dot(left, right, dims):
    return lax.dot_general(left, right, (dims, ((), ())), preferred_element_type=jnp.float32)


def key_valid(info_ref, keys_total):
    spots = lax.broadcasted_iota(jnp.int32, (keys_total, 1), 0)
    blocks = info_ref.shape[0] - 1
    block_len = keys_total // blocks
    places = spots
    for index in range(blocks):
        inside = (spots >= index * block_len) & (spots < (index + 1) * block_len)
        places = jnp.where(inside, spots - index * block_len + info_ref[index + 1], places)
    return places < info_ref[0]


def attend_body(info_ref, q_ref, k_ref, v_ref, out_ref, lse_ref):
    lane = lax.broadcasted_iota(jnp.int32, (1, PAIR), 1)
    scale = jnp.bfloat16(HEAD_DIM ** (-0.5))
    queries = q_ref[...] * scale
    keys = k_ref[...]
    values_t = v_ref[...].T
    valid = key_valid(info_ref, keys.shape[0])
    outs = []
    for head in range(2):
        mine = (lane < HEAD_DIM) if head == 0 else (lane >= HEAD_DIM)
        scores = dot(keys, jnp.where(mine, queries, jnp.zeros_like(queries)), NT)
        scores = jnp.where(valid, scores, NEGATIVE)
        top = jnp.max(scores, axis=0, keepdims=True)
        weights = jnp.exp(scores - top)
        total = jnp.sum(weights, axis=0, keepdims=True)
        mixed = dot(
            values_t[HEAD_DIM * head : HEAD_DIM * (head + 1)], weights.astype(jnp.bfloat16), NN
        )
        outs.append(mixed * (1.0 / total))
        lse_ref[0, head : head + 1, :] = top + jnp.log(total)
    out_ref[...] = jnp.concatenate(outs, axis=0).T.astype(jnp.bfloat16)


def attend(info, queries, keys, values, block):
    tokens, width = queries.shape
    total = keys.shape[0]
    pairs = width // PAIR
    q_spec = pl.BlockSpec((block, PAIR), lambda h, i, n: (i, h))
    k_spec = pl.BlockSpec((total, PAIR), lambda h, i, n: (0, h))
    return pl.pallas_call(
        attend_body,
        grid_spec=pltpu.PrefetchScalarGridSpec(
            num_scalar_prefetch=1,
            grid=(pairs, tokens // block),
            in_specs=[q_spec, k_spec, k_spec],
            out_specs=[q_spec, pl.BlockSpec((1, 2, block), lambda h, i, n: (h, 0, i))],
        ),
        out_shape=[
            jax.ShapeDtypeStruct((tokens, width), jnp.bfloat16),
            jax.ShapeDtypeStruct((pairs, 2, tokens), jnp.float32),
        ],
        compiler_params=pltpu.CompilerParams(vmem_limit_bytes=48 << 20),
        cost_estimate=pl.CostEstimate(
            flops=16 * tokens * total * width, bytes_accessed=1 << 23, transcendentals=0
        ),
        name="attend",
    )(info, queries, keys, values)


def attend_back_body(
    info_ref,
    q_ref,
    k_ref,
    v_ref,
    do_ref,
    o_ref,
    lse_ref,
    dq_ref,
    dk_ref,
    dv_ref,
    dk_acc,
    dv_acc,
    before=None,
    after=None,
):
    step = pl.program_id(1)
    lane = lax.broadcasted_iota(jnp.int32, (1, PAIR), 1)
    scale = jnp.bfloat16(HEAD_DIM ** (-0.5))
    grad_out = do_ref[...]
    queries = q_ref[...] * scale
    keys = k_ref[...]
    keys_t = keys.T
    values = v_ref[...]
    product = grad_out.astype(jnp.float32) * o_ref[...].astype(jnp.float32)
    pick = (
        lax.broadcasted_iota(jnp.int32, (8, PAIR), 1) // HEAD_DIM
        == lax.broadcasted_iota(jnp.int32, (8, PAIR), 0)
    ).astype(jnp.float32)
    row_sums = lax.dot_general(
        pick,
        product,
        (NT, ((), ())),
        precision=lax.Precision.HIGHEST,
        preferred_element_type=jnp.float32,
    )
    valid = key_valid(info_ref, keys.shape[0])
    zero = jnp.zeros_like(queries)
    grad_k = 0
    grad_v = 0
    grad_q = []
    for head in range(2):
        if before is not None:
            before(head)
        mine = (lane < HEAD_DIM) if head == 0 else (lane >= HEAD_DIM)
        query_h = jnp.where(mine, queries, zero)
        out_h = jnp.where(mine, grad_out, zero)
        scores = jnp.where(valid, dot(keys, query_h, NT), NEGATIVE)
        weights = jnp.exp(scores - lse_ref[0, head : head + 1, :])
        grad_w = dot(values, out_h, NT)
        grad_s = (weights * (grad_w - row_sums[head : head + 1])).astype(jnp.bfloat16)
        grad_v = grad_v + dot(weights.astype(jnp.bfloat16), out_h, NN)
        grad_k = grad_k + dot(grad_s, query_h, NN)
        grad_q.append(dot(keys_t[HEAD_DIM * head : HEAD_DIM * (head + 1)], grad_s, NN))
    grad_q = jnp.concatenate(grad_q, axis=0) * (HEAD_DIM ** (-0.5))
    dq_ref[...] = grad_q.T.astype(jnp.bfloat16)

    @pl.when(step == 0)
    def _():
        dk_acc[...] = grad_k
        dv_acc[...] = grad_v

    @pl.when(step > 0)
    def _():
        dk_acc[...] += grad_k
        dv_acc[...] += grad_v

    @pl.when(step == pl.num_programs(1) - 1)
    def _():
        near = dk_ref.shape[0]
        dk_ref[...] = dk_acc[:near].astype(jnp.bfloat16)
        dv_ref[...] = dv_acc[:near].astype(jnp.bfloat16)
        if after is not None:
            after()


def attend_back(info, queries, keys, values, grad_out, out, log_sums, block):
    tokens, width = queries.shape
    total = keys.shape[0]
    pairs = width // PAIR
    q_spec = pl.BlockSpec((block, PAIR), lambda h, i, n: (i, h))
    k_spec = pl.BlockSpec((total, PAIR), lambda h, i, n: (0, h))
    return pl.pallas_call(
        attend_back_body,
        grid_spec=pltpu.PrefetchScalarGridSpec(
            num_scalar_prefetch=1,
            grid=(pairs, tokens // block),
            in_specs=[
                q_spec,
                k_spec,
                k_spec,
                q_spec,
                q_spec,
                pl.BlockSpec((1, 2, block), lambda h, i, n: (h, 0, i)),
            ],
            out_specs=[q_spec, k_spec, k_spec],
            scratch_shapes=[pltpu.VMEM((total, PAIR), jnp.float32)] * 2,
        ),
        out_shape=[
            jax.ShapeDtypeStruct((tokens, width), jnp.bfloat16),
            jax.ShapeDtypeStruct((total, width), jnp.bfloat16),
            jax.ShapeDtypeStruct((total, width), jnp.bfloat16),
        ],
        compiler_params=pltpu.CompilerParams(vmem_limit_bytes=48 << 20),
        cost_estimate=pl.CostEstimate(
            flops=40 * tokens * total * width, bytes_accessed=1 << 24, transcendentals=0
        ),
        name="attend_back",
    )(info, queries, keys, values, grad_out, out, log_sums)


MESH_IDS = pl.DeviceIdType.MESH
AXES = ("zhi", "zlo", "x", "y")
LATE = (("x", "zlo", "y", "zhi"), ("zlo", "x", "y", "zhi"), ("x", "zlo", "zhi", "y"))


def where_am_i():
    data = lax.axis_index("dp")
    seq = lax.axis_index("seq")
    bits = {
        "zhi": data // 4,
        "zlo": (data // 2) % 2,
        "x": data % 2,
        "y": seq // 2,
        "core": seq % 2,
    }

    def across(axis):
        if axis == "core":
            return (data, seq + 1 - 2 * bits["core"])
        if axis == "y":
            return (data, seq + 2 - 4 * bits["y"])
        step = {"zhi": 4, "zlo": 2, "x": 1}[axis]
        return (data + step - 2 * step * bits[axis], seq)

    return bits, across


def spot_of(piece, order):
    bits = {axis: (piece >> (3 - k)) & 1 for k, axis in enumerate(AXES)}
    return sum(bits[axis] << (3 - k) for k, axis in enumerate(order))


class Color:
    def __init__(self, source, acc, lands, gathers, sems, order):
        self.source, self.acc, self.lands, self.gathers = source, acc, lands, gathers
        self.sems, self.order = sems, order
        self.pieces, self.rows, self.cols = acc.shape
        self.bits, self.across = where_am_i()

    def base(self, stage):
        return sum(self.bits[self.order[k]] * (self.pieces >> (k + 1)) for k in range(stage))

    def remote(self, src, dst, slot, axis):
        return pltpu.make_async_remote_copy(
            src_ref=src,
            dst_ref=dst,
            send_sem=self.sems.at[0, slot],
            recv_sem=self.sems.at[1, slot],
            device_id=self.across(axis),
            device_id_type=MESH_IDS,
        )

    def begin(self):
        core = self.bits["core"]
        mine = pl.ds(pl.multiple_of(core * self.cols, 128), self.cols)
        theirs = pl.ds(pl.multiple_of((1 - core) * self.cols, 128), self.cols)
        for piece in range(self.pieces):
            spot = spot_of(piece, self.order)
            span = pl.ds(piece * self.rows, self.rows)
            self.remote(
                self.source.at[span, theirs], self.lands[0].at[spot], 0, "core"
            ).start()
            pltpu.make_async_copy(
                self.source.at[span, mine], self.acc.at[spot], self.sems.at[0, 7]
            ).start()

    def add(self, base, count, land):
        @pl.loop(0, count)
        def _(index):
            total = self.acc[base + index].astype(jnp.float32) + land[index].astype(jnp.float32)
            self.acc[base + index] = total.astype(jnp.bfloat16)

    def transfer(self, stage):
        if stage < 4:
            axis = self.order[stage]
            half = self.pieces >> (stage + 1)
            start = self.base(stage) + (1 - self.bits[axis]) * half
            return self.remote(
                self.acc.at[pl.ds(start, half)], self.lands[stage + 1], stage + 1, axis
            )
        if stage == 4:
            there = self.gathers[0].at[self.bits["y"]]
            return self.remote(self.acc.at[self.base(4)], there, 5, "y")
        return self.remote(self.gathers[0], self.gathers[1], 6, "core")

    def step(self, stage):
        if stage == 0:
            whole = self.remote(self.lands[0], self.lands[0], 0, "core")
            pltpu.make_async_copy(self.acc, self.acc, self.sems.at[0, 7]).wait()
            whole.wait_send()
            whole.wait_recv()
        else:
            self.transfer(stage - 1).wait()
        if stage <= 4:
            self.add(self.base(stage), self.pieces >> stage, self.lands[stage])
        if stage == 4:
            self.gathers[0][self.bits["y"]] = self.acc[self.base(4)]
        if stage < 6:
            self.transfer(stage).start()


def swap_copy(source, landing, sems, across):
    return pltpu.make_async_remote_copy(
        src_ref=source,
        dst_ref=landing,
        send_sem=sems.at[0],
        recv_sem=sems.at[1],
        device_id=across("y"),
        device_id_type=MESH_IDS,
    )


def greet(across):
    barrier = pltpu.get_barrier_semaphore()
    for axis in ("core", *AXES):
        pl.semaphore_signal(barrier, inc=1, device_id=across(axis), device_id_type=MESH_IDS)
    pl.semaphore_wait(barrier, 5)


def color_scratch(arrays):
    scratch = []
    outs = []
    for array in arrays:
        rows, cols = array.shape[0] // 16, array.shape[1] // 2
        scratch.append(pltpu.VMEM((16, rows, cols), jnp.bfloat16))
        for size in (16, 8, 4, 2, 1):
            scratch.append(pltpu.VMEM((size, rows, cols), jnp.bfloat16))
        scratch += [pltpu.VMEM((2, rows, cols), jnp.bfloat16)] * 2
        scratch.append(pltpu.SemaphoreType.DMA((2, 8)))
        outs += [jax.ShapeDtypeStruct((2, rows, cols), jnp.bfloat16)] * 2
    return scratch, outs


def colors_of(sources, scratch, orders):
    colors = []
    for index, source in enumerate(sources):
        acc, *lands = scratch[9 * index : 9 * index + 6]
        gathers = scratch[9 * index + 6 : 9 * index + 8]
        sems = scratch[9 * index + 8]
        colors.append(Color(source, acc, lands, gathers, sems, orders[index]))
    return colors


def hand_out(colors, outs):
    for index, color in enumerate(colors):
        outs[2 * index][...] = color.gathers[0][...]
        outs[2 * index + 1][...] = color.gathers[1][...]


def assemble(arrays, got):
    core = lax.axis_index("seq") % 2
    sums = []
    for index, array in enumerate(arrays):
        mine, other = got[2 * index], got[2 * index + 1]
        rows = array.shape[0] // 8
        left = jnp.where(core == 0, mine, other).reshape(rows, -1)
        right = jnp.where(core == 0, other, mine).reshape(rows, -1)
        sums.append(jnp.concatenate([left, right], axis=1).astype(jnp.float32))
    return sums


def vector_sum(source, held, lands, sems, bits_across):
    bits, across = bits_across
    held[...] = source[...]
    for slot, axis in enumerate(("core", "y", "x", "zlo", "zhi")):
        copy = pltpu.make_async_remote_copy(
            src_ref=held,
            dst_ref=lands.at[slot],
            send_sem=sems.at[0, slot],
            recv_sem=sems.at[1, slot],
            device_id=across(axis),
            device_id_type=MESH_IDS,
        )
        copy.start()
        yield
        copy.wait()
        held[...] = held[...] + lands[slot]


def reduce_body(count, orders, *refs):
    sources, vector, far = refs[:count], refs[count], refs[count + 1]
    outs = refs[count + 2 : count + 2 + 2 * count]
    vector_out, far_out = refs[3 * count + 2 : 3 * count + 4]
    swap_sems, *scratch = refs[3 * count + 4 :]
    bits, across = where_am_i()
    greet(across)
    swap = swap_copy(far, far_out, swap_sems, across)
    swap.start()
    colors = colors_of(sources, scratch, orders)
    vector_lands, vector_sems = scratch[9 * count :]
    small = vector_sum(vector, vector_out, vector_lands, vector_sems, (bits, across))
    for color in colors:
        color.begin()
    next(small)
    for stage in range(7):
        for color in colors:
            color.step(stage)
        next(small, None)
    hand_out(colors, outs)
    swap.wait()


def reduce_all(arrays, orders, vector, far, collective):
    scratch, outs = color_scratch(arrays)
    scratch.append(pltpu.VMEM((5, *vector.shape), jnp.float32))
    scratch.append(pltpu.SemaphoreType.DMA((2, 5)))
    outs.append(jax.ShapeDtypeStruct(vector.shape, jnp.float32))
    outs.append(jax.ShapeDtypeStruct(far.shape, far.dtype))
    anywhere = pl.BlockSpec(memory_space=pl.ANY)
    vmem = pl.BlockSpec(memory_space=pltpu.VMEM)
    got = pl.pallas_call(
        functools.partial(reduce_body, len(arrays), orders),
        out_shape=outs,
        in_specs=[*[anywhere] * len(arrays), vmem, anywhere],
        out_specs=[*[vmem] * (len(outs) - 1), anywhere],
        scratch_shapes=[pltpu.SemaphoreType.DMA((2,)), *scratch],
        compiler_params=pltpu.CompilerParams(
            collective_id=collective, has_side_effects=True, vmem_limit_bytes=40 << 20
        ),
        cost_estimate=pl.CostEstimate(flops=1 << 34, bytes_accessed=1 << 24, transcendentals=0),
        name="reduce_all",
    )(*arrays, vector, far)
    return assemble(arrays, got), got[-2], got[-1]


TIMES = ((3, 11, 15, 17, 20, 22, 24), (4, 12, 16, 18, 21, 22, 24), (5, 8, 10, 13, 16, 19, 21))
EARLY = (("x", "y", "zlo", "zhi"), ("zlo", "x", "y", "zhi"), ("y", "x", "zlo", "zhi"))


def attend_back_reduce_body(count, orders, *refs):
    info_ref, *blocks = refs[:7]
    swap_in, *sources = refs[7 : 8 + count]
    results = refs[8 + count : 11 + count]
    outs = refs[11 + count : 11 + 3 * count]
    far = refs[11 + 3 * count : 13 + 3 * count]
    swap_out = refs[13 + 3 * count]
    dk_acc, dv_acc, send_k, send_v, trade_sems, swap_sems, *scratch = refs[14 + 3 * count :]
    pair = pl.program_id(0)
    pairs = pl.num_programs(0)
    now = 2 * (pair * pl.num_programs(1) + pl.program_id(1))
    last = 2 * pairs * pl.num_programs(1)
    bits, across = where_am_i()
    colors = colors_of(sources, scratch, orders)

    def trade(index, which):
        return pltpu.make_async_remote_copy(
            src_ref=(send_k, send_v)[which].at[index],
            dst_ref=far[which].at[:, pl.ds(pl.multiple_of(index * PAIR, PAIR), PAIR)],
            send_sem=trade_sems.at[0, which, index],
            recv_sem=trade_sems.at[1, which, index],
            device_id=across("core"),
            device_id_type=MESH_IDS,
        )

    def before(head):
        if head == 0:

            @pl.when(now == 0)
            def _():
                greet(across)
                swap_copy(swap_in, swap_out, swap_sems, across).start()
                for color in colors:
                    color.begin()

        for when in sorted({when for times in TIMES for when in times if when % 2 == head}):

            @pl.when(now + head == when)
            def _(when=when):
                for color, times in zip(colors, TIMES):
                    for stage in range(7):
                        if times[stage] == when:
                            color.step(stage)

    def after():
        near = results[1].shape[0]
        send_k[pair] = dk_acc[near:].astype(jnp.bfloat16)
        send_v[pair] = dv_acc[near:].astype(jnp.bfloat16)
        trade(pair, 0).start()
        trade(pair, 1).start()

    attend_back_body(info_ref, *blocks, *results, dk_acc, dv_acc, before, after)

    @pl.when(now + 2 == last)
    def _():
        for color, times in zip(colors, TIMES):
            for stage in range(7):
                if times[stage] >= last:
                    color.step(stage)
        hand_out(colors, outs)
        swap_copy(swap_in, swap_out, swap_sems, across).wait()

        @pl.loop(0, pairs)
        def _(index):
            trade(index, 0).wait()
            trade(index, 1).wait()


def attend_back_reduce(
    info, queries, keys, values, grad_out, out, log_sums, block, swap, arrays, orders, collective
):
    tokens, width = queries.shape
    total = keys.shape[0]
    near = total // 2
    pairs = width // PAIR
    scratch, outs = color_scratch(arrays)
    q_spec = pl.BlockSpec((block, PAIR), lambda h, i, n: (i, h))
    k_spec = pl.BlockSpec((total, PAIR), lambda h, i, n: (0, h))
    near_spec = pl.BlockSpec((near, PAIR), lambda h, i, n: (0, h))
    whole = pl.BlockSpec(memory_space=pltpu.VMEM)
    anywhere = pl.BlockSpec(memory_space=pl.ANY)
    far = jax.ShapeDtypeStruct((near, width), jnp.bfloat16)
    got = pl.pallas_call(
        functools.partial(attend_back_reduce_body, len(arrays), orders),
        grid_spec=pltpu.PrefetchScalarGridSpec(
            num_scalar_prefetch=1,
            grid=(pairs, tokens // block),
            in_specs=[
                q_spec,
                k_spec,
                k_spec,
                q_spec,
                q_spec,
                pl.BlockSpec((1, 2, block), lambda h, i, n: (h, 0, i)),
                *[anywhere] * (1 + len(arrays)),
            ],
            out_specs=[q_spec, near_spec, near_spec, *[whole] * len(outs), *[anywhere] * 3],
            scratch_shapes=[
                pltpu.VMEM((total, PAIR), jnp.float32),
                pltpu.VMEM((total, PAIR), jnp.float32),
                pltpu.VMEM((pairs, near, PAIR), jnp.bfloat16),
                pltpu.VMEM((pairs, near, PAIR), jnp.bfloat16),
                pltpu.SemaphoreType.DMA((2, 2, pairs)),
                pltpu.SemaphoreType.DMA((2,)),
                *scratch,
            ],
        ),
        out_shape=[
            jax.ShapeDtypeStruct((tokens, width), jnp.bfloat16),
            jax.ShapeDtypeStruct((near, width), jnp.bfloat16),
            jax.ShapeDtypeStruct((near, width), jnp.bfloat16),
            *outs,
            far,
            far,
            jax.ShapeDtypeStruct(swap.shape, swap.dtype),
        ],
        compiler_params=pltpu.CompilerParams(
            collective_id=collective, has_side_effects=True, vmem_limit_bytes=62 << 20
        ),
        cost_estimate=pl.CostEstimate(
            flops=40 * tokens * total * width, bytes_accessed=1 << 25, transcendentals=0
        ),
        name="attend_back_reduce",
    )(info, queries, keys, values, grad_out, out, log_sums, swap, *arrays)

    def joined(own, other):
        return (own.astype(jnp.float32) + other.astype(jnp.float32)).astype(jnp.bfloat16)

    grads = (got[0], joined(got[1], got[-3]), joined(got[2], got[-2]))
    return grads, got[-1], assemble(arrays, got[3:-3])


def feed_body(
    x_ref,
    att_ref,
    cot_ref,
    keep_ref,
    rows_ref,
    inner_bias_ref,
    wo_ref,
    wi_ref,
    wf_ref,
    result_ref,
    normed_ref,
    act_ref,
    g_inner_ref,
    g_ffn_ref,
    g_attn_ref,
    g_att_ref,
    g_hidden_ref,
    sums_ref,
):
    low = jnp.bfloat16
    width = x_ref.shape[1]
    inner_total = inner_bias_ref.shape[1]
    gain, shift = rows_ref[0:1], rows_ref[1:2]
    out_bias, outer_bias = rows_ref[2:3], rows_ref[3:4]
    keep = keep_ref[...]
    branch_attn = dot(att_ref[...], wo_ref[...], NN) + out_bias
    hidden = x_ref[...].astype(jnp.float32) + branch_attn
    centered = hidden - jnp.mean(hidden, axis=-1, keepdims=True)
    spread = lax.rsqrt(jnp.mean(centered * centered, axis=-1, keepdims=True) + EPSILON)
    normal = centered * spread
    normed = (normal * gain + shift).astype(low)
    normed_ref[...] = normed
    g_stream = keep * cot_ref[...].astype(jnp.float32)
    g_ffn = g_stream.astype(low)
    g_ffn_ref[...] = g_ffn
    branch = jnp.zeros_like(hidden) + outer_bias
    g_normed = jnp.zeros_like(hidden)
    sums = []
    for start in range(0, inner_total, width):
        span = slice(start, start + width)
        inner = dot(normed, wi_ref[:, span], NN) + inner_bias_ref[:, span]
        g_act = dot(g_ffn, wf_ref[span, :], NT)
        cdf = 0.5 + 0.5 * lax.erf(inner * (0.5**0.5))
        act = (inner * cdf).astype(low)
        slope = cdf + inner * (jnp.exp(-0.5 * inner * inner) * ((0.5 / jnp.pi) ** 0.5))
        g_inner = (g_act * slope).astype(low)
        act_ref[:, span] = act
        g_inner_ref[:, span] = g_inner
        branch = branch + dot(act, wf_ref[span, :], NN)
        g_normed = g_normed + dot(g_inner, wi_ref[:, span], NT)
        sums.append(jnp.sum(g_inner.astype(jnp.float32), axis=0, keepdims=True))
    stream = keep * (hidden + branch)
    result_ref[...] = stream.astype(low)
    e = g_normed * gain
    g_hidden = g_stream + spread * (
        e
        - jnp.mean(e, axis=-1, keepdims=True)
        - normal * jnp.mean(e * normal, axis=-1, keepdims=True)
    )
    g_hidden_ref[...] = g_hidden
    g_attn = g_hidden.astype(low)
    g_attn_ref[...] = g_attn
    g_att_ref[...] = dot(g_attn, wo_ref[...], NT).astype(low)
    for item in (
        stream * stream,
        keep * branch_attn * branch_attn,
        keep * branch * branch,
        jnp.broadcast_to(keep, hidden.shape),
        g_attn.astype(jnp.float32),
        g_normed * normal,
        g_normed,
        g_ffn.astype(jnp.float32),
    ):
        sums.append(jnp.sum(item, axis=0, keepdims=True))
    block = jnp.concatenate(sums, axis=0)

    @pl.when(pl.program_id(0) == 0)
    def _():
        sums_ref[...] = block

    @pl.when(pl.program_id(0) > 0)
    def _():
        sums_ref[...] += block


def feed(x, att, cot, keep, rows, inner_bias, wo, wi, wf, block):
    tokens, width = x.shape
    inner_total = wi.shape[1]
    low = jnp.bfloat16
    slot = pl.BlockSpec((block, width), lambda i: (i, 0))
    wide = pl.BlockSpec((block, inner_total), lambda i: (i, 0))

    def fixed(shape):
        return pl.BlockSpec(shape, lambda i: (0, 0), pipeline_mode=pl.Buffered(1))

    sums_rows = inner_total // width + 8
    return pl.pallas_call(
        feed_body,
        grid=(tokens // block,),
        in_specs=[
            slot,
            slot,
            slot,
            pl.BlockSpec((block, 1), lambda i: (i, 0)),
            fixed(rows.shape),
            fixed(inner_bias.shape),
            fixed(wo.shape),
            fixed(wi.shape),
            fixed(wf.shape),
        ],
        out_specs=[
            slot,
            slot,
            wide,
            wide,
            slot,
            slot,
            slot,
            slot,
            pl.BlockSpec((sums_rows, width), lambda i: (0, 0)),
        ],
        out_shape=[
            jax.ShapeDtypeStruct((tokens, width), low),
            jax.ShapeDtypeStruct((tokens, width), low),
            jax.ShapeDtypeStruct((tokens, inner_total), low),
            jax.ShapeDtypeStruct((tokens, inner_total), low),
            jax.ShapeDtypeStruct((tokens, width), low),
            jax.ShapeDtypeStruct((tokens, width), low),
            jax.ShapeDtypeStruct((tokens, width), low),
            jax.ShapeDtypeStruct((tokens, width), jnp.float32),
            jax.ShapeDtypeStruct((sums_rows, width), jnp.float32),
        ],
        compiler_params=pltpu.CompilerParams(vmem_limit_bytes=60 << 20),
        cost_estimate=pl.CostEstimate(
            flops=4 * tokens * width * (width + 2 * inner_total),
            bytes_accessed=1 << 25,
            transcendentals=0,
        ),
        name="feed",
    )(x, att, cot, keep, rows, inner_bias, wo, wi, wf)


def local(
    inputs,
    lengths,
    first_gain,
    first_shift,
    query_weight,
    query_bias,
    key_weight,
    value_weight,
    value_bias,
    output_weight,
    output_bias,
    second_gain,
    second_shift,
    inner_weight,
    inner_bias,
    outer_weight,
    outer_bias,
    cotangent,
):
    groups = lax.axis_size("seq")
    seq_count, local_len, width = inputs.shape
    full_len = local_len * groups
    tokens_here = seq_count * local_len
    place = lax.axis_index("seq")
    half = groups // 2
    row = place // half
    across = [(i, (i + half) % groups) for i in range(groups)]
    beside = [(i, i ^ 1) for i in range(groups)]
    there = lax.rem(place + half, groups)
    near = place + 1 - 2 * lax.rem(place, 2)

    def mine_of(array):
        return lax.dynamic_index_in_dim(array, row, 0, keepdims=False)

    def swap(array):
        return lax.ppermute(
            lax.dynamic_index_in_dim(array, 1 - row, 0, keepdims=False), "seq", across
        )

    def in_order(own, other):
        return jnp.where(row == 0, jnp.stack([own, other]), jnp.stack([other, own]))

    def give_back(array):
        return in_order(array[:local_len], lax.ppermute(array[local_len:], "seq", across))

    length = lax.dynamic_index_in_dim(lengths, row, 0, keepdims=False)
    starts = jnp.stack(
        [place, there, near, lax.rem(near + half, groups)]
    ).astype(jnp.int32) * local_len
    info = jnp.concatenate([length[None], starts])
    spots = jnp.concatenate(
        [starts[0] + jnp.arange(local_len, dtype=jnp.int32), starts[1] + jnp.arange(local_len, dtype=jnp.int32)]
    )
    keep_rows = (spots < length).astype(jnp.float32)[:, None]
    own_in = mine_of(inputs)
    far_in = swap(inputs)
    cot = jnp.concatenate([mine_of(cotangent), swap(cotangent)], axis=0)

    def project(rows):
        normed = norm_apply(rows.astype(jnp.float32), first_gain, first_shift).astype(jnp.bfloat16)
        q = (
            jnp.dot(normed, query_weight, preferred_element_type=jnp.float32) + query_bias
        ).astype(jnp.bfloat16)
        k = jnp.dot(normed, key_weight, preferred_element_type=jnp.float32).astype(jnp.bfloat16)
        v = (
            jnp.dot(normed, value_weight, preferred_element_type=jnp.float32) + value_bias
        ).astype(jnp.bfloat16)
        return q, k, v

    parts = (project(own_in), project(far_in))
    queries = jnp.concatenate([parts[0][0], parts[1][0]], axis=0)

    def all_keys(index):
        sent = [lax.ppermute(part[index], "seq", beside) for part in parts]
        return jnp.concatenate([parts[0][index], parts[1][index], *sent], axis=0)

    keys = all_keys(1)
    values = all_keys(2)
    both_in = jnp.concatenate([own_in, far_in], axis=0)
    flat_in = both_in.astype(jnp.float32)
    normed_one, norm_one_back = jax.vjp(norm_apply, flat_in, first_gain, first_shift)
    normed_one_low = normed_one.astype(jnp.bfloat16)
    attended, log_sums = attend(info, queries, keys, values, 512)
    (
        stream,
        normed_two,
        activated,
        grad_inner,
        grad_ffn,
        grad_attn,
        grad_attended,
        grad_hidden,
        sums,
    ) = feed(
        both_in,
        attended,
        cot,
        keep_rows,
        jnp.stack([second_gain, second_shift, output_bias, outer_bias]),
        inner_bias[None],
        output_weight,
        inner_weight,
        outer_weight,
        512,
    )
    grad_outer_weight = dot(activated, grad_ffn, TN)
    grad_inner_weight = dot(normed_two, grad_inner, TN)
    grad_output_weight = dot(attended, grad_attn, TN)
    data_groups = lax.axis_size("dp")
    linked = data_groups == 8 and groups == 4
    low = jnp.bfloat16
    back_args = (info, queries, keys, values, grad_attended, attended, log_sums, 512)
    grads_early = (
        grad_outer_weight.astype(low),
        grad_inner_weight.astype(low),
        grad_output_weight.astype(low),
    )
    def join(partial):
        far = lax.ppermute(partial[tokens_here:], "seq", beside)
        return (partial[:tokens_here].astype(jnp.float32) + far.astype(jnp.float32)).astype(
            jnp.bfloat16
        )

    if linked:
        (grad_q_tok, grad_k_tok, grad_v_tok), other_result, sums_early = attend_back_reduce(
            *back_args, stream[local_len:], grads_early, EARLY, 2
        )
        result = in_order(stream[:local_len], other_result)
    else:
        grad_q_tok, grad_k_part, grad_v_part = attend_back(*back_args)
        grad_k_tok, grad_v_tok = join(grad_k_part), join(grad_v_part)

    grads_late = tuple(
        dot(normed_one_low, grad, TN).astype(low) for grad in (grad_q_tok, grad_k_tok, grad_v_tok)
    )
    grad_query_bias = jnp.sum(grad_q_tok, axis=0, dtype=jnp.float32)
    grad_value_bias = jnp.sum(grad_v_tok, axis=0, dtype=jnp.float32)
    grad_normed_one = (
        jnp.einsum("te,de->td", grad_q_tok, query_weight, preferred_element_type=jnp.float32)
        + jnp.einsum("te,de->td", grad_k_tok, key_weight, preferred_element_type=jnp.float32)
        + jnp.einsum("te,de->td", grad_v_tok, value_weight, preferred_element_type=jnp.float32)
    )
    grad_in_norm, grad_first_gain, grad_first_shift = norm_one_back(grad_normed_one)
    grad_in = (grad_hidden + grad_in_norm).astype(jnp.bfloat16)
    packed = jnp.concatenate(
        [
            sums,
            jnp.stack([grad_first_gain, grad_first_shift, grad_query_bias, grad_value_bias]),
        ]
    )
    if linked:
        sums_late, packed, other_in = reduce_all(grads_late, LATE, packed, grad_in[local_len:], 1)
        grad_inputs = in_order(grad_in[:local_len], other_in)
    else:

        def reduced(partial):
            piece = lax.psum_scatter(partial, ("dp", "seq"), scatter_dimension=0, tiled=True)
            return lax.all_gather(piece, "seq", axis=0, tiled=True).astype(jnp.float32)

        result = give_back(stream)
        grad_inputs = give_back(grad_in)
        sums_early = [reduced(item) for item in grads_early]
        sums_late = [reduced(item) for item in grads_late]
        packed = lax.psum(packed, ("dp", "seq"))
    summed_outer, summed_inner, summed_output = sums_early
    summed_query, summed_key, summed_value = sums_late
    inner_rows = inner_weight.shape[1] // width
    grad_inner_bias = packed[:inner_rows].reshape(-1)
    tail = packed[inner_rows:]
    denominator = tail[3, 0] * width
    stream_scale = jnp.sqrt(jnp.sum(tail[0]) / denominator)
    attention_scale = jnp.sqrt(jnp.sum(tail[1]) / denominator)
    feedforward_scale = jnp.sqrt(jnp.sum(tail[2]) / denominator)
    return (
        result,
        grad_inputs,
        tail[8],
        tail[9],
        summed_query,
        tail[10],
        summed_key,
        summed_value,
        tail[11],
        summed_output,
        tail[4],
        tail[5],
        tail[6],
        summed_inner,
        grad_inner_bias,
        summed_outer,
        tail[7],
        stream_scale,
        attention_scale,
        feedforward_scale,
    )


def solution(mesh):
    return jax.shard_map(
        local,
        mesh=mesh,
        in_specs=(
            P("dp", "seq", None),
            P("dp"),
            P(),
            P(),
            P(),
            P(),
            P(),
            P(),
            P(),
            P(),
            P(),
            P(),
            P(),
            P(),
            P(),
            P(),
            P(),
            P("dp", "seq", None),
        ),
        out_specs=(
            P("dp", "seq", None),
            P("dp", "seq", None),
            P(),
            P(),
            P("dp", None),
            P(),
            P("dp", None),
            P("dp", None),
            P(),
            P("dp", None),
            P(),
            P(),
            P(),
            P("dp", None),
            P(),
            P("dp", None),
            P(),
            P(),
            P(),
            P(),
        ),
        check_vma=False,
    )
```

```python
import functools

import jax
import jax.numpy as jnp
from jax import lax
from jax.experimental import pallas as pl
from jax.experimental.pallas import tpu as pltpu
from jax.sharding import PartitionSpec as P

HEADS = 12
HEAD_DIM = 64
EPSILON = 1e-12
NEGATIVE = -1e30
PAIR = 2 * HEAD_DIM
NT = ((1,), (1,))
NN = ((1,), (0,))
TN = ((0,), (0,))


def norm_apply(values, gain_vec, shift_vec):
    average = jnp.mean(values, axis=-1, keepdims=True)
    centered = values - average
    spread = jnp.mean(centered * centered, axis=-1, keepdims=True)
    return centered * lax.rsqrt(spread + EPSILON) * gain_vec + shift_vec


def dot(left, right, dims):
    return lax.dot_general(left, right, (dims, ((), ())), preferred_element_type=jnp.float32)


def block_places():
    seq = lax.axis_index("seq")
    beside = seq + 1 - 2 * lax.rem(seq, 2)
    return seq, lax.rem(seq + 2, 4), beside, lax.rem(beside + 2, 4)


def own_length(lengths_ref):
    return lengths_ref[lax.axis_index("seq") // 2]


def key_valid(lengths_ref, keys_total):
    block = keys_total // 4
    spots = lax.broadcasted_iota(jnp.int32, (keys_total, 1), 0)
    shift = 0
    for index, place in enumerate(block_places()):
        shift = jnp.where(spots >= index * block, (place - index) * block, shift)
    return spots + shift < own_length(lengths_ref)


def attend_body(
    info_ref, q_ref, k_ref, v_ref, cot_ref, out_ref, lse_ref, far_ref, swap_sems
):
    bits, across = where_am_i()
    swap = swap_copy(cot_ref.at[1 - bits["y"]], far_ref, swap_sems, across)
    now = pl.program_id(0) * pl.num_programs(1) + pl.program_id(1)

    @pl.when(now == 0)
    def _():
        greet(across, ("y",))
        swap.start()

    lane = lax.broadcasted_iota(jnp.int32, (1, PAIR), 1)
    scale = jnp.bfloat16(HEAD_DIM ** (-0.5))
    queries = q_ref[...] * scale
    keys = k_ref[...]
    values_t = v_ref[...].T
    valid = key_valid(info_ref, keys.shape[0])
    outs = []
    for head in range(2):
        mine = (lane < HEAD_DIM) if head == 0 else (lane >= HEAD_DIM)
        scores = dot(keys, jnp.where(mine, queries, jnp.zeros_like(queries)), NT)
        scores = jnp.where(valid, scores, NEGATIVE)
        top = jnp.max(scores, axis=0, keepdims=True)
        weights = jnp.exp(scores - top)
        total = jnp.sum(weights, axis=0, keepdims=True)
        mixed = dot(
            values_t[HEAD_DIM * head : HEAD_DIM * (head + 1)], weights.astype(jnp.bfloat16), NN
        )
        outs.append(mixed * (1.0 / total))
        lse_ref[0, head : head + 1, :] = top + jnp.log(total)
    out_ref[...] = jnp.concatenate(outs, axis=0).T.astype(jnp.bfloat16)

    @pl.when(now == pl.num_programs(0) * pl.num_programs(1) - 1)
    def _():
        swap.wait()


def attend(info, queries, keys, values, cotangent, block, collective):
    tokens, width = queries.shape
    total = keys.shape[0]
    pairs = width // PAIR
    q_spec = pl.BlockSpec((block, PAIR), lambda h, i, n: (i, h))
    k_spec = pl.BlockSpec((total, PAIR), lambda h, i, n: (0, h))
    return pl.pallas_call(
        attend_body,
        grid_spec=pltpu.PrefetchScalarGridSpec(
            num_scalar_prefetch=1,
            grid=(pairs, tokens // block),
            in_specs=[q_spec, k_spec, k_spec, pl.BlockSpec(memory_space=pl.ANY)],
            out_specs=[
                q_spec,
                pl.BlockSpec((1, 2, block), lambda h, i, n: (h, 0, i)),
                pl.BlockSpec(memory_space=pl.ANY),
            ],
            scratch_shapes=[pltpu.SemaphoreType.DMA((2,))],
        ),
        out_shape=[
            jax.ShapeDtypeStruct((tokens, width), jnp.bfloat16),
            jax.ShapeDtypeStruct((pairs, 2, tokens), jnp.float32),
            jax.ShapeDtypeStruct(cotangent.shape[1:], cotangent.dtype),
        ],
        compiler_params=pltpu.CompilerParams(
            collective_id=collective, has_side_effects=True, vmem_limit_bytes=48 << 20
        ),
        cost_estimate=pl.CostEstimate(
            flops=16 * tokens * total * width, bytes_accessed=1 << 23, transcendentals=0
        ),
        name="attend",
    )(info, queries, keys, values, cotangent)


def attend_back_body(
    info_ref,
    q_ref,
    k_ref,
    v_ref,
    do_ref,
    o_ref,
    lse_ref,
    dq_ref,
    dk_ref,
    dv_ref,
    dk_acc,
    dv_acc,
    before=None,
    after=None,
):
    step = pl.program_id(1)
    lane = lax.broadcasted_iota(jnp.int32, (1, PAIR), 1)
    scale = jnp.bfloat16(HEAD_DIM ** (-0.5))
    grad_out = do_ref[...]
    queries = q_ref[...] * scale
    keys = k_ref[...]
    keys_t = keys.T
    values = v_ref[...]
    product = grad_out.astype(jnp.float32) * o_ref[...].astype(jnp.float32)
    pick = (
        lax.broadcasted_iota(jnp.int32, (8, PAIR), 1) // HEAD_DIM
        == lax.broadcasted_iota(jnp.int32, (8, PAIR), 0)
    ).astype(jnp.float32)
    row_sums = lax.dot_general(
        pick,
        product,
        (NT, ((), ())),
        precision=lax.Precision.HIGHEST,
        preferred_element_type=jnp.float32,
    )
    valid = key_valid(info_ref, keys.shape[0])
    zero = jnp.zeros_like(queries)
    grad_k = 0
    grad_v = 0
    grad_q = []
    for head in range(2):
        if before is not None:
            before(head)
        mine = (lane < HEAD_DIM) if head == 0 else (lane >= HEAD_DIM)
        query_h = jnp.where(mine, queries, zero)
        out_h = jnp.where(mine, grad_out, zero)
        scores = jnp.where(valid, dot(keys, query_h, NT), NEGATIVE)
        weights = jnp.exp(scores - lse_ref[0, head : head + 1, :])
        grad_w = dot(values, out_h, NT)
        grad_s = (weights * (grad_w - row_sums[head : head + 1])).astype(jnp.bfloat16)
        grad_v = grad_v + dot(weights.astype(jnp.bfloat16), out_h, NN)
        grad_k = grad_k + dot(grad_s, query_h, NN)
        grad_q.append(dot(keys_t[HEAD_DIM * head : HEAD_DIM * (head + 1)], grad_s, NN))
    grad_q = jnp.concatenate(grad_q, axis=0) * (HEAD_DIM ** (-0.5))
    dq_ref[...] = grad_q.T.astype(jnp.bfloat16)

    @pl.when(step == 0)
    def _():
        dk_acc[...] = grad_k
        dv_acc[...] = grad_v

    @pl.when(step > 0)
    def _():
        dk_acc[...] += grad_k
        dv_acc[...] += grad_v

    @pl.when(step == pl.num_programs(1) - 1)
    def _():
        near = dk_ref.shape[0]
        dk_ref[...] = dk_acc[:near].astype(jnp.bfloat16)
        dv_ref[...] = dv_acc[:near].astype(jnp.bfloat16)
        if after is not None:
            after()


def attend_back(info, queries, keys, values, grad_out, out, log_sums, block):
    tokens, width = queries.shape
    total = keys.shape[0]
    pairs = width // PAIR
    q_spec = pl.BlockSpec((block, PAIR), lambda h, i, n: (i, h))
    k_spec = pl.BlockSpec((total, PAIR), lambda h, i, n: (0, h))
    return pl.pallas_call(
        attend_back_body,
        grid_spec=pltpu.PrefetchScalarGridSpec(
            num_scalar_prefetch=1,
            grid=(pairs, tokens // block),
            in_specs=[
                q_spec,
                k_spec,
                k_spec,
                q_spec,
                q_spec,
                pl.BlockSpec((1, 2, block), lambda h, i, n: (h, 0, i)),
            ],
            out_specs=[q_spec, k_spec, k_spec],
            scratch_shapes=[pltpu.VMEM((total, PAIR), jnp.float32)] * 2,
        ),
        out_shape=[
            jax.ShapeDtypeStruct((tokens, width), jnp.bfloat16),
            jax.ShapeDtypeStruct((total, width), jnp.bfloat16),
            jax.ShapeDtypeStruct((total, width), jnp.bfloat16),
        ],
        compiler_params=pltpu.CompilerParams(vmem_limit_bytes=48 << 20),
        cost_estimate=pl.CostEstimate(
            flops=40 * tokens * total * width, bytes_accessed=1 << 24, transcendentals=0
        ),
        name="attend_back",
    )(info, queries, keys, values, grad_out, out, log_sums)


MESH_IDS = pl.DeviceIdType.MESH
AXES = ("zhi", "zlo", "x", "y")
LATE = (("x", "zlo", "y", "zhi"), ("zlo", "x", "y", "zhi"), ("x", "zlo", "zhi", "y"))


def where_am_i():
    data = lax.axis_index("dp")
    seq = lax.axis_index("seq")
    bits = {
        "zhi": data // 4,
        "zlo": (data // 2) % 2,
        "x": data % 2,
        "y": seq // 2,
        "core": seq % 2,
    }

    def across(axis):
        if axis == "core":
            return (data, seq + 1 - 2 * bits["core"])
        if axis == "y":
            return (data, seq + 2 - 4 * bits["y"])
        step = {"zhi": 4, "zlo": 2, "x": 1}[axis]
        return (data + step - 2 * step * bits[axis], seq)

    return bits, across


def spot_of(piece, order):
    bits = {axis: (piece >> (3 - k)) & 1 for k, axis in enumerate(AXES)}
    return sum(bits[axis] << (3 - k) for k, axis in enumerate(order))


class Color:
    def __init__(self, source, acc, lands, gathers, sems, order):
        self.source, self.acc, self.lands, self.gathers = source, acc, lands, gathers
        self.sems, self.order = sems, order
        self.pieces, self.rows, self.cols = acc.shape
        self.bits, self.across = where_am_i()

    def base(self, stage):
        return sum(self.bits[self.order[k]] * (self.pieces >> (k + 1)) for k in range(stage))

    def remote(self, src, dst, slot, axis):
        return pltpu.make_async_remote_copy(
            src_ref=src,
            dst_ref=dst,
            send_sem=self.sems.at[0, slot],
            recv_sem=self.sems.at[1, slot],
            device_id=self.across(axis),
            device_id_type=MESH_IDS,
        )

    def begin(self):
        core = self.bits["core"]
        mine = pl.ds(pl.multiple_of(core * self.cols, 128), self.cols)
        theirs = pl.ds(pl.multiple_of((1 - core) * self.cols, 128), self.cols)
        for piece in range(self.pieces):
            spot = spot_of(piece, self.order)
            span = pl.ds(piece * self.rows, self.rows)
            self.remote(
                self.source.at[span, theirs], self.lands[0].at[spot], 0, "core"
            ).start()
            pltpu.make_async_copy(
                self.source.at[span, mine], self.acc.at[spot], self.sems.at[0, 7]
            ).start()

    def add(self, base, count, land):
        @pl.loop(0, count)
        def _(index):
            total = self.acc[base + index].astype(jnp.float32) + land[index].astype(jnp.float32)
            self.acc[base + index] = total.astype(jnp.bfloat16)

    def transfer(self, stage):
        if stage < 4:
            axis = self.order[stage]
            half = self.pieces >> (stage + 1)
            start = self.base(stage) + (1 - self.bits[axis]) * half
            return self.remote(
                self.acc.at[pl.ds(start, half)], self.lands[stage + 1], stage + 1, axis
            )
        if stage == 4:
            there = self.gathers[0].at[self.bits["y"]]
            return self.remote(self.acc.at[self.base(4)], there, 5, "y")
        return self.remote(self.gathers[0], self.gathers[1], 6, "core")

    def step(self, stage):
        if stage == 0:
            whole = self.remote(self.lands[0], self.lands[0], 0, "core")
            pltpu.make_async_copy(self.acc, self.acc, self.sems.at[0, 7]).wait()
            whole.wait_send()
            whole.wait_recv()
        else:
            self.transfer(stage - 1).wait()
        if stage <= 4:
            self.add(self.base(stage), self.pieces >> stage, self.lands[stage])
        if stage == 4:
            self.gathers[0][self.bits["y"]] = self.acc[self.base(4)]
        if stage < 6:
            self.transfer(stage).start()


def swap_copy(source, landing, sems, across):
    return pltpu.make_async_remote_copy(
        src_ref=source,
        dst_ref=landing,
        send_sem=sems.at[0],
        recv_sem=sems.at[1],
        device_id=across("y"),
        device_id_type=MESH_IDS,
    )


def greet(across, axes=("core", *AXES)):
    barrier = pltpu.get_barrier_semaphore()
    for axis in axes:
        pl.semaphore_signal(barrier, inc=1, device_id=across(axis), device_id_type=MESH_IDS)
    pl.semaphore_wait(barrier, len(axes))


CHUNKS = 4


def enter_body(
    in_ref,
    gain_ref,
    shift_ref,
    q_bias_ref,
    v_bias_ref,
    wq_ref,
    wk_ref,
    wv_ref,
    x_ref,
    normed_ref,
    q_ref,
    k_ref,
    v_ref,
    swap_sems,
    own_sem,
    trade_sems,
):
    low = jnp.bfloat16
    bits, across = where_am_i()
    row = bits["y"]
    size = x_ref.shape[0] // CHUNKS
    tokens = x_ref.shape[0]
    half = CHUNKS // 2
    own = pltpu.make_async_copy(in_ref.at[row], x_ref.at[pl.ds(0, tokens // 2)], own_sem)
    own.start()
    greet(across, ("core", "y"))

    def arrival(chunk):
        return pltpu.make_async_remote_copy(
            src_ref=in_ref.at[1 - row, pl.ds(pl.multiple_of(chunk * size, size), size)],
            dst_ref=x_ref.at[pl.ds(pl.multiple_of((half + chunk) * size, size), size)],
            send_sem=swap_sems.at[0, chunk],
            recv_sem=swap_sems.at[1, chunk],
            device_id=across("y"),
            device_id_type=MESH_IDS,
        )

    def trade(chunk, which):
        ref = (k_ref, v_ref)[which]
        return pltpu.make_async_remote_copy(
            src_ref=ref.at[pl.ds(pl.multiple_of(chunk * size, size), size)],
            dst_ref=ref.at[pl.ds(pl.multiple_of(tokens + chunk * size, size), size)],
            send_sem=trade_sems.at[0, which, chunk],
            recv_sem=trade_sems.at[1, which, chunk],
            device_id=across("core"),
            device_id_type=MESH_IDS,
        )

    for chunk in range(half):
        arrival(chunk).start()
    own.wait()

    @pl.loop(0, CHUNKS)
    def _(chunk):
        @pl.when(chunk >= half)
        def _():
            arrival(chunk - half).wait()

        span = pl.ds(pl.multiple_of(chunk * size, size), size)
        rows = x_ref[span, :].astype(jnp.float32)
        normed = norm_apply(rows, gain_ref[...], shift_ref[...]).astype(low)
        normed_ref[span, :] = normed
        k_ref[span, :] = dot(normed, wk_ref[...], NN).astype(low)
        trade(chunk, 0).start()
        v_ref[span, :] = (dot(normed, wv_ref[...], NN) + v_bias_ref[...]).astype(low)
        trade(chunk, 1).start()
        q_ref[span, :] = (dot(normed, wq_ref[...], NN) + q_bias_ref[...]).astype(low)

    @pl.loop(0, CHUNKS)
    def _(chunk):
        trade(chunk, 0).wait()
        trade(chunk, 1).wait()


def enter(inputs, gain, shift, q_bias, v_bias, wq, wk, wv, collective):
    _, local_len, width = inputs.shape
    vmem = pl.BlockSpec(memory_space=pltpu.VMEM)

    def made(blocks):
        return jax.ShapeDtypeStruct((blocks * local_len, width), jnp.bfloat16)

    return pl.pallas_call(
        enter_body,
        out_shape=[made(2), made(2), made(2), made(4), made(4)],
        in_specs=[pl.BlockSpec(memory_space=pl.ANY)] + [vmem] * 7,
        out_specs=[vmem] * 5,
        scratch_shapes=[
            pltpu.SemaphoreType.DMA((2, CHUNKS // 2)),
            pltpu.SemaphoreType.DMA,
            pltpu.SemaphoreType.DMA((2, 2, CHUNKS)),
        ],
        compiler_params=pltpu.CompilerParams(
            collective_id=collective, has_side_effects=True, vmem_limit_bytes=48 << 20
        ),
        name="enter",
    )(inputs, gain[None], shift[None], q_bias[None], v_bias[None], wq, wk, wv)


def color_scratch(arrays):
    scratch = []
    outs = []
    for array in arrays:
        rows, cols = array.shape[0] // 16, array.shape[1] // 2
        scratch.append(pltpu.VMEM((16, rows, cols), jnp.bfloat16))
        for size in (16, 8, 4, 2, 1):
            scratch.append(pltpu.VMEM((size, rows, cols), jnp.bfloat16))
        scratch += [pltpu.VMEM((2, rows, cols), jnp.bfloat16)] * 2
        scratch.append(pltpu.SemaphoreType.DMA((2, 8)))
        outs += [jax.ShapeDtypeStruct((2, rows, cols), jnp.bfloat16)] * 2
    return scratch, outs


def colors_of(sources, scratch, orders):
    colors = []
    for index, source in enumerate(sources):
        acc, *lands = scratch[9 * index : 9 * index + 6]
        gathers = scratch[9 * index + 6 : 9 * index + 8]
        sems = scratch[9 * index + 8]
        colors.append(Color(source, acc, lands, gathers, sems, orders[index]))
    return colors


def hand_out(colors, outs):
    for index, color in enumerate(colors):
        outs[2 * index][...] = color.gathers[0][...]
        outs[2 * index + 1][...] = color.gathers[1][...]


def assemble(arrays, got):
    core = lax.axis_index("seq") % 2
    sums = []
    for index, array in enumerate(arrays):
        mine, other = got[2 * index], got[2 * index + 1]
        rows = array.shape[0] // 8
        left = jnp.where(core == 0, mine, other).reshape(rows, -1)
        right = jnp.where(core == 0, other, mine).reshape(rows, -1)
        sums.append(jnp.concatenate([left, right], axis=1).astype(jnp.float32))
    return sums


def vector_sum(source, held, lands, sems, bits_across):
    bits, across = bits_across
    held[...] = source[...]
    for slot, axis in enumerate(("core", "y", "x", "zlo", "zhi")):
        copy = pltpu.make_async_remote_copy(
            src_ref=held,
            dst_ref=lands.at[slot],
            send_sem=sems.at[0, slot],
            recv_sem=sems.at[1, slot],
            device_id=across(axis),
            device_id_type=MESH_IDS,
        )
        copy.start()
        yield
        copy.wait()
        held[...] = held[...] + lands[slot]


def reduce_body(count, orders, *refs):
    sources, vector, far = refs[:count], refs[count], refs[count + 1]
    outs = refs[count + 2 : count + 2 + 2 * count]
    vector_out, far_out = refs[3 * count + 2 : 3 * count + 4]
    swap_sems, *scratch = refs[3 * count + 4 :]
    bits, across = where_am_i()
    greet(across)
    swap = swap_copy(far, far_out, swap_sems, across)
    swap.start()
    colors = colors_of(sources, scratch, orders)
    vector_lands, vector_sems = scratch[9 * count :]
    small = vector_sum(vector, vector_out, vector_lands, vector_sems, (bits, across))
    for color in colors:
        color.begin()
    next(small)
    for stage in range(7):
        for color in colors:
            color.step(stage)
        next(small, None)
    hand_out(colors, outs)
    swap.wait()


def reduce_all(arrays, orders, vector, far, collective):
    scratch, outs = color_scratch(arrays)
    scratch.append(pltpu.VMEM((5, *vector.shape), jnp.float32))
    scratch.append(pltpu.SemaphoreType.DMA((2, 5)))
    outs.append(jax.ShapeDtypeStruct(vector.shape, jnp.float32))
    outs.append(jax.ShapeDtypeStruct(far.shape, far.dtype))
    anywhere = pl.BlockSpec(memory_space=pl.ANY)
    vmem = pl.BlockSpec(memory_space=pltpu.VMEM)
    got = pl.pallas_call(
        functools.partial(reduce_body, len(arrays), orders),
        out_shape=outs,
        in_specs=[*[anywhere] * len(arrays), vmem, anywhere],
        out_specs=[*[vmem] * (len(outs) - 1), anywhere],
        scratch_shapes=[pltpu.SemaphoreType.DMA((2,)), *scratch],
        compiler_params=pltpu.CompilerParams(
            collective_id=collective, has_side_effects=True, vmem_limit_bytes=40 << 20
        ),
        cost_estimate=pl.CostEstimate(flops=1 << 34, bytes_accessed=1 << 24, transcendentals=0),
        name="reduce_all",
    )(*arrays, vector, far)
    return assemble(arrays, got), got[-2], got[-1]


TIMES = ((3, 11, 15, 17, 20, 22, 24), (4, 12, 16, 18, 21, 22, 24), (5, 8, 10, 13, 16, 19, 21))
EARLY = (("x", "y", "zlo", "zhi"), ("zlo", "x", "y", "zhi"), ("y", "x", "zlo", "zhi"))


def attend_back_reduce_body(count, orders, *refs):
    info_ref, *blocks = refs[:7]
    swap_in, *sources = refs[7 : 8 + count]
    results = refs[8 + count : 11 + count]
    outs = refs[11 + count : 11 + 3 * count]
    far = refs[11 + 3 * count : 13 + 3 * count]
    swap_out = refs[13 + 3 * count]
    dk_acc, dv_acc, send_k, send_v, trade_sems, swap_sems, *scratch = refs[14 + 3 * count :]
    pair = pl.program_id(0)
    pairs = pl.num_programs(0)
    now = 2 * (pair * pl.num_programs(1) + pl.program_id(1))
    last = 2 * pairs * pl.num_programs(1)
    bits, across = where_am_i()
    colors = colors_of(sources, scratch, orders)

    def trade(index, which):
        return pltpu.make_async_remote_copy(
            src_ref=(send_k, send_v)[which].at[index],
            dst_ref=far[which].at[:, pl.ds(pl.multiple_of(index * PAIR, PAIR), PAIR)],
            send_sem=trade_sems.at[0, which, index],
            recv_sem=trade_sems.at[1, which, index],
            device_id=across("core"),
            device_id_type=MESH_IDS,
        )

    def before(head):
        if head == 0:

            @pl.when(now == 0)
            def _():
                greet(across)
                swap_copy(swap_in, swap_out, swap_sems, across).start()
                for color in colors:
                    color.begin()

        for when in sorted({when for times in TIMES for when in times if when % 2 == head}):

            @pl.when(now + head == when)
            def _(when=when):
                for color, times in zip(colors, TIMES):
                    for stage in range(7):
                        if times[stage] == when:
                            color.step(stage)

    def after():
        near = results[1].shape[0]
        send_k[pair] = dk_acc[near:].astype(jnp.bfloat16)
        send_v[pair] = dv_acc[near:].astype(jnp.bfloat16)
        trade(pair, 0).start()
        trade(pair, 1).start()

    attend_back_body(info_ref, *blocks, *results, dk_acc, dv_acc, before, after)

    @pl.when(now + 2 == last)
    def _():
        for color, times in zip(colors, TIMES):
            for stage in range(7):
                if times[stage] >= last:
                    color.step(stage)
        hand_out(colors, outs)
        swap_copy(swap_in, swap_out, swap_sems, across).wait()

        @pl.loop(0, pairs)
        def _(index):
            trade(index, 0).wait()
            trade(index, 1).wait()


def attend_back_reduce(
    info, queries, keys, values, grad_out, out, log_sums, block, swap, arrays, orders, collective
):
    tokens, width = queries.shape
    total = keys.shape[0]
    near = total // 2
    pairs = width // PAIR
    scratch, outs = color_scratch(arrays)
    q_spec = pl.BlockSpec((block, PAIR), lambda h, i, n: (i, h))
    k_spec = pl.BlockSpec((total, PAIR), lambda h, i, n: (0, h))
    near_spec = pl.BlockSpec((near, PAIR), lambda h, i, n: (0, h))
    whole = pl.BlockSpec(memory_space=pltpu.VMEM)
    anywhere = pl.BlockSpec(memory_space=pl.ANY)
    far = jax.ShapeDtypeStruct((near, width), jnp.bfloat16)
    got = pl.pallas_call(
        functools.partial(attend_back_reduce_body, len(arrays), orders),
        grid_spec=pltpu.PrefetchScalarGridSpec(
            num_scalar_prefetch=1,
            grid=(pairs, tokens // block),
            in_specs=[
                q_spec,
                k_spec,
                k_spec,
                q_spec,
                q_spec,
                pl.BlockSpec((1, 2, block), lambda h, i, n: (h, 0, i)),
                *[anywhere] * (1 + len(arrays)),
            ],
            out_specs=[q_spec, near_spec, near_spec, *[whole] * len(outs), *[anywhere] * 3],
            scratch_shapes=[
                pltpu.VMEM((total, PAIR), jnp.float32),
                pltpu.VMEM((total, PAIR), jnp.float32),
                pltpu.VMEM((pairs, near, PAIR), jnp.bfloat16),
                pltpu.VMEM((pairs, near, PAIR), jnp.bfloat16),
                pltpu.SemaphoreType.DMA((2, 2, pairs)),
                pltpu.SemaphoreType.DMA((2,)),
                *scratch,
            ],
        ),
        out_shape=[
            jax.ShapeDtypeStruct((tokens, width), jnp.bfloat16),
            jax.ShapeDtypeStruct((near, width), jnp.bfloat16),
            jax.ShapeDtypeStruct((near, width), jnp.bfloat16),
            *outs,
            far,
            far,
            jax.ShapeDtypeStruct(swap.shape, swap.dtype),
        ],
        compiler_params=pltpu.CompilerParams(
            collective_id=collective, has_side_effects=True, vmem_limit_bytes=62 << 20
        ),
        cost_estimate=pl.CostEstimate(
            flops=40 * tokens * total * width, bytes_accessed=1 << 25, transcendentals=0
        ),
        name="attend_back_reduce",
    )(info, queries, keys, values, grad_out, out, log_sums, swap, *arrays)

    def joined(own, other):
        return (own.astype(jnp.float32) + other.astype(jnp.float32)).astype(jnp.bfloat16)

    grads = (got[0], joined(got[1], got[-3]), joined(got[2], got[-2]))
    return grads, got[-1], assemble(arrays, got[3:-3])


def feed_body(
    lengths_ref,
    x_ref,
    att_ref,
    cot_ref,
    cot_far_ref,
    gain_ref,
    shift_ref,
    out_bias_ref,
    outer_bias_ref,
    inner_bias_ref,
    wo_ref,
    wi_ref,
    wf_ref,
    result_ref,
    normed_ref,
    act_ref,
    g_inner_ref,
    g_ffn_ref,
    g_attn_ref,
    g_att_ref,
    g_hidden_ref,
    sums_ref,
):
    low = jnp.bfloat16
    width = x_ref.shape[1]
    inner_total = inner_bias_ref.shape[1]
    gain, shift = gain_ref[...], shift_ref[...]
    out_bias, outer_bias = out_bias_ref[...], outer_bias_ref[...]
    own = pl.program_id(0) == 0
    block = x_ref.shape[0]
    seq = lax.axis_index("seq")
    start_at = jnp.where(own, seq, lax.rem(seq + 2, 4)) * block
    spots = lax.broadcasted_iota(jnp.int32, (block, 1), 0) + start_at
    keep = (spots < own_length(lengths_ref)).astype(jnp.float32)
    cot = jnp.where(own, cot_ref[...], cot_far_ref[...])
    branch_attn = dot(att_ref[...], wo_ref[...], NN) + out_bias
    hidden = x_ref[...].astype(jnp.float32) + branch_attn
    centered = hidden - jnp.mean(hidden, axis=-1, keepdims=True)
    spread = lax.rsqrt(jnp.mean(centered * centered, axis=-1, keepdims=True) + EPSILON)
    normal = centered * spread
    normed = (normal * gain + shift).astype(low)
    normed_ref[...] = normed
    g_stream = keep * cot.astype(jnp.float32)
    g_ffn = g_stream.astype(low)
    g_ffn_ref[...] = g_ffn
    branch = jnp.zeros_like(hidden) + outer_bias
    g_normed = jnp.zeros_like(hidden)
    sums = []
    for start in range(0, inner_total, width):
        span = slice(start, start + width)
        inner = dot(normed, wi_ref[:, span], NN) + inner_bias_ref[:, span]
        g_act = dot(g_ffn, wf_ref[span, :], NT)
        cdf = 0.5 + 0.5 * lax.erf(inner * (0.5**0.5))
        act = (inner * cdf).astype(low)
        slope = cdf + inner * (jnp.exp(-0.5 * inner * inner) * ((0.5 / jnp.pi) ** 0.5))
        g_inner = (g_act * slope).astype(low)
        act_ref[:, span] = act
        g_inner_ref[:, span] = g_inner
        branch = branch + dot(act, wf_ref[span, :], NN)
        g_normed = g_normed + dot(g_inner, wi_ref[:, span], NT)
        sums.append(jnp.sum(g_inner.astype(jnp.float32), axis=0, keepdims=True))
    stream = keep * (hidden + branch)
    result_ref[...] = stream.astype(low)
    e = g_normed * gain
    g_hidden = g_stream + spread * (
        e
        - jnp.mean(e, axis=-1, keepdims=True)
        - normal * jnp.mean(e * normal, axis=-1, keepdims=True)
    )
    g_hidden_ref[...] = g_hidden
    g_attn = g_hidden.astype(low)
    g_attn_ref[...] = g_attn
    g_att_ref[...] = dot(g_attn, wo_ref[...], NT).astype(low)
    for item in (
        stream * stream,
        keep * branch_attn * branch_attn,
        keep * branch * branch,
        jnp.broadcast_to(keep, hidden.shape),
        g_attn.astype(jnp.float32),
        g_normed * normal,
        g_normed,
        g_ffn.astype(jnp.float32),
    ):
        sums.append(jnp.sum(item, axis=0, keepdims=True))
    block = jnp.concatenate(sums, axis=0)

    @pl.when(pl.program_id(0) == 0)
    def _():
        sums_ref[...] = block

    @pl.when(pl.program_id(0) > 0)
    def _():
        sums_ref[...] += block


def feed(lengths, x, att, cot, cot_far, vectors, wo, wi, wf):
    tokens, width = x.shape
    inner_total = wi.shape[1]
    low = jnp.bfloat16
    block = tokens // 2
    slot = pl.BlockSpec((block, width), lambda i, n: (i, 0))
    wide = pl.BlockSpec((block, inner_total), lambda i, n: (i, 0))

    def fixed(shape):
        return pl.BlockSpec(shape, lambda i, n: (0, 0), pipeline_mode=pl.Buffered(1))

    sums_rows = inner_total // width + 8
    return pl.pallas_call(
        feed_body,
        grid_spec=pltpu.PrefetchScalarGridSpec(
            num_scalar_prefetch=1,
            grid=(2,),
            in_specs=[
                slot,
                slot,
                fixed(cot.shape),
                fixed(cot.shape),
                *[fixed((1, item.shape[0])) for item in vectors],
                fixed(wo.shape),
                fixed(wi.shape),
                fixed(wf.shape),
            ],
            out_specs=[
                slot,
                slot,
                wide,
                wide,
                slot,
                slot,
                slot,
                slot,
                pl.BlockSpec((sums_rows, width), lambda i, n: (0, 0)),
            ],
        ),
        out_shape=[
            jax.ShapeDtypeStruct((tokens, width), low),
            jax.ShapeDtypeStruct((tokens, width), low),
            jax.ShapeDtypeStruct((tokens, inner_total), low),
            jax.ShapeDtypeStruct((tokens, inner_total), low),
            jax.ShapeDtypeStruct((tokens, width), low),
            jax.ShapeDtypeStruct((tokens, width), low),
            jax.ShapeDtypeStruct((tokens, width), low),
            jax.ShapeDtypeStruct((tokens, width), jnp.float32),
            jax.ShapeDtypeStruct((sums_rows, width), jnp.float32),
        ],
        compiler_params=pltpu.CompilerParams(vmem_limit_bytes=60 << 20),
        cost_estimate=pl.CostEstimate(
            flops=4 * tokens * width * (width + 2 * inner_total),
            bytes_accessed=1 << 25,
            transcendentals=0,
        ),
        name="feed",
    )(lengths, x, att, cot, cot_far, *[item[None] for item in vectors], wo, wi, wf)


def local(
    inputs,
    lengths,
    first_gain,
    first_shift,
    query_weight,
    query_bias,
    key_weight,
    value_weight,
    value_bias,
    output_weight,
    output_bias,
    second_gain,
    second_shift,
    inner_weight,
    inner_bias,
    outer_weight,
    outer_bias,
    cotangent,
):
    groups = lax.axis_size("seq")
    seq_count, local_len, width = inputs.shape
    full_len = local_len * groups
    tokens_here = seq_count * local_len
    place = lax.axis_index("seq")
    half = groups // 2
    row = place // half
    across = [(i, (i + half) % groups) for i in range(groups)]
    beside = [(i, i ^ 1) for i in range(groups)]

    def mine_of(array):
        return lax.dynamic_index_in_dim(array, row, 0, keepdims=False)

    def in_order(own, other):
        return jnp.where(row == 0, jnp.stack([own, other]), jnp.stack([other, own]))

    def give_back(array):
        return in_order(array[:local_len], lax.ppermute(array[local_len:], "seq", across))

    both_in, normed_one_low, queries, keys, values = enter(
        inputs,
        first_gain,
        first_shift,
        query_bias,
        value_bias,
        query_weight,
        key_weight,
        value_weight,
        3,
    )
    flat_in = both_in.astype(jnp.float32)
    normed_one, norm_one_back = jax.vjp(norm_apply, flat_in, first_gain, first_shift)
    attended, log_sums, far_cot = attend(lengths, queries, keys, values, cotangent, 512, 4)
    (
        stream,
        normed_two,
        activated,
        grad_inner,
        grad_ffn,
        grad_attn,
        grad_attended,
        grad_hidden,
        sums,
    ) = feed(
        lengths,
        both_in,
        attended,
        mine_of(cotangent),
        far_cot,
        (second_gain, second_shift, output_bias, outer_bias, inner_bias),
        output_weight,
        inner_weight,
        outer_weight,
    )
    grad_outer_weight = dot(activated, grad_ffn, TN)
    grad_inner_weight = dot(normed_two, grad_inner, TN)
    grad_output_weight = dot(attended, grad_attn, TN)
    data_groups = lax.axis_size("dp")
    linked = data_groups == 8 and groups == 4
    low = jnp.bfloat16
    back_args = (lengths, queries, keys, values, grad_attended, attended, log_sums, 512)
    grads_early = (
        grad_outer_weight.astype(low),
        grad_inner_weight.astype(low),
        grad_output_weight.astype(low),
    )
    def join(partial):
        far = lax.ppermute(partial[tokens_here:], "seq", beside)
        return (partial[:tokens_here].astype(jnp.float32) + far.astype(jnp.float32)).astype(
            jnp.bfloat16
        )

    if linked:
        (grad_q_tok, grad_k_tok, grad_v_tok), other_result, sums_early = attend_back_reduce(
            *back_args, stream[local_len:], grads_early, EARLY, 2
        )
        result = in_order(stream[:local_len], other_result)
    else:
        grad_q_tok, grad_k_part, grad_v_part = attend_back(*back_args)
        grad_k_tok, grad_v_tok = join(grad_k_part), join(grad_v_part)

    grads_late = tuple(
        dot(normed_one_low, grad, TN).astype(low) for grad in (grad_q_tok, grad_k_tok, grad_v_tok)
    )
    grad_query_bias = jnp.sum(grad_q_tok, axis=0, dtype=jnp.float32)
    grad_value_bias = jnp.sum(grad_v_tok, axis=0, dtype=jnp.float32)
    grad_normed_one = (
        jnp.einsum("te,de->td", grad_q_tok, query_weight, preferred_element_type=jnp.float32)
        + jnp.einsum("te,de->td", grad_k_tok, key_weight, preferred_element_type=jnp.float32)
        + jnp.einsum("te,de->td", grad_v_tok, value_weight, preferred_element_type=jnp.float32)
    )
    grad_in_norm, grad_first_gain, grad_first_shift = norm_one_back(grad_normed_one)
    grad_in = (grad_hidden + grad_in_norm).astype(jnp.bfloat16)
    packed = jnp.concatenate(
        [
            sums,
            jnp.stack([grad_first_gain, grad_first_shift, grad_query_bias, grad_value_bias]),
        ]
    )
    if linked:
        sums_late, packed, other_in = reduce_all(grads_late, LATE, packed, grad_in[local_len:], 1)
        grad_inputs = in_order(grad_in[:local_len], other_in)
    else:

        def reduced(partial):
            piece = lax.psum_scatter(partial, ("dp", "seq"), scatter_dimension=0, tiled=True)
            return lax.all_gather(piece, "seq", axis=0, tiled=True).astype(jnp.float32)

        result = give_back(stream)
        grad_inputs = give_back(grad_in)
        sums_early = [reduced(item) for item in grads_early]
        sums_late = [reduced(item) for item in grads_late]
        packed = lax.psum(packed, ("dp", "seq"))
    summed_outer, summed_inner, summed_output = sums_early
    summed_query, summed_key, summed_value = sums_late
    inner_rows = inner_weight.shape[1] // width
    grad_inner_bias = packed[:inner_rows].reshape(-1)
    tail = packed[inner_rows:]
    denominator = tail[3, 0] * width
    stream_scale = jnp.sqrt(jnp.sum(tail[0]) / denominator)
    attention_scale = jnp.sqrt(jnp.sum(tail[1]) / denominator)
    feedforward_scale = jnp.sqrt(jnp.sum(tail[2]) / denominator)
    return (
        result,
        grad_inputs,
        tail[8],
        tail[9],
        summed_query,
        tail[10],
        summed_key,
        summed_value,
        tail[11],
        summed_output,
        tail[4],
        tail[5],
        tail[6],
        summed_inner,
        grad_inner_bias,
        summed_outer,
        tail[7],
        stream_scale,
        attention_scale,
        feedforward_scale,
    )


def solution(mesh):
    return jax.shard_map(
        local,
        mesh=mesh,
        in_specs=(
            P("dp", "seq", None),
            P("dp"),
            P(),
            P(),
            P(),
            P(),
            P(),
            P(),
            P(),
            P(),
            P(),
            P(),
            P(),
            P(),
            P(),
            P(),
            P(),
            P("dp", "seq", None),
        ),
        out_specs=(
            P("dp", "seq", None),
            P("dp", "seq", None),
            P(),
            P(),
            P("dp", None),
            P(),
            P("dp", None),
            P("dp", None),
            P(),
            P("dp", None),
            P(),
            P(),
            P(),
            P("dp", None),
            P(),
            P("dp", None),
            P(),
            P(),
            P(),
            P(),
        ),
        check_vma=False,
    )
```

```python
import functools

import jax
import jax.numpy as jnp
from jax import lax
from jax.experimental import pallas as pl
from jax.experimental.pallas import tpu as pltpu
from jax.sharding import PartitionSpec as P

HEADS = 12
HEAD_DIM = 64
EPSILON = 1e-12
NEGATIVE = -1e30
PAIR = 2 * HEAD_DIM
NT = ((1,), (1,))
NN = ((1,), (0,))
TN = ((0,), (0,))


def norm_apply(values, gain_vec, shift_vec):
    average = jnp.mean(values, axis=-1, keepdims=True)
    centered = values - average
    spread = jnp.mean(centered * centered, axis=-1, keepdims=True)
    return centered * lax.rsqrt(spread + EPSILON) * gain_vec + shift_vec


def dot(left, right, dims):
    return lax.dot_general(left, right, (dims, ((), ())), preferred_element_type=jnp.float32)


def block_places():
    seq = lax.axis_index("seq")
    beside = seq + 1 - 2 * lax.rem(seq, 2)
    return seq, lax.rem(seq + 2, 4), beside, lax.rem(beside + 2, 4)


def own_length(lengths_ref):
    return lengths_ref[lax.axis_index("seq") // 2]


def fill_bias(lengths_ref, bias_ref):
    total = bias_ref.shape[0]
    block = total // 4
    spots = lax.broadcasted_iota(jnp.int32, (total, 1), 0)
    shift = 0
    for index, place in enumerate(block_places()):
        shift = jnp.where(spots >= index * block, (place - index) * block, shift)
    bias = jnp.where(spots + shift < own_length(lengths_ref), 0.0, NEGATIVE)
    bias_ref[...] = jnp.broadcast_to(bias, bias_ref.shape).astype(jnp.bfloat16)


def masked_scores(keys, bias, queries, head):
    lane = lax.broadcasted_iota(jnp.int32, (1, PAIR), 1)
    spare = HEAD_DIM * (1 - head)
    mine = (lane < HEAD_DIM) if head == 0 else (lane >= HEAD_DIM)
    ones = jnp.where(lane == spare, 1.0, 0.0).astype(jnp.bfloat16)
    left = jnp.where(lane == spare, bias, keys)
    right = jnp.where(mine, queries, jnp.broadcast_to(ones, queries.shape))
    return dot(left, right, NT)


def attend_body(
    lengths_ref, q_ref, k_ref, v_ref, cot_ref, out_ref, lse_ref, far_ref, bias_ref, swap_sems
):
    bits, across = where_am_i()
    swap = swap_copy(cot_ref.at[1 - bits["y"]], far_ref, swap_sems, across)
    now = pl.program_id(0) * pl.num_programs(1) + pl.program_id(1)

    @pl.when(now == 0)
    def _():
        greet(across, ("y",))
        swap.start()
        fill_bias(lengths_ref, bias_ref)

    scale = jnp.bfloat16(HEAD_DIM ** (-0.5))
    queries = q_ref[...] * scale
    keys = k_ref[...]
    values_t = v_ref[...].T
    bias = bias_ref[...]
    outs = []
    for head in range(2):
        scores = masked_scores(keys, bias, queries, head)
        top = jnp.max(scores, axis=0, keepdims=True)
        weights = jnp.exp(scores - top)
        total = jnp.sum(weights, axis=0, keepdims=True)
        mixed = dot(
            values_t[HEAD_DIM * head : HEAD_DIM * (head + 1)], weights.astype(jnp.bfloat16), NN
        )
        outs.append(mixed * (1.0 / total))
        lse_ref[0, head : head + 1, :] = top + jnp.log(total)
    out_ref[...] = jnp.concatenate(outs, axis=0).T.astype(jnp.bfloat16)

    @pl.when(now == pl.num_programs(0) * pl.num_programs(1) - 1)
    def _():
        swap.wait()


def attend(info, queries, keys, values, cotangent, block, collective):
    tokens, width = queries.shape
    total = keys.shape[0]
    pairs = width // PAIR
    q_spec = pl.BlockSpec((block, PAIR), lambda h, i, n: (i, h))
    k_spec = pl.BlockSpec((total, PAIR), lambda h, i, n: (0, h))
    return pl.pallas_call(
        attend_body,
        grid_spec=pltpu.PrefetchScalarGridSpec(
            num_scalar_prefetch=1,
            grid=(pairs, tokens // block),
            in_specs=[q_spec, k_spec, k_spec, pl.BlockSpec(memory_space=pl.ANY)],
            out_specs=[
                q_spec,
                pl.BlockSpec((1, 2, block), lambda h, i, n: (h, 0, i)),
                pl.BlockSpec(memory_space=pl.ANY),
            ],
            scratch_shapes=[
                pltpu.VMEM((total, PAIR), jnp.bfloat16),
                pltpu.SemaphoreType.DMA((2,)),
            ],
        ),
        out_shape=[
            jax.ShapeDtypeStruct((tokens, width), jnp.bfloat16),
            jax.ShapeDtypeStruct((pairs, 2, tokens), jnp.float32),
            jax.ShapeDtypeStruct(cotangent.shape[1:], cotangent.dtype),
        ],
        compiler_params=pltpu.CompilerParams(
            collective_id=collective, has_side_effects=True, vmem_limit_bytes=48 << 20
        ),
        cost_estimate=pl.CostEstimate(
            flops=16 * tokens * total * width, bytes_accessed=1 << 23, transcendentals=0
        ),
        name="attend",
    )(info, queries, keys, values, cotangent)


def attend_back_body(
    lengths_ref,
    q_ref,
    k_ref,
    v_ref,
    do_ref,
    o_ref,
    lse_ref,
    dq_ref,
    dk_ref,
    dv_ref,
    bias_ref,
    dk_acc,
    dv_acc,
    before=None,
    after=None,
):
    step = pl.program_id(1)

    @pl.when((step == 0) & (pl.program_id(0) == 0))
    def _():
        fill_bias(lengths_ref, bias_ref)

    lane = lax.broadcasted_iota(jnp.int32, (1, PAIR), 1)
    scale = jnp.bfloat16(HEAD_DIM ** (-0.5))
    grad_out = do_ref[...]
    queries = q_ref[...] * scale
    keys = k_ref[...]
    keys_t = keys.T
    values = v_ref[...]
    product = grad_out.astype(jnp.float32) * o_ref[...].astype(jnp.float32)
    pick = (
        lax.broadcasted_iota(jnp.int32, (8, PAIR), 1) // HEAD_DIM
        == lax.broadcasted_iota(jnp.int32, (8, PAIR), 0)
    ).astype(jnp.float32)
    row_sums = lax.dot_general(
        pick,
        product,
        (NT, ((), ())),
        precision=lax.Precision.HIGHEST,
        preferred_element_type=jnp.float32,
    )
    bias = bias_ref[...]
    zero = jnp.zeros_like(queries)
    grad_k = 0
    grad_v = 0
    grad_q = []
    for head in range(2):
        if before is not None:
            before(head)
        mine = (lane < HEAD_DIM) if head == 0 else (lane >= HEAD_DIM)
        query_h = jnp.where(mine, queries, zero)
        out_h = jnp.where(mine, grad_out, zero)
        scores = masked_scores(keys, bias, queries, head)
        weights = jnp.exp(scores - lse_ref[0, head : head + 1, :])
        grad_w = dot(values, out_h, NT)
        grad_s = (weights * (grad_w - row_sums[head : head + 1])).astype(jnp.bfloat16)
        grad_v = grad_v + dot(weights.astype(jnp.bfloat16), out_h, NN)
        grad_k = grad_k + dot(grad_s, query_h, NN)
        grad_q.append(dot(keys_t[HEAD_DIM * head : HEAD_DIM * (head + 1)], grad_s, NN))
    grad_q = jnp.concatenate(grad_q, axis=0) * (HEAD_DIM ** (-0.5))
    dq_ref[...] = grad_q.T.astype(jnp.bfloat16)

    @pl.when(step == 0)
    def _():
        dk_acc[...] = grad_k
        dv_acc[...] = grad_v

    @pl.when(step > 0)
    def _():
        dk_acc[...] += grad_k
        dv_acc[...] += grad_v

    @pl.when(step == pl.num_programs(1) - 1)
    def _():
        near = dk_ref.shape[0]
        dk_ref[...] = dk_acc[:near].astype(jnp.bfloat16)
        dv_ref[...] = dv_acc[:near].astype(jnp.bfloat16)
        if after is not None:
            after()


def attend_back(info, queries, keys, values, grad_out, out, log_sums, block):
    tokens, width = queries.shape
    total = keys.shape[0]
    pairs = width // PAIR
    q_spec = pl.BlockSpec((block, PAIR), lambda h, i, n: (i, h))
    k_spec = pl.BlockSpec((total, PAIR), lambda h, i, n: (0, h))
    return pl.pallas_call(
        attend_back_body,
        grid_spec=pltpu.PrefetchScalarGridSpec(
            num_scalar_prefetch=1,
            grid=(pairs, tokens // block),
            in_specs=[
                q_spec,
                k_spec,
                k_spec,
                q_spec,
                q_spec,
                pl.BlockSpec((1, 2, block), lambda h, i, n: (h, 0, i)),
            ],
            out_specs=[q_spec, k_spec, k_spec],
            scratch_shapes=[
                pltpu.VMEM((total, PAIR), jnp.bfloat16),
                pltpu.VMEM((total, PAIR), jnp.float32),
                pltpu.VMEM((total, PAIR), jnp.float32),
            ],
        ),
        out_shape=[
            jax.ShapeDtypeStruct((tokens, width), jnp.bfloat16),
            jax.ShapeDtypeStruct((total, width), jnp.bfloat16),
            jax.ShapeDtypeStruct((total, width), jnp.bfloat16),
        ],
        compiler_params=pltpu.CompilerParams(vmem_limit_bytes=48 << 20),
        cost_estimate=pl.CostEstimate(
            flops=40 * tokens * total * width, bytes_accessed=1 << 24, transcendentals=0
        ),
        name="attend_back",
    )(info, queries, keys, values, grad_out, out, log_sums)


MESH_IDS = pl.DeviceIdType.MESH
AXES = ("zhi", "zlo", "x", "y")
LATE = (("x", "zlo", "y", "zhi"), ("zlo", "x", "y", "zhi"), ("x", "zlo", "zhi", "y"))


def where_am_i():
    data = lax.axis_index("dp")
    seq = lax.axis_index("seq")
    bits = {
        "zhi": data // 4,
        "zlo": (data // 2) % 2,
        "x": data % 2,
        "y": seq // 2,
        "core": seq % 2,
    }

    def across(axis):
        if axis == "core":
            return (data, seq + 1 - 2 * bits["core"])
        if axis == "y":
            return (data, seq + 2 - 4 * bits["y"])
        step = {"zhi": 4, "zlo": 2, "x": 1}[axis]
        return (data + step - 2 * step * bits[axis], seq)

    return bits, across


def spot_of(piece, order):
    bits = {axis: (piece >> (3 - k)) & 1 for k, axis in enumerate(AXES)}
    return sum(bits[axis] << (3 - k) for k, axis in enumerate(order))


class Color:
    def __init__(self, source, acc, lands, gathers, sems, order):
        self.source, self.acc, self.lands, self.gathers = source, acc, lands, gathers
        self.sems, self.order = sems, order
        self.pieces, self.rows, self.cols = acc.shape
        self.bits, self.across = where_am_i()

    def base(self, stage):
        return sum(self.bits[self.order[k]] * (self.pieces >> (k + 1)) for k in range(stage))

    def remote(self, src, dst, slot, axis):
        return pltpu.make_async_remote_copy(
            src_ref=src,
            dst_ref=dst,
            send_sem=self.sems.at[0, slot],
            recv_sem=self.sems.at[1, slot],
            device_id=self.across(axis),
            device_id_type=MESH_IDS,
        )

    def begin(self):
        core = self.bits["core"]
        mine = pl.ds(pl.multiple_of(core * self.cols, 128), self.cols)
        theirs = pl.ds(pl.multiple_of((1 - core) * self.cols, 128), self.cols)
        for piece in range(self.pieces):
            spot = spot_of(piece, self.order)
            span = pl.ds(piece * self.rows, self.rows)
            self.remote(
                self.source.at[span, theirs], self.lands[0].at[spot], 0, "core"
            ).start()
            pltpu.make_async_copy(
                self.source.at[span, mine], self.acc.at[spot], self.sems.at[0, 7]
            ).start()

    def add(self, base, count, land):
        @pl.loop(0, count)
        def _(index):
            total = self.acc[base + index].astype(jnp.float32) + land[index].astype(jnp.float32)
            self.acc[base + index] = total.astype(jnp.bfloat16)

    def transfer(self, stage):
        if stage < 4:
            axis = self.order[stage]
            half = self.pieces >> (stage + 1)
            start = self.base(stage) + (1 - self.bits[axis]) * half
            return self.remote(
                self.acc.at[pl.ds(start, half)], self.lands[stage + 1], stage + 1, axis
            )
        if stage == 4:
            there = self.gathers[0].at[self.bits["y"]]
            return self.remote(self.acc.at[self.base(4)], there, 5, "y")
        return self.remote(self.gathers[0], self.gathers[1], 6, "core")

    def step(self, stage):
        if stage == 0:
            whole = self.remote(self.lands[0], self.lands[0], 0, "core")
            pltpu.make_async_copy(self.acc, self.acc, self.sems.at[0, 7]).wait()
            whole.wait_send()
            whole.wait_recv()
        else:
            self.transfer(stage - 1).wait()
        if stage <= 4:
            self.add(self.base(stage), self.pieces >> stage, self.lands[stage])
        if stage == 4:
            self.gathers[0][self.bits["y"]] = self.acc[self.base(4)]
        if stage < 6:
            self.transfer(stage).start()


def swap_copy(source, landing, sems, across):
    return pltpu.make_async_remote_copy(
        src_ref=source,
        dst_ref=landing,
        send_sem=sems.at[0],
        recv_sem=sems.at[1],
        device_id=across("y"),
        device_id_type=MESH_IDS,
    )


def greet(across, axes=("core", *AXES)):
    barrier = pltpu.get_barrier_semaphore()
    for axis in axes:
        pl.semaphore_signal(barrier, inc=1, device_id=across(axis), device_id_type=MESH_IDS)
    pl.semaphore_wait(barrier, len(axes))


CHUNKS = 4


def enter_body(
    in_ref,
    gain_ref,
    shift_ref,
    q_bias_ref,
    v_bias_ref,
    wq_ref,
    wk_ref,
    wv_ref,
    x_ref,
    normed_ref,
    q_ref,
    k_ref,
    v_ref,
    swap_sems,
    own_sem,
    trade_sems,
):
    low = jnp.bfloat16
    bits, across = where_am_i()
    row = bits["y"]
    size = x_ref.shape[0] // CHUNKS
    tokens = x_ref.shape[0]
    half = CHUNKS // 2
    own = pltpu.make_async_copy(in_ref.at[row], x_ref.at[pl.ds(0, tokens // 2)], own_sem)
    own.start()
    greet(across, ("core", "y"))

    def arrival(chunk):
        return pltpu.make_async_remote_copy(
            src_ref=in_ref.at[1 - row, pl.ds(pl.multiple_of(chunk * size, size), size)],
            dst_ref=x_ref.at[pl.ds(pl.multiple_of((half + chunk) * size, size), size)],
            send_sem=swap_sems.at[0, chunk],
            recv_sem=swap_sems.at[1, chunk],
            device_id=across("y"),
            device_id_type=MESH_IDS,
        )

    def trade(chunk, which):
        ref = (k_ref, v_ref)[which]
        return pltpu.make_async_remote_copy(
            src_ref=ref.at[pl.ds(pl.multiple_of(chunk * size, size), size)],
            dst_ref=ref.at[pl.ds(pl.multiple_of(tokens + chunk * size, size), size)],
            send_sem=trade_sems.at[0, which, chunk],
            recv_sem=trade_sems.at[1, which, chunk],
            device_id=across("core"),
            device_id_type=MESH_IDS,
        )

    for chunk in range(half):
        arrival(chunk).start()
    own.wait()

    @pl.loop(0, CHUNKS)
    def _(chunk):
        @pl.when(chunk >= half)
        def _():
            arrival(chunk - half).wait()

        span = pl.ds(pl.multiple_of(chunk * size, size), size)
        rows = x_ref[span, :].astype(jnp.float32)
        normed = norm_apply(rows, gain_ref[...], shift_ref[...]).astype(low)
        normed_ref[span, :] = normed
        k_ref[span, :] = dot(normed, wk_ref[...], NN).astype(low)
        trade(chunk, 0).start()
        v_ref[span, :] = (dot(normed, wv_ref[...], NN) + v_bias_ref[...]).astype(low)
        trade(chunk, 1).start()
        q_ref[span, :] = (dot(normed, wq_ref[...], NN) + q_bias_ref[...]).astype(low)

    @pl.loop(0, CHUNKS)
    def _(chunk):
        trade(chunk, 0).wait()
        trade(chunk, 1).wait()


def enter(inputs, gain, shift, q_bias, v_bias, wq, wk, wv, collective):
    _, local_len, width = inputs.shape
    vmem = pl.BlockSpec(memory_space=pltpu.VMEM)

    def made(blocks):
        return jax.ShapeDtypeStruct((blocks * local_len, width), jnp.bfloat16)

    return pl.pallas_call(
        enter_body,
        out_shape=[made(2), made(2), made(2), made(4), made(4)],
        in_specs=[pl.BlockSpec(memory_space=pl.ANY)] + [vmem] * 7,
        out_specs=[vmem] * 5,
        scratch_shapes=[
            pltpu.SemaphoreType.DMA((2, CHUNKS // 2)),
            pltpu.SemaphoreType.DMA,
            pltpu.SemaphoreType.DMA((2, 2, CHUNKS)),
        ],
        compiler_params=pltpu.CompilerParams(
            collective_id=collective, has_side_effects=True, vmem_limit_bytes=48 << 20
        ),
        name="enter",
    )(inputs, gain[None], shift[None], q_bias[None], v_bias[None], wq, wk, wv)


def color_scratch(arrays):
    scratch = []
    outs = []
    for array in arrays:
        rows, cols = array.shape[0] // 16, array.shape[1] // 2
        scratch.append(pltpu.VMEM((16, rows, cols), jnp.bfloat16))
        for size in (16, 8, 4, 2, 1):
            scratch.append(pltpu.VMEM((size, rows, cols), jnp.bfloat16))
        scratch += [pltpu.VMEM((2, rows, cols), jnp.bfloat16)] * 2
        scratch.append(pltpu.SemaphoreType.DMA((2, 8)))
        outs += [jax.ShapeDtypeStruct((2, rows, cols), jnp.bfloat16)] * 2
    return scratch, outs


def colors_of(sources, scratch, orders):
    colors = []
    for index, source in enumerate(sources):
        acc, *lands = scratch[9 * index : 9 * index + 6]
        gathers = scratch[9 * index + 6 : 9 * index + 8]
        sems = scratch[9 * index + 8]
        colors.append(Color(source, acc, lands, gathers, sems, orders[index]))
    return colors


def hand_out(colors, outs):
    for index, color in enumerate(colors):
        outs[2 * index][...] = color.gathers[0][...]
        outs[2 * index + 1][...] = color.gathers[1][...]


def assemble(arrays, got):
    core = lax.axis_index("seq") % 2
    sums = []
    for index, array in enumerate(arrays):
        mine, other = got[2 * index], got[2 * index + 1]
        rows = array.shape[0] // 8
        left = jnp.where(core == 0, mine, other).reshape(rows, -1)
        right = jnp.where(core == 0, other, mine).reshape(rows, -1)
        sums.append(jnp.concatenate([left, right], axis=1).astype(jnp.float32))
    return sums


def vector_sum(source, held, lands, sems, bits_across):
    bits, across = bits_across
    held[...] = source[...]
    for slot, axis in enumerate(("core", "y", "x", "zlo", "zhi")):
        copy = pltpu.make_async_remote_copy(
            src_ref=held,
            dst_ref=lands.at[slot],
            send_sem=sems.at[0, slot],
            recv_sem=sems.at[1, slot],
            device_id=across(axis),
            device_id_type=MESH_IDS,
        )
        copy.start()
        yield
        copy.wait()
        held[...] = held[...] + lands[slot]


def reduce_body(count, orders, *refs):
    sources, vector, far = refs[:count], refs[count], refs[count + 1]
    outs = refs[count + 2 : count + 2 + 2 * count]
    vector_out, far_out = refs[3 * count + 2 : 3 * count + 4]
    swap_sems, *scratch = refs[3 * count + 4 :]
    bits, across = where_am_i()
    greet(across)
    swap = swap_copy(far, far_out, swap_sems, across)
    swap.start()
    colors = colors_of(sources, scratch, orders)
    vector_lands, vector_sems = scratch[9 * count :]
    small = vector_sum(vector, vector_out, vector_lands, vector_sems, (bits, across))
    for color in colors:
        color.begin()
    next(small)
    for stage in range(7):
        for color in colors:
            color.step(stage)
        next(small, None)
    hand_out(colors, outs)
    swap.wait()


def reduce_all(arrays, orders, vector, far, collective):
    scratch, outs = color_scratch(arrays)
    scratch.append(pltpu.VMEM((5, *vector.shape), jnp.float32))
    scratch.append(pltpu.SemaphoreType.DMA((2, 5)))
    outs.append(jax.ShapeDtypeStruct(vector.shape, jnp.float32))
    outs.append(jax.ShapeDtypeStruct(far.shape, far.dtype))
    anywhere = pl.BlockSpec(memory_space=pl.ANY)
    vmem = pl.BlockSpec(memory_space=pltpu.VMEM)
    got = pl.pallas_call(
        functools.partial(reduce_body, len(arrays), orders),
        out_shape=outs,
        in_specs=[*[anywhere] * len(arrays), vmem, anywhere],
        out_specs=[*[vmem] * (len(outs) - 1), anywhere],
        scratch_shapes=[pltpu.SemaphoreType.DMA((2,)), *scratch],
        compiler_params=pltpu.CompilerParams(
            collective_id=collective, has_side_effects=True, vmem_limit_bytes=40 << 20
        ),
        cost_estimate=pl.CostEstimate(flops=1 << 34, bytes_accessed=1 << 24, transcendentals=0),
        name="reduce_all",
    )(*arrays, vector, far)
    return assemble(arrays, got), got[-2], got[-1]


TIMES = ((3, 11, 15, 17, 20, 22, 24), (4, 12, 16, 18, 21, 22, 24), (5, 8, 10, 13, 16, 19, 21))
EARLY = (("x", "y", "zlo", "zhi"), ("zlo", "x", "y", "zhi"), ("y", "x", "zlo", "zhi"))


def attend_back_reduce_body(count, orders, *refs):
    info_ref, *blocks = refs[:7]
    swap_in, *sources = refs[7 : 8 + count]
    results = refs[8 + count : 11 + count]
    outs = refs[11 + count : 11 + 3 * count]
    far = refs[11 + 3 * count : 13 + 3 * count]
    swap_out = refs[13 + 3 * count]
    bias_ref, dk_acc, dv_acc, *scratch = refs[14 + 3 * count :]
    send_k, send_v, trade_sems, swap_sems, *scratch = scratch
    pair = pl.program_id(0)
    pairs = pl.num_programs(0)
    now = 2 * (pair * pl.num_programs(1) + pl.program_id(1))
    last = 2 * pairs * pl.num_programs(1)
    bits, across = where_am_i()
    colors = colors_of(sources, scratch, orders)

    def trade(index, which):
        return pltpu.make_async_remote_copy(
            src_ref=(send_k, send_v)[which].at[index],
            dst_ref=far[which].at[:, pl.ds(pl.multiple_of(index * PAIR, PAIR), PAIR)],
            send_sem=trade_sems.at[0, which, index],
            recv_sem=trade_sems.at[1, which, index],
            device_id=across("core"),
            device_id_type=MESH_IDS,
        )

    def before(head):
        if head == 0:

            @pl.when(now == 0)
            def _():
                greet(across)
                swap_copy(swap_in, swap_out, swap_sems, across).start()
                for color in colors:
                    color.begin()

        for when in sorted({when for times in TIMES for when in times if when % 2 == head}):

            @pl.when(now + head == when)
            def _(when=when):
                for color, times in zip(colors, TIMES):
                    for stage in range(7):
                        if times[stage] == when:
                            color.step(stage)

    def after():
        near = results[1].shape[0]
        send_k[pair] = dk_acc[near:].astype(jnp.bfloat16)
        send_v[pair] = dv_acc[near:].astype(jnp.bfloat16)
        trade(pair, 0).start()
        trade(pair, 1).start()

    attend_back_body(info_ref, *blocks, *results, bias_ref, dk_acc, dv_acc, before, after)

    @pl.when(now + 2 == last)
    def _():
        for color, times in zip(colors, TIMES):
            for stage in range(7):
                if times[stage] >= last:
                    color.step(stage)
        hand_out(colors, outs)
        swap_copy(swap_in, swap_out, swap_sems, across).wait()

        @pl.loop(0, pairs)
        def _(index):
            trade(index, 0).wait()
            trade(index, 1).wait()


def attend_back_reduce(
    info, queries, keys, values, grad_out, out, log_sums, block, swap, arrays, orders, collective
):
    tokens, width = queries.shape
    total = keys.shape[0]
    near = total // 2
    pairs = width // PAIR
    scratch, outs = color_scratch(arrays)
    q_spec = pl.BlockSpec((block, PAIR), lambda h, i, n: (i, h))
    k_spec = pl.BlockSpec((total, PAIR), lambda h, i, n: (0, h))
    near_spec = pl.BlockSpec((near, PAIR), lambda h, i, n: (0, h))
    whole = pl.BlockSpec(memory_space=pltpu.VMEM)
    anywhere = pl.BlockSpec(memory_space=pl.ANY)
    far = jax.ShapeDtypeStruct((near, width), jnp.bfloat16)
    got = pl.pallas_call(
        functools.partial(attend_back_reduce_body, len(arrays), orders),
        grid_spec=pltpu.PrefetchScalarGridSpec(
            num_scalar_prefetch=1,
            grid=(pairs, tokens // block),
            in_specs=[
                q_spec,
                k_spec,
                k_spec,
                q_spec,
                q_spec,
                pl.BlockSpec((1, 2, block), lambda h, i, n: (h, 0, i)),
                *[anywhere] * (1 + len(arrays)),
            ],
            out_specs=[q_spec, near_spec, near_spec, *[whole] * len(outs), *[anywhere] * 3],
            scratch_shapes=[
                pltpu.VMEM((total, PAIR), jnp.bfloat16),
                pltpu.VMEM((total, PAIR), jnp.float32),
                pltpu.VMEM((total, PAIR), jnp.float32),
                pltpu.VMEM((pairs, near, PAIR), jnp.bfloat16),
                pltpu.VMEM((pairs, near, PAIR), jnp.bfloat16),
                pltpu.SemaphoreType.DMA((2, 2, pairs)),
                pltpu.SemaphoreType.DMA((2,)),
                *scratch,
            ],
        ),
        out_shape=[
            jax.ShapeDtypeStruct((tokens, width), jnp.bfloat16),
            jax.ShapeDtypeStruct((near, width), jnp.bfloat16),
            jax.ShapeDtypeStruct((near, width), jnp.bfloat16),
            *outs,
            far,
            far,
            jax.ShapeDtypeStruct(swap.shape, swap.dtype),
        ],
        compiler_params=pltpu.CompilerParams(
            collective_id=collective, has_side_effects=True, vmem_limit_bytes=62 << 20
        ),
        cost_estimate=pl.CostEstimate(
            flops=40 * tokens * total * width, bytes_accessed=1 << 25, transcendentals=0
        ),
        name="attend_back_reduce",
    )(info, queries, keys, values, grad_out, out, log_sums, swap, *arrays)

    def joined(own, other):
        return (own.astype(jnp.float32) + other.astype(jnp.float32)).astype(jnp.bfloat16)

    grads = (got[0], joined(got[1], got[-3]), joined(got[2], got[-2]))
    return grads, got[-1], assemble(arrays, got[3:-3])


def feed_body(
    lengths_ref,
    x_ref,
    att_ref,
    cot_ref,
    cot_far_ref,
    gain_ref,
    shift_ref,
    out_bias_ref,
    outer_bias_ref,
    inner_bias_ref,
    wo_ref,
    wi_ref,
    wf_ref,
    result_ref,
    g_att_ref,
    g_hidden_ref,
    sums_ref,
    g_wf_ref,
    g_wi_ref,
    g_wo_ref,
    act_all,
    g_inner_all,
    normed_all,
    g_ffn_all,
    att_all,
    g_attn_all,
):
    step = pl.program_id(0)
    block, width = x_ref.shape
    chunks = wi_ref.shape[1] // width

    @pl.when(step < 2)
    def _():
        span = pl.ds(pl.multiple_of(step * block, block), block)
        att_all[span, :] = att_ref[...]
        feed_block(
            lengths_ref,
            x_ref,
            att_ref,
            cot_ref,
            cot_far_ref,
            gain_ref,
            shift_ref,
            out_bias_ref,
            outer_bias_ref,
            inner_bias_ref,
            wo_ref,
            wi_ref,
            wf_ref,
            result_ref,
            normed_all.at[span],
            act_all.at[span],
            g_inner_all.at[span],
            g_ffn_all.at[span],
            g_attn_all.at[span],
            g_att_ref,
            g_hidden_ref,
            sums_ref,
        )

    @pl.when((step >= 2) & (step < 2 + chunks))
    def _():
        span = pl.ds(pl.multiple_of((step - 2) * width, width), width)
        g_wf_ref[...] = dot(act_all[:, span], g_ffn_all[...], TN).astype(jnp.bfloat16)

    @pl.when((step >= 2 + chunks) & (step < 2 + 2 * chunks))
    def _():
        span = pl.ds(pl.multiple_of((step - 2 - chunks) * width, width), width)
        g_wi_ref[...] = dot(normed_all[...], g_inner_all[:, span], TN).astype(jnp.bfloat16)

    @pl.when(step == 2 + 2 * chunks)
    def _():
        g_wo_ref[...] = dot(att_all[...], g_attn_all[...], TN).astype(jnp.bfloat16)


def feed_block(
    lengths_ref,
    x_ref,
    att_ref,
    cot_ref,
    cot_far_ref,
    gain_ref,
    shift_ref,
    out_bias_ref,
    outer_bias_ref,
    inner_bias_ref,
    wo_ref,
    wi_ref,
    wf_ref,
    result_ref,
    normed_ref,
    act_ref,
    g_inner_ref,
    g_ffn_ref,
    g_attn_ref,
    g_att_ref,
    g_hidden_ref,
    sums_ref,
):
    low = jnp.bfloat16
    width = x_ref.shape[1]
    inner_total = inner_bias_ref.shape[1]
    gain, shift = gain_ref[...], shift_ref[...]
    out_bias, outer_bias = out_bias_ref[...], outer_bias_ref[...]
    own = pl.program_id(0) == 0
    block = x_ref.shape[0]
    seq = lax.axis_index("seq")
    start_at = jnp.where(own, seq, lax.rem(seq + 2, 4)) * block
    spots = lax.broadcasted_iota(jnp.int32, (block, 1), 0) + start_at
    keep = (spots < own_length(lengths_ref)).astype(jnp.float32)
    cot = jnp.where(own, cot_ref[...], cot_far_ref[...])
    branch_attn = dot(att_ref[...], wo_ref[...], NN) + out_bias
    hidden = x_ref[...].astype(jnp.float32) + branch_attn
    centered = hidden - jnp.mean(hidden, axis=-1, keepdims=True)
    spread = lax.rsqrt(jnp.mean(centered * centered, axis=-1, keepdims=True) + EPSILON)
    normal = centered * spread
    normed = (normal * gain + shift).astype(low)
    normed_ref[...] = normed
    g_stream = keep * cot.astype(jnp.float32)
    g_ffn = g_stream.astype(low)
    g_ffn_ref[...] = g_ffn
    branch = jnp.zeros_like(hidden) + outer_bias
    g_normed = jnp.zeros_like(hidden)
    sums = []
    for start in range(0, inner_total, width):
        span = slice(start, start + width)
        inner = dot(normed, wi_ref[:, span], NN) + inner_bias_ref[:, span]
        g_act = dot(g_ffn, wf_ref[span, :], NT)
        cdf = 0.5 + 0.5 * lax.erf(inner * (0.5**0.5))
        act = (inner * cdf).astype(low)
        slope = cdf + inner * (jnp.exp(-0.5 * inner * inner) * ((0.5 / jnp.pi) ** 0.5))
        g_inner = (g_act * slope).astype(low)
        act_ref[:, span] = act
        g_inner_ref[:, span] = g_inner
        branch = branch + dot(act, wf_ref[span, :], NN)
        g_normed = g_normed + dot(g_inner, wi_ref[:, span], NT)
        sums.append(jnp.sum(g_inner.astype(jnp.float32), axis=0, keepdims=True))
    stream = keep * (hidden + branch)
    result_ref[...] = stream.astype(low)
    e = g_normed * gain
    g_hidden = g_stream + spread * (
        e
        - jnp.mean(e, axis=-1, keepdims=True)
        - normal * jnp.mean(e * normal, axis=-1, keepdims=True)
    )
    g_hidden_ref[...] = g_hidden
    g_attn = g_hidden.astype(low)
    g_attn_ref[...] = g_attn
    g_att_ref[...] = dot(g_attn, wo_ref[...], NT).astype(low)
    for item in (
        stream * stream,
        keep * branch_attn * branch_attn,
        keep * branch * branch,
        jnp.broadcast_to(keep, hidden.shape),
        g_attn.astype(jnp.float32),
        g_normed * normal,
        g_normed,
        g_ffn.astype(jnp.float32),
    ):
        sums.append(jnp.sum(item, axis=0, keepdims=True))
    block = jnp.concatenate(sums, axis=0)

    @pl.when(pl.program_id(0) == 0)
    def _():
        sums_ref[...] = block

    @pl.when(pl.program_id(0) > 0)
    def _():
        sums_ref[...] += block


def feed(lengths, x, att, cot, cot_far, vectors, wo, wi, wf):
    tokens, width = x.shape
    inner_total = wi.shape[1]
    low = jnp.bfloat16
    block = tokens // 2
    chunks = inner_total // width
    slot = pl.BlockSpec((block, width), lambda i, n: (jnp.minimum(i, 1), 0))

    def fixed(shape):
        return pl.BlockSpec(shape, lambda i, n: (0, 0), pipeline_mode=pl.Buffered(1))

    sums_rows = chunks + 8
    return pl.pallas_call(
        feed_body,
        grid_spec=pltpu.PrefetchScalarGridSpec(
            num_scalar_prefetch=1,
            grid=(3 + 2 * chunks,),
            in_specs=[
                slot,
                slot,
                fixed(cot.shape),
                fixed(cot.shape),
                *[fixed((1, item.shape[0])) for item in vectors],
                fixed(wo.shape),
                fixed(wi.shape),
                fixed(wf.shape),
            ],
            out_specs=[
                slot,
                slot,
                slot,
                pl.BlockSpec((sums_rows, width), lambda i, n: (0, 0)),
                pl.BlockSpec((width, width), lambda i, n: (jnp.clip(i - 2, 0, chunks - 1), 0)),
                pl.BlockSpec(
                    (width, width), lambda i, n: (0, jnp.clip(i - 2 - chunks, 0, chunks - 1))
                ),
                pl.BlockSpec((width, width), lambda i, n: (0, 0)),
            ],
            scratch_shapes=[
                pltpu.VMEM((tokens, inner_total), low),
                pltpu.VMEM((tokens, inner_total), low),
                *[pltpu.VMEM((tokens, width), low)] * 4,
            ],
        ),
        out_shape=[
            jax.ShapeDtypeStruct((tokens, width), low),
            jax.ShapeDtypeStruct((tokens, width), low),
            jax.ShapeDtypeStruct((tokens, width), jnp.float32),
            jax.ShapeDtypeStruct((sums_rows, width), jnp.float32),
            jax.ShapeDtypeStruct((inner_total, width), low),
            jax.ShapeDtypeStruct((width, inner_total), low),
            jax.ShapeDtypeStruct((width, width), low),
        ],
        compiler_params=pltpu.CompilerParams(vmem_limit_bytes=62 << 20),
        cost_estimate=pl.CostEstimate(
            flops=6 * tokens * width * (width + 2 * inner_total),
            bytes_accessed=1 << 25,
            transcendentals=0,
        ),
        name="feed",
    )(lengths, x, att, cot, cot_far, *[item[None] for item in vectors], wo, wi, wf)


def local(
    inputs,
    lengths,
    first_gain,
    first_shift,
    query_weight,
    query_bias,
    key_weight,
    value_weight,
    value_bias,
    output_weight,
    output_bias,
    second_gain,
    second_shift,
    inner_weight,
    inner_bias,
    outer_weight,
    outer_bias,
    cotangent,
):
    groups = lax.axis_size("seq")
    seq_count, local_len, width = inputs.shape
    full_len = local_len * groups
    tokens_here = seq_count * local_len
    place = lax.axis_index("seq")
    half = groups // 2
    row = place // half
    across = [(i, (i + half) % groups) for i in range(groups)]
    beside = [(i, i ^ 1) for i in range(groups)]

    def mine_of(array):
        return lax.dynamic_index_in_dim(array, row, 0, keepdims=False)

    def in_order(own, other):
        return jnp.where(row == 0, jnp.stack([own, other]), jnp.stack([other, own]))

    def give_back(array):
        return in_order(array[:local_len], lax.ppermute(array[local_len:], "seq", across))

    both_in, normed_one_low, queries, keys, values = enter(
        inputs,
        first_gain,
        first_shift,
        query_bias,
        value_bias,
        query_weight,
        key_weight,
        value_weight,
        3,
    )
    flat_in = both_in.astype(jnp.float32)
    normed_one, norm_one_back = jax.vjp(norm_apply, flat_in, first_gain, first_shift)
    attended, log_sums, far_cot = attend(lengths, queries, keys, values, cotangent, 512, 4)
    (
        stream,
        grad_attended,
        grad_hidden,
        sums,
        grad_outer_weight,
        grad_inner_weight,
        grad_output_weight,
    ) = feed(
        lengths,
        both_in,
        attended,
        mine_of(cotangent),
        far_cot,
        (second_gain, second_shift, output_bias, outer_bias, inner_bias),
        output_weight,
        inner_weight,
        outer_weight,
    )
    data_groups = lax.axis_size("dp")
    linked = data_groups == 8 and groups == 4
    low = jnp.bfloat16
    back_args = (lengths, queries, keys, values, grad_attended, attended, log_sums, 512)
    grads_early = (grad_outer_weight, grad_inner_weight, grad_output_weight)
    def join(partial):
        far = lax.ppermute(partial[tokens_here:], "seq", beside)
        return (partial[:tokens_here].astype(jnp.float32) + far.astype(jnp.float32)).astype(
            jnp.bfloat16
        )

    if linked:
        (grad_q_tok, grad_k_tok, grad_v_tok), other_result, sums_early = attend_back_reduce(
            *back_args, stream[local_len:], grads_early, EARLY, 2
        )
        result = in_order(stream[:local_len], other_result)
    else:
        grad_q_tok, grad_k_part, grad_v_part = attend_back(*back_args)
        grad_k_tok, grad_v_tok = join(grad_k_part), join(grad_v_part)

    grads_late = tuple(
        dot(normed_one_low, grad, TN).astype(low) for grad in (grad_q_tok, grad_k_tok, grad_v_tok)
    )
    grad_query_bias = jnp.sum(grad_q_tok, axis=0, dtype=jnp.float32)
    grad_value_bias = jnp.sum(grad_v_tok, axis=0, dtype=jnp.float32)
    grad_normed_one = (
        jnp.einsum("te,de->td", grad_q_tok, query_weight, preferred_element_type=jnp.float32)
        + jnp.einsum("te,de->td", grad_k_tok, key_weight, preferred_element_type=jnp.float32)
        + jnp.einsum("te,de->td", grad_v_tok, value_weight, preferred_element_type=jnp.float32)
    )
    grad_in_norm, grad_first_gain, grad_first_shift = norm_one_back(grad_normed_one)
    grad_in = (grad_hidden + grad_in_norm).astype(jnp.bfloat16)
    packed = jnp.concatenate(
        [
            sums,
            jnp.stack([grad_first_gain, grad_first_shift, grad_query_bias, grad_value_bias]),
        ]
    )
    if linked:
        sums_late, packed, other_in = reduce_all(grads_late, LATE, packed, grad_in[local_len:], 1)
        grad_inputs = in_order(grad_in[:local_len], other_in)
    else:

        def reduced(partial):
            piece = lax.psum_scatter(partial, ("dp", "seq"), scatter_dimension=0, tiled=True)
            return lax.all_gather(piece, "seq", axis=0, tiled=True).astype(jnp.float32)

        result = give_back(stream)
        grad_inputs = give_back(grad_in)
        sums_early = [reduced(item) for item in grads_early]
        sums_late = [reduced(item) for item in grads_late]
        packed = lax.psum(packed, ("dp", "seq"))
    summed_outer, summed_inner, summed_output = sums_early
    summed_query, summed_key, summed_value = sums_late
    inner_rows = inner_weight.shape[1] // width
    grad_inner_bias = packed[:inner_rows].reshape(-1)
    tail = packed[inner_rows:]
    denominator = tail[3, 0] * width
    stream_scale = jnp.sqrt(jnp.sum(tail[0]) / denominator)
    attention_scale = jnp.sqrt(jnp.sum(tail[1]) / denominator)
    feedforward_scale = jnp.sqrt(jnp.sum(tail[2]) / denominator)
    return (
        result,
        grad_inputs,
        tail[8],
        tail[9],
        summed_query,
        tail[10],
        summed_key,
        summed_value,
        tail[11],
        summed_output,
        tail[4],
        tail[5],
        tail[6],
        summed_inner,
        grad_inner_bias,
        summed_outer,
        tail[7],
        stream_scale,
        attention_scale,
        feedforward_scale,
    )


def solution(mesh):
    return jax.shard_map(
        local,
        mesh=mesh,
        in_specs=(
            P("dp", "seq", None),
            P("dp"),
            P(),
            P(),
            P(),
            P(),
            P(),
            P(),
            P(),
            P(),
            P(),
            P(),
            P(),
            P(),
            P(),
            P(),
            P(),
            P("dp", "seq", None),
        ),
        out_specs=(
            P("dp", "seq", None),
            P("dp", "seq", None),
            P(),
            P(),
            P("dp", None),
            P(),
            P("dp", None),
            P("dp", None),
            P(),
            P("dp", None),
            P(),
            P(),
            P(),
            P("dp", None),
            P(),
            P("dp", None),
            P(),
            P(),
            P(),
            P(),
        ),
        check_vma=False,
    )
```

```python
import functools

import jax
import jax.numpy as jnp
from jax import lax
from jax.experimental import pallas as pl
from jax.experimental.pallas import tpu as pltpu
from jax.sharding import PartitionSpec as P

HEADS = 12
HEAD_DIM = 64
EPSILON = 1e-12
NEGATIVE = -1e30
PAIR = 2 * HEAD_DIM
NT = ((1,), (1,))
NN = ((1,), (0,))
TN = ((0,), (0,))


def norm_apply(values, gain_vec, shift_vec):
    average = jnp.mean(values, axis=-1, keepdims=True)
    centered = values - average
    spread = jnp.mean(centered * centered, axis=-1, keepdims=True)
    return centered * lax.rsqrt(spread + EPSILON) * gain_vec + shift_vec


def dot(left, right, dims):
    return lax.dot_general(left, right, (dims, ((), ())), preferred_element_type=jnp.float32)


def block_places():
    seq = lax.axis_index("seq")
    beside = seq + 1 - 2 * lax.rem(seq, 2)
    return seq, lax.rem(seq + 2, 4), beside, lax.rem(beside + 2, 4)


def own_length(lengths_ref):
    return lengths_ref[lax.axis_index("seq") // 2]


def fill_bias(lengths_ref, bias_ref):
    total = bias_ref.shape[0]
    block = total // 4
    spots = lax.broadcasted_iota(jnp.int32, (total, 1), 0)
    shift = 0
    for index, place in enumerate(block_places()):
        shift = jnp.where(spots >= index * block, (place - index) * block, shift)
    bias = jnp.where(spots + shift < own_length(lengths_ref), 0.0, NEGATIVE)
    bias_ref[...] = jnp.broadcast_to(bias, bias_ref.shape).astype(jnp.bfloat16)


def masked_scores(keys, bias, queries, head):
    lane = lax.broadcasted_iota(jnp.int32, (1, PAIR), 1)
    spare = HEAD_DIM * (1 - head)
    mine = (lane < HEAD_DIM) if head == 0 else (lane >= HEAD_DIM)
    ones = jnp.where(lane == spare, 1.0, 0.0).astype(jnp.bfloat16)
    left = jnp.where(lane == spare, bias, keys)
    right = jnp.where(mine, queries, jnp.broadcast_to(ones, queries.shape))
    return dot(left, right, NT)


def attend_body(
    lengths_ref, q_ref, k_ref, v_ref, cot_ref, out_ref, lse_ref, far_ref, bias_ref, swap_sems
):
    bits, across = where_am_i()
    swap = swap_copy(cot_ref.at[1 - bits["y"]], far_ref, swap_sems, across)
    now = pl.program_id(0) * pl.num_programs(1) + pl.program_id(1)

    @pl.when(now == 0)
    def _():
        greet(across, ("y",))
        swap.start()
        fill_bias(lengths_ref, bias_ref)

    scale = jnp.bfloat16(HEAD_DIM ** (-0.5))
    queries = q_ref[...] * scale
    keys = k_ref[...]
    values_t = v_ref[...].T
    bias = bias_ref[...]
    outs = []
    for head in range(2):
        scores = masked_scores(keys, bias, queries, head)
        top = jnp.max(scores, axis=0, keepdims=True)
        weights = jnp.exp(scores - top)
        total = jnp.sum(weights, axis=0, keepdims=True)
        mixed = dot(
            values_t[HEAD_DIM * head : HEAD_DIM * (head + 1)], weights.astype(jnp.bfloat16), NN
        )
        outs.append(mixed * (1.0 / total))
        lse_ref[0, head : head + 1, :] = top + jnp.log(total)
    out_ref[...] = jnp.concatenate(outs, axis=0).T.astype(jnp.bfloat16)

    @pl.when(now == pl.num_programs(0) * pl.num_programs(1) - 1)
    def _():
        swap.wait()


def attend(info, queries, keys, values, cotangent, block, collective):
    tokens, width = queries.shape
    total = keys.shape[0]
    pairs = width // PAIR
    q_spec = pl.BlockSpec((block, PAIR), lambda h, i, n: (i, h))
    k_spec = pl.BlockSpec((total, PAIR), lambda h, i, n: (0, h))
    return pl.pallas_call(
        attend_body,
        grid_spec=pltpu.PrefetchScalarGridSpec(
            num_scalar_prefetch=1,
            grid=(pairs, tokens // block),
            in_specs=[q_spec, k_spec, k_spec, pl.BlockSpec(memory_space=pl.ANY)],
            out_specs=[
                q_spec,
                pl.BlockSpec((1, 2, block), lambda h, i, n: (h, 0, i)),
                pl.BlockSpec(memory_space=pl.ANY),
            ],
            scratch_shapes=[
                pltpu.VMEM((total, PAIR), jnp.bfloat16),
                pltpu.SemaphoreType.DMA((2,)),
            ],
        ),
        out_shape=[
            jax.ShapeDtypeStruct((tokens, width), jnp.bfloat16),
            jax.ShapeDtypeStruct((pairs, 2, tokens), jnp.float32),
            jax.ShapeDtypeStruct(cotangent.shape[1:], cotangent.dtype),
        ],
        compiler_params=pltpu.CompilerParams(
            collective_id=collective, has_side_effects=True, vmem_limit_bytes=48 << 20
        ),
        cost_estimate=pl.CostEstimate(
            flops=16 * tokens * total * width, bytes_accessed=1 << 23, transcendentals=0
        ),
        name="attend",
    )(info, queries, keys, values, cotangent)


def attend_back_body(
    lengths_ref,
    q_ref,
    k_ref,
    v_ref,
    do_ref,
    o_ref,
    lse_ref,
    dq_ref,
    dk_ref,
    dv_ref,
    bias_ref,
    dk_acc,
    dv_acc,
    before=None,
    after=None,
):
    step = pl.program_id(1)

    @pl.when((step == 0) & (pl.program_id(0) == 0))
    def _():
        fill_bias(lengths_ref, bias_ref)

    lane = lax.broadcasted_iota(jnp.int32, (1, PAIR), 1)
    scale = jnp.bfloat16(HEAD_DIM ** (-0.5))
    grad_out = do_ref[...]
    queries = q_ref[...] * scale
    keys = k_ref[...]
    keys_t = keys.T
    values = v_ref[...]
    product = grad_out.astype(jnp.float32) * o_ref[...].astype(jnp.float32)
    pick = (
        lax.broadcasted_iota(jnp.int32, (8, PAIR), 1) // HEAD_DIM
        == lax.broadcasted_iota(jnp.int32, (8, PAIR), 0)
    ).astype(jnp.float32)
    row_sums = lax.dot_general(
        pick,
        product,
        (NT, ((), ())),
        precision=lax.Precision.HIGHEST,
        preferred_element_type=jnp.float32,
    )
    bias = bias_ref[...]
    zero = jnp.zeros_like(queries)
    grad_k = 0
    grad_v = 0
    grad_q = []
    for head in range(2):
        if before is not None:
            before(head)
        mine = (lane < HEAD_DIM) if head == 0 else (lane >= HEAD_DIM)
        query_h = jnp.where(mine, queries, zero)
        out_h = jnp.where(mine, grad_out, zero)
        scores = masked_scores(keys, bias, queries, head)
        weights = jnp.exp(scores - lse_ref[0, head : head + 1, :])
        grad_w = dot(values, out_h, NT)
        grad_s = (weights * (grad_w - row_sums[head : head + 1])).astype(jnp.bfloat16)
        grad_v = grad_v + dot(weights.astype(jnp.bfloat16), out_h, NN)
        grad_k = grad_k + dot(grad_s, query_h, NN)
        grad_q.append(dot(keys_t[HEAD_DIM * head : HEAD_DIM * (head + 1)], grad_s, NN))
    grad_q = jnp.concatenate(grad_q, axis=0) * (HEAD_DIM ** (-0.5))
    dq_ref[...] = grad_q.T.astype(jnp.bfloat16)

    @pl.when(step == 0)
    def _():
        dk_acc[...] = grad_k
        dv_acc[...] = grad_v

    @pl.when(step > 0)
    def _():
        dk_acc[...] += grad_k
        dv_acc[...] += grad_v

    @pl.when(step == pl.num_programs(1) - 1)
    def _():
        near = dk_ref.shape[0]
        dk_ref[...] = dk_acc[:near].astype(jnp.bfloat16)
        dv_ref[...] = dv_acc[:near].astype(jnp.bfloat16)
        if after is not None:
            after()


def attend_back(info, queries, keys, values, grad_out, out, log_sums, block):
    tokens, width = queries.shape
    total = keys.shape[0]
    pairs = width // PAIR
    q_spec = pl.BlockSpec((block, PAIR), lambda h, i, n: (i, h))
    k_spec = pl.BlockSpec((total, PAIR), lambda h, i, n: (0, h))
    return pl.pallas_call(
        attend_back_body,
        grid_spec=pltpu.PrefetchScalarGridSpec(
            num_scalar_prefetch=1,
            grid=(pairs, tokens // block),
            in_specs=[
                q_spec,
                k_spec,
                k_spec,
                q_spec,
                q_spec,
                pl.BlockSpec((1, 2, block), lambda h, i, n: (h, 0, i)),
            ],
            out_specs=[q_spec, k_spec, k_spec],
            scratch_shapes=[
                pltpu.VMEM((total, PAIR), jnp.bfloat16),
                pltpu.VMEM((total, PAIR), jnp.float32),
                pltpu.VMEM((total, PAIR), jnp.float32),
            ],
        ),
        out_shape=[
            jax.ShapeDtypeStruct((tokens, width), jnp.bfloat16),
            jax.ShapeDtypeStruct((total, width), jnp.bfloat16),
            jax.ShapeDtypeStruct((total, width), jnp.bfloat16),
        ],
        compiler_params=pltpu.CompilerParams(vmem_limit_bytes=48 << 20),
        cost_estimate=pl.CostEstimate(
            flops=40 * tokens * total * width, bytes_accessed=1 << 24, transcendentals=0
        ),
        name="attend_back",
    )(info, queries, keys, values, grad_out, out, log_sums)


MESH_IDS = pl.DeviceIdType.MESH
AXES = ("zhi", "zlo", "x", "y")
LATE = (("x", "zlo", "zhi", "y"), ("zlo", "x", "zhi", "y"), ("x", "zlo", "zhi", "y"))


def where_am_i():
    data = lax.axis_index("dp")
    seq = lax.axis_index("seq")
    bits = {
        "zhi": data // 4,
        "zlo": (data // 2) % 2,
        "x": data % 2,
        "y": seq // 2,
        "core": seq % 2,
    }

    def across(axis):
        if axis == "core":
            return (data, seq + 1 - 2 * bits["core"])
        if axis == "y":
            return (data, seq + 2 - 4 * bits["y"])
        step = {"zhi": 4, "zlo": 2, "x": 1}[axis]
        return (data + step - 2 * step * bits[axis], seq)

    return bits, across


def spot_of(piece, order):
    bits = {axis: (piece >> (3 - k)) & 1 for k, axis in enumerate(AXES)}
    return sum(bits[axis] << (3 - k) for k, axis in enumerate(order))


class Color:
    def __init__(self, source, acc, lands, gathers, sems, order):
        self.source, self.acc, self.lands, self.gathers = source, acc, lands, gathers
        self.sems, self.order = sems, order
        self.pieces, self.rows, self.cols = acc.shape
        self.bits, self.across = where_am_i()

    def base(self, stage):
        return sum(self.bits[self.order[k]] * (self.pieces >> (k + 1)) for k in range(stage))

    def remote(self, src, dst, slot, axis):
        return pltpu.make_async_remote_copy(
            src_ref=src,
            dst_ref=dst,
            send_sem=self.sems.at[0, slot],
            recv_sem=self.sems.at[1, slot],
            device_id=self.across(axis),
            device_id_type=MESH_IDS,
        )

    def begin(self):
        core = self.bits["core"]
        mine = pl.ds(pl.multiple_of(core * self.cols, 128), self.cols)
        theirs = pl.ds(pl.multiple_of((1 - core) * self.cols, 128), self.cols)
        for piece in range(self.pieces):
            spot = spot_of(piece, self.order)
            span = pl.ds(piece * self.rows, self.rows)
            self.remote(
                self.source.at[span, theirs], self.lands[0].at[spot], 0, "core"
            ).start()
            pltpu.make_async_copy(
                self.source.at[span, mine], self.acc.at[spot], self.sems.at[0, 7]
            ).start()

    def add(self, base, count, land):
        @pl.loop(0, count)
        def _(index):
            total = self.acc[base + index].astype(jnp.float32) + land[index].astype(jnp.float32)
            self.acc[base + index] = total.astype(jnp.bfloat16)

    def transfer(self, stage):
        if stage < 4:
            axis = self.order[stage]
            half = self.pieces >> (stage + 1)
            start = self.base(stage) + (1 - self.bits[axis]) * half
            return self.remote(
                self.acc.at[pl.ds(start, half)], self.lands[stage + 1], stage + 1, axis
            )
        if stage == 4:
            there = self.gathers[0].at[self.bits["y"]]
            return self.remote(self.acc.at[self.base(4)], there, 5, "y")
        return self.remote(self.gathers[0], self.gathers[1], 6, "core")

    def step(self, stage):
        if stage == 0:
            whole = self.remote(self.lands[0], self.lands[0], 0, "core")
            pltpu.make_async_copy(self.acc, self.acc, self.sems.at[0, 7]).wait()
            whole.wait_send()
            whole.wait_recv()
        else:
            self.transfer(stage - 1).wait()
        if stage <= 4:
            self.add(self.base(stage), self.pieces >> stage, self.lands[stage])
        if stage == 4:
            self.gathers[0][self.bits["y"]] = self.acc[self.base(4)]
        if stage < 6:
            self.transfer(stage).start()


def swap_copy(source, landing, sems, across):
    return pltpu.make_async_remote_copy(
        src_ref=source,
        dst_ref=landing,
        send_sem=sems.at[0],
        recv_sem=sems.at[1],
        device_id=across("y"),
        device_id_type=MESH_IDS,
    )


def greet(across, axes=("core", *AXES)):
    barrier = pltpu.get_barrier_semaphore()
    for axis in axes:
        pl.semaphore_signal(barrier, inc=1, device_id=across(axis), device_id_type=MESH_IDS)
    pl.semaphore_wait(barrier, len(axes))


CHUNKS = 4


def enter_body(
    in_ref,
    gain_ref,
    shift_ref,
    q_bias_ref,
    v_bias_ref,
    wq_ref,
    wk_ref,
    wv_ref,
    x_ref,
    normed_ref,
    q_ref,
    k_ref,
    v_ref,
    swap_sems,
    own_sem,
    trade_sems,
):
    low = jnp.bfloat16
    bits, across = where_am_i()
    row = bits["y"]
    size = x_ref.shape[0] // CHUNKS
    tokens = x_ref.shape[0]
    half = CHUNKS // 2
    own = pltpu.make_async_copy(in_ref.at[row], x_ref.at[pl.ds(0, tokens // 2)], own_sem)
    own.start()
    greet(across, ("core", "y"))

    def arrival(chunk):
        return pltpu.make_async_remote_copy(
            src_ref=in_ref.at[1 - row, pl.ds(pl.multiple_of(chunk * size, size), size)],
            dst_ref=x_ref.at[pl.ds(pl.multiple_of((half + chunk) * size, size), size)],
            send_sem=swap_sems.at[0, chunk],
            recv_sem=swap_sems.at[1, chunk],
            device_id=across("y"),
            device_id_type=MESH_IDS,
        )

    def trade(chunk, which):
        ref = (k_ref, v_ref)[which]
        return pltpu.make_async_remote_copy(
            src_ref=ref.at[pl.ds(pl.multiple_of(chunk * size, size), size)],
            dst_ref=ref.at[pl.ds(pl.multiple_of(tokens + chunk * size, size), size)],
            send_sem=trade_sems.at[0, which, chunk],
            recv_sem=trade_sems.at[1, which, chunk],
            device_id=across("core"),
            device_id_type=MESH_IDS,
        )

    for chunk in range(half):
        arrival(chunk).start()
    own.wait()

    @pl.loop(0, CHUNKS)
    def _(chunk):
        @pl.when(chunk >= half)
        def _():
            arrival(chunk - half).wait()

        span = pl.ds(pl.multiple_of(chunk * size, size), size)
        rows = x_ref[span, :].astype(jnp.float32)
        normed = norm_apply(rows, gain_ref[...], shift_ref[...]).astype(low)
        normed_ref[span, :] = normed
        k_ref[span, :] = dot(normed, wk_ref[...], NN).astype(low)
        trade(chunk, 0).start()
        v_ref[span, :] = (dot(normed, wv_ref[...], NN) + v_bias_ref[...]).astype(low)
        trade(chunk, 1).start()
        q_ref[span, :] = (dot(normed, wq_ref[...], NN) + q_bias_ref[...]).astype(low)

    @pl.loop(0, CHUNKS)
    def _(chunk):
        trade(chunk, 0).wait()
        trade(chunk, 1).wait()


def enter(inputs, gain, shift, q_bias, v_bias, wq, wk, wv, collective):
    _, local_len, width = inputs.shape
    vmem = pl.BlockSpec(memory_space=pltpu.VMEM)

    def made(blocks):
        return jax.ShapeDtypeStruct((blocks * local_len, width), jnp.bfloat16)

    return pl.pallas_call(
        enter_body,
        out_shape=[made(2), made(2), made(2), made(4), made(4)],
        in_specs=[pl.BlockSpec(memory_space=pl.ANY)] + [vmem] * 7,
        out_specs=[vmem] * 5,
        scratch_shapes=[
            pltpu.SemaphoreType.DMA((2, CHUNKS // 2)),
            pltpu.SemaphoreType.DMA,
            pltpu.SemaphoreType.DMA((2, 2, CHUNKS)),
        ],
        compiler_params=pltpu.CompilerParams(
            collective_id=collective, has_side_effects=True, vmem_limit_bytes=48 << 20
        ),
        name="enter",
    )(inputs, gain[None], shift[None], q_bias[None], v_bias[None], wq, wk, wv)


def color_scratch(arrays):
    scratch = []
    outs = []
    for array in arrays:
        rows, cols = array.shape[0] // 16, array.shape[1] // 2
        scratch.append(pltpu.VMEM((16, rows, cols), jnp.bfloat16))
        for size in (16, 8, 4, 2, 1):
            scratch.append(pltpu.VMEM((size, rows, cols), jnp.bfloat16))
        scratch += [pltpu.VMEM((2, rows, cols), jnp.bfloat16)] * 2
        scratch.append(pltpu.SemaphoreType.DMA((2, 8)))
        outs += [jax.ShapeDtypeStruct((2, rows, cols), jnp.bfloat16)] * 2
    return scratch, outs


def colors_of(sources, scratch, orders):
    colors = []
    for index, source in enumerate(sources):
        acc, *lands = scratch[9 * index : 9 * index + 6]
        gathers = scratch[9 * index + 6 : 9 * index + 8]
        sems = scratch[9 * index + 8]
        colors.append(Color(source, acc, lands, gathers, sems, orders[index]))
    return colors


def hand_out(colors, outs):
    for index, color in enumerate(colors):
        outs[2 * index][...] = color.gathers[0][...]
        outs[2 * index + 1][...] = color.gathers[1][...]


def assemble(arrays, got):
    core = lax.axis_index("seq") % 2
    sums = []
    for index, array in enumerate(arrays):
        mine, other = got[2 * index], got[2 * index + 1]
        rows = array.shape[0] // 8
        left = jnp.where(core == 0, mine, other).reshape(rows, -1)
        right = jnp.where(core == 0, other, mine).reshape(rows, -1)
        sums.append(jnp.concatenate([left, right], axis=1).astype(jnp.float32))
    return sums


def vector_sum(held, lands, sems, across):
    for slot, axis in enumerate(("core", "y", "x", "zlo", "zhi")):
        copy = pltpu.make_async_remote_copy(
            src_ref=held,
            dst_ref=lands.at[slot],
            send_sem=sems.at[0, slot],
            recv_sem=sems.at[1, slot],
            device_id=across(axis),
            device_id_type=MESH_IDS,
        )
        copy.start()
        yield
        copy.wait()
        held[...] = held[...] + lands[slot]


def leave_body(
    orders,
    x_ref,
    normed_ref,
    gq_ref,
    gk_ref,
    gk_far_ref,
    gv_ref,
    gv_far_ref,
    g_hidden_ref,
    gain_ref,
    wq_ref,
    wk_ref,
    wv_ref,
    sums_ref,
    *refs,
):
    outs = refs[:6]
    vector_ref, grad_ref, far_ref = refs[6:9]
    gk_all, gv_all, *products = refs[9:14]
    vector_lands, vector_sems, swap_sems, *scratch = refs[14:]
    low = jnp.bfloat16
    bits, across = where_am_i()
    colors = colors_of(products, scratch, orders)
    gk_all[...] = (gk_ref[...].astype(jnp.float32) + gk_far_ref[...].astype(jnp.float32)).astype(low)
    gv_all[...] = (gv_ref[...].astype(jnp.float32) + gv_far_ref[...].astype(jnp.float32)).astype(low)
    greet(across)
    for product, grads, color in zip(products, (gq_ref, gk_all, gv_all), colors):
        product[...] = dot(normed_ref[...], grads[...], TN).astype(low)
        color.begin()
    colors[0].step(0)
    colors[1].step(0)
    count = x_ref.shape[0] // 2
    swap = swap_copy(grad_ref.at[pl.ds(count, count)], far_ref, swap_sems, across)
    early = sums_ref.shape[0]
    vector_ref[:early] = sums_ref[...]
    vector_ref[early:] = jnp.zeros_like(vector_ref[early:])
    gain = gain_ref[...]
    for start in (count, 0):
        span = slice(start, start + count)
        rows = x_ref[span].astype(jnp.float32)
        centered = rows - jnp.mean(rows, axis=-1, keepdims=True)
        spread = lax.rsqrt(jnp.mean(centered * centered, axis=-1, keepdims=True) + EPSILON)
        normal = centered * spread
        gq, gv = gq_ref[span], gv_all[span]
        g_normed = (
            dot(gq, wq_ref[...], NT)
            + dot(gk_all[span], wk_ref[...], NT)
            + dot(gv, wv_ref[...], NT)
        )
        e = g_normed * gain
        g_rows = spread * (
            e
            - jnp.mean(e, axis=-1, keepdims=True)
            - normal * jnp.mean(e * normal, axis=-1, keepdims=True)
        )
        grad_ref[span] = (g_hidden_ref[span] + g_rows).astype(low)
        if start:
            swap.start()
            colors[2].step(0)
        late = [g_normed * normal, g_normed, gq.astype(jnp.float32), gv.astype(jnp.float32)]
        vector_ref[early:] += jnp.concatenate(
            [jnp.sum(item, axis=0, keepdims=True) for item in late], axis=0
        )
    small = vector_sum(vector_ref, vector_lands, vector_sems, across)
    next(small)
    for stage in range(1, 7):
        for color in colors:
            color.step(stage)
        next(small, None)
    hand_out(colors, outs)
    swap.wait()


def leave(x, normed, gq, gks, gvs, g_hidden, gain, wq, wk, wv, sums, orders, collective):
    tokens, width = x.shape
    vmem = pl.BlockSpec(memory_space=pltpu.VMEM)
    square = jax.ShapeDtypeStruct((width, width), jnp.bfloat16)
    arrays = (square,) * 3
    scratch, outs = color_scratch(arrays)
    vector = (sums.shape[0] + 4, width)
    outs += [
        jax.ShapeDtypeStruct(vector, jnp.float32),
        jax.ShapeDtypeStruct((tokens, width), jnp.bfloat16),
        jax.ShapeDtypeStruct((tokens // 2, width), jnp.bfloat16),
    ]
    got = pl.pallas_call(
        functools.partial(leave_body, orders),
        out_shape=outs,
        in_specs=[vmem] * 13,
        out_specs=[*[vmem] * (len(outs) - 1), pl.BlockSpec(memory_space=pl.ANY)],
        scratch_shapes=[
            *[pltpu.VMEM((tokens, width), jnp.bfloat16)] * 2,
            *[pltpu.VMEM((width, width), jnp.bfloat16)] * 3,
            pltpu.VMEM((5, *vector), jnp.float32),
            pltpu.SemaphoreType.DMA((2, 5)),
            pltpu.SemaphoreType.DMA((2,)),
            *scratch,
        ],
        compiler_params=pltpu.CompilerParams(
            collective_id=collective, has_side_effects=True, vmem_limit_bytes=56 << 20
        ),
        cost_estimate=pl.CostEstimate(flops=1 << 34, bytes_accessed=1 << 24, transcendentals=0),
        name="leave",
    )(x, normed, gq, *gks, *gvs, g_hidden, gain[None], wq, wk, wv, sums)
    return assemble(arrays, got), got[6], got[7], got[8]


TIMES = ((3, 11, 15, 17, 20, 22, 24), (4, 12, 16, 18, 21, 22, 24), (5, 8, 10, 13, 16, 19, 21))
EARLY = (("x", "y", "zlo", "zhi"), ("zlo", "x", "y", "zhi"), ("y", "x", "zlo", "zhi"))


def attend_back_reduce_body(count, orders, *refs):
    info_ref, *blocks = refs[:7]
    swap_in, *sources = refs[7 : 8 + count]
    results = refs[8 + count : 11 + count]
    outs = refs[11 + count : 11 + 3 * count]
    far = refs[11 + 3 * count : 13 + 3 * count]
    swap_out = refs[13 + 3 * count]
    bias_ref, dk_acc, dv_acc, *scratch = refs[14 + 3 * count :]
    send_k, send_v, trade_sems, swap_sems, *scratch = scratch
    pair = pl.program_id(0)
    pairs = pl.num_programs(0)
    now = 2 * (pair * pl.num_programs(1) + pl.program_id(1))
    last = 2 * pairs * pl.num_programs(1)
    bits, across = where_am_i()
    colors = colors_of(sources, scratch, orders)

    def trade(index, which):
        return pltpu.make_async_remote_copy(
            src_ref=(send_k, send_v)[which].at[index],
            dst_ref=far[which].at[:, pl.ds(pl.multiple_of(index * PAIR, PAIR), PAIR)],
            send_sem=trade_sems.at[0, which, index],
            recv_sem=trade_sems.at[1, which, index],
            device_id=across("core"),
            device_id_type=MESH_IDS,
        )

    def before(head):
        if head == 0:

            @pl.when(now == 0)
            def _():
                greet(across)
                swap_copy(swap_in, swap_out, swap_sems, across).start()
                for color in colors:
                    color.begin()

        for when in sorted({when for times in TIMES for when in times if when % 2 == head}):

            @pl.when(now + head == when)
            def _(when=when):
                for color, times in zip(colors, TIMES):
                    for stage in range(7):
                        if times[stage] == when:
                            color.step(stage)

    def after():
        near = results[1].shape[0]
        send_k[pair] = dk_acc[near:].astype(jnp.bfloat16)
        send_v[pair] = dv_acc[near:].astype(jnp.bfloat16)
        trade(pair, 0).start()
        trade(pair, 1).start()

    attend_back_body(info_ref, *blocks, *results, bias_ref, dk_acc, dv_acc, before, after)

    @pl.when(now + 2 == last)
    def _():
        for color, times in zip(colors, TIMES):
            for stage in range(7):
                if times[stage] >= last:
                    color.step(stage)
        hand_out(colors, outs)
        swap_copy(swap_in, swap_out, swap_sems, across).wait()

        @pl.loop(0, pairs)
        def _(index):
            trade(index, 0).wait()
            trade(index, 1).wait()


def attend_back_reduce(
    info, queries, keys, values, grad_out, out, log_sums, block, swap, arrays, orders, collective
):
    tokens, width = queries.shape
    total = keys.shape[0]
    near = total // 2
    pairs = width // PAIR
    scratch, outs = color_scratch(arrays)
    q_spec = pl.BlockSpec((block, PAIR), lambda h, i, n: (i, h))
    k_spec = pl.BlockSpec((total, PAIR), lambda h, i, n: (0, h))
    near_spec = pl.BlockSpec((near, PAIR), lambda h, i, n: (0, h))
    whole = pl.BlockSpec(memory_space=pltpu.VMEM)
    anywhere = pl.BlockSpec(memory_space=pl.ANY)
    far = jax.ShapeDtypeStruct((near, width), jnp.bfloat16)
    got = pl.pallas_call(
        functools.partial(attend_back_reduce_body, len(arrays), orders),
        grid_spec=pltpu.PrefetchScalarGridSpec(
            num_scalar_prefetch=1,
            grid=(pairs, tokens // block),
            in_specs=[
                q_spec,
                k_spec,
                k_spec,
                q_spec,
                q_spec,
                pl.BlockSpec((1, 2, block), lambda h, i, n: (h, 0, i)),
                *[anywhere] * (1 + len(arrays)),
            ],
            out_specs=[q_spec, near_spec, near_spec, *[whole] * len(outs), *[anywhere] * 3],
            scratch_shapes=[
                pltpu.VMEM((total, PAIR), jnp.bfloat16),
                pltpu.VMEM((total, PAIR), jnp.float32),
                pltpu.VMEM((total, PAIR), jnp.float32),
                pltpu.VMEM((pairs, near, PAIR), jnp.bfloat16),
                pltpu.VMEM((pairs, near, PAIR), jnp.bfloat16),
                pltpu.SemaphoreType.DMA((2, 2, pairs)),
                pltpu.SemaphoreType.DMA((2,)),
                *scratch,
            ],
        ),
        out_shape=[
            jax.ShapeDtypeStruct((tokens, width), jnp.bfloat16),
            jax.ShapeDtypeStruct((near, width), jnp.bfloat16),
            jax.ShapeDtypeStruct((near, width), jnp.bfloat16),
            *outs,
            far,
            far,
            jax.ShapeDtypeStruct(swap.shape, swap.dtype),
        ],
        compiler_params=pltpu.CompilerParams(
            collective_id=collective, has_side_effects=True, vmem_limit_bytes=62 << 20
        ),
        cost_estimate=pl.CostEstimate(
            flops=40 * tokens * total * width, bytes_accessed=1 << 25, transcendentals=0
        ),
        name="attend_back_reduce",
    )(info, queries, keys, values, grad_out, out, log_sums, swap, *arrays)

    grads = (got[0], (got[1], got[-3]), (got[2], got[-2]))
    return grads, got[-1], assemble(arrays, got[3:-3])


def feed_body(
    lengths_ref,
    x_ref,
    att_ref,
    cot_ref,
    cot_far_ref,
    gain_ref,
    shift_ref,
    out_bias_ref,
    outer_bias_ref,
    inner_bias_ref,
    wo_ref,
    wi_ref,
    wf_ref,
    result_ref,
    g_att_ref,
    g_hidden_ref,
    sums_ref,
    g_wf_ref,
    g_wi_ref,
    g_wo_ref,
    act_all,
    g_inner_all,
    normed_all,
    g_ffn_all,
    att_all,
    g_attn_all,
):
    step = pl.program_id(0)
    block, width = x_ref.shape
    chunks = wi_ref.shape[1] // width

    @pl.when(step < 2)
    def _():
        span = pl.ds(pl.multiple_of(step * block, block), block)
        att_all[span, :] = att_ref[...]
        feed_block(
            lengths_ref,
            x_ref,
            att_ref,
            cot_ref,
            cot_far_ref,
            gain_ref,
            shift_ref,
            out_bias_ref,
            outer_bias_ref,
            inner_bias_ref,
            wo_ref,
            wi_ref,
            wf_ref,
            result_ref,
            normed_all.at[span],
            act_all.at[span],
            g_inner_all.at[span],
            g_ffn_all.at[span],
            g_attn_all.at[span],
            g_att_ref,
            g_hidden_ref,
            sums_ref,
        )

    @pl.when((step >= 2) & (step < 2 + chunks))
    def _():
        span = pl.ds(pl.multiple_of((step - 2) * width, width), width)
        g_wf_ref[...] = dot(act_all[:, span], g_ffn_all[...], TN).astype(jnp.bfloat16)

    @pl.when((step >= 2 + chunks) & (step < 2 + 2 * chunks))
    def _():
        span = pl.ds(pl.multiple_of((step - 2 - chunks) * width, width), width)
        g_wi_ref[...] = dot(normed_all[...], g_inner_all[:, span], TN).astype(jnp.bfloat16)

    @pl.when(step == 2 + 2 * chunks)
    def _():
        g_wo_ref[...] = dot(att_all[...], g_attn_all[...], TN).astype(jnp.bfloat16)


def feed_block(
    lengths_ref,
    x_ref,
    att_ref,
    cot_ref,
    cot_far_ref,
    gain_ref,
    shift_ref,
    out_bias_ref,
    outer_bias_ref,
    inner_bias_ref,
    wo_ref,
    wi_ref,
    wf_ref,
    result_ref,
    normed_ref,
    act_ref,
    g_inner_ref,
    g_ffn_ref,
    g_attn_ref,
    g_att_ref,
    g_hidden_ref,
    sums_ref,
):
    low = jnp.bfloat16
    width = x_ref.shape[1]
    inner_total = inner_bias_ref.shape[1]
    gain, shift = gain_ref[...], shift_ref[...]
    out_bias, outer_bias = out_bias_ref[...], outer_bias_ref[...]
    own = pl.program_id(0) == 0
    block = x_ref.shape[0]
    seq = lax.axis_index("seq")
    start_at = jnp.where(own, seq, lax.rem(seq + 2, 4)) * block
    spots = lax.broadcasted_iota(jnp.int32, (block, 1), 0) + start_at
    keep = (spots < own_length(lengths_ref)).astype(jnp.float32)
    cot = jnp.where(own, cot_ref[...], cot_far_ref[...])
    branch_attn = dot(att_ref[...], wo_ref[...], NN) + out_bias
    hidden = x_ref[...].astype(jnp.float32) + branch_attn
    centered = hidden - jnp.mean(hidden, axis=-1, keepdims=True)
    spread = lax.rsqrt(jnp.mean(centered * centered, axis=-1, keepdims=True) + EPSILON)
    normal = centered * spread
    normed = (normal * gain + shift).astype(low)
    normed_ref[...] = normed
    g_stream = keep * cot.astype(jnp.float32)
    g_ffn = g_stream.astype(low)
    g_ffn_ref[...] = g_ffn
    branch = jnp.zeros_like(hidden) + outer_bias
    g_normed = jnp.zeros_like(hidden)
    sums = []
    for start in range(0, inner_total, width):
        span = slice(start, start + width)
        inner = dot(normed, wi_ref[:, span], NN) + inner_bias_ref[:, span]
        g_act = dot(g_ffn, wf_ref[span, :], NT)
        cdf = 0.5 + 0.5 * lax.erf(inner * (0.5**0.5))
        act = (inner * cdf).astype(low)
        slope = cdf + inner * (jnp.exp(-0.5 * inner * inner) * ((0.5 / jnp.pi) ** 0.5))
        g_inner = (g_act * slope).astype(low)
        act_ref[:, span] = act
        g_inner_ref[:, span] = g_inner
        branch = branch + dot(act, wf_ref[span, :], NN)
        g_normed = g_normed + dot(g_inner, wi_ref[:, span], NT)
        sums.append(jnp.sum(g_inner.astype(jnp.float32), axis=0, keepdims=True))
    stream = keep * (hidden + branch)
    result_ref[...] = stream.astype(low)
    e = g_normed * gain
    g_hidden = g_stream + spread * (
        e
        - jnp.mean(e, axis=-1, keepdims=True)
        - normal * jnp.mean(e * normal, axis=-1, keepdims=True)
    )
    g_hidden_ref[...] = g_hidden
    g_attn = g_hidden.astype(low)
    g_attn_ref[...] = g_attn
    g_att_ref[...] = dot(g_attn, wo_ref[...], NT).astype(low)
    for item in (
        stream * stream,
        keep * branch_attn * branch_attn,
        keep * branch * branch,
        jnp.broadcast_to(keep, hidden.shape),
        g_attn.astype(jnp.float32),
        g_normed * normal,
        g_normed,
        g_ffn.astype(jnp.float32),
    ):
        sums.append(jnp.sum(item, axis=0, keepdims=True))
    block = jnp.concatenate(sums, axis=0)

    @pl.when(pl.program_id(0) == 0)
    def _():
        sums_ref[...] = block

    @pl.when(pl.program_id(0) > 0)
    def _():
        sums_ref[...] += block


def feed(lengths, x, att, cot, cot_far, vectors, wo, wi, wf):
    tokens, width = x.shape
    inner_total = wi.shape[1]
    low = jnp.bfloat16
    block = tokens // 2
    chunks = inner_total // width
    slot = pl.BlockSpec((block, width), lambda i, n: (jnp.minimum(i, 1), 0))

    def fixed(shape):
        return pl.BlockSpec(shape, lambda i, n: (0, 0), pipeline_mode=pl.Buffered(1))

    sums_rows = chunks + 8
    return pl.pallas_call(
        feed_body,
        grid_spec=pltpu.PrefetchScalarGridSpec(
            num_scalar_prefetch=1,
            grid=(3 + 2 * chunks,),
            in_specs=[
                slot,
                slot,
                fixed(cot.shape),
                fixed(cot.shape),
                *[fixed((1, item.shape[0])) for item in vectors],
                fixed(wo.shape),
                fixed(wi.shape),
                fixed(wf.shape),
            ],
            out_specs=[
                slot,
                slot,
                slot,
                pl.BlockSpec((sums_rows, width), lambda i, n: (0, 0)),
                pl.BlockSpec((width, width), lambda i, n: (jnp.clip(i - 2, 0, chunks - 1), 0)),
                pl.BlockSpec(
                    (width, width), lambda i, n: (0, jnp.clip(i - 2 - chunks, 0, chunks - 1))
                ),
                pl.BlockSpec((width, width), lambda i, n: (0, 0)),
            ],
            scratch_shapes=[
                pltpu.VMEM((tokens, inner_total), low),
                pltpu.VMEM((tokens, inner_total), low),
                *[pltpu.VMEM((tokens, width), low)] * 4,
            ],
        ),
        out_shape=[
            jax.ShapeDtypeStruct((tokens, width), low),
            jax.ShapeDtypeStruct((tokens, width), low),
            jax.ShapeDtypeStruct((tokens, width), jnp.float32),
            jax.ShapeDtypeStruct((sums_rows, width), jnp.float32),
            jax.ShapeDtypeStruct((inner_total, width), low),
            jax.ShapeDtypeStruct((width, inner_total), low),
            jax.ShapeDtypeStruct((width, width), low),
        ],
        compiler_params=pltpu.CompilerParams(vmem_limit_bytes=62 << 20),
        cost_estimate=pl.CostEstimate(
            flops=6 * tokens * width * (width + 2 * inner_total),
            bytes_accessed=1 << 25,
            transcendentals=0,
        ),
        name="feed",
    )(lengths, x, att, cot, cot_far, *[item[None] for item in vectors], wo, wi, wf)


def local(
    inputs,
    lengths,
    first_gain,
    first_shift,
    query_weight,
    query_bias,
    key_weight,
    value_weight,
    value_bias,
    output_weight,
    output_bias,
    second_gain,
    second_shift,
    inner_weight,
    inner_bias,
    outer_weight,
    outer_bias,
    cotangent,
):
    groups = lax.axis_size("seq")
    seq_count, local_len, width = inputs.shape
    full_len = local_len * groups
    tokens_here = seq_count * local_len
    place = lax.axis_index("seq")
    half = groups // 2
    row = place // half
    across = [(i, (i + half) % groups) for i in range(groups)]
    beside = [(i, i ^ 1) for i in range(groups)]

    def mine_of(array):
        return lax.dynamic_index_in_dim(array, row, 0, keepdims=False)

    def in_order(own, other):
        return jnp.where(row == 0, jnp.stack([own, other]), jnp.stack([other, own]))

    def give_back(array):
        return in_order(array[:local_len], lax.ppermute(array[local_len:], "seq", across))

    both_in, normed_one_low, queries, keys, values = enter(
        inputs,
        first_gain,
        first_shift,
        query_bias,
        value_bias,
        query_weight,
        key_weight,
        value_weight,
        3,
    )
    attended, log_sums, far_cot = attend(lengths, queries, keys, values, cotangent, 512, 4)
    (
        stream,
        grad_attended,
        grad_hidden,
        sums,
        grad_outer_weight,
        grad_inner_weight,
        grad_output_weight,
    ) = feed(
        lengths,
        both_in,
        attended,
        mine_of(cotangent),
        far_cot,
        (second_gain, second_shift, output_bias, outer_bias, inner_bias),
        output_weight,
        inner_weight,
        outer_weight,
    )
    data_groups = lax.axis_size("dp")
    linked = data_groups == 8 and groups == 4
    low = jnp.bfloat16
    back_args = (lengths, queries, keys, values, grad_attended, attended, log_sums, 512)
    grads_early = (grad_outer_weight, grad_inner_weight, grad_output_weight)

    if linked:
        (grad_q, grads_k, grads_v), other_result, sums_early = attend_back_reduce(
            *back_args, stream[local_len:], grads_early, EARLY, 2
        )
        result = in_order(stream[:local_len], other_result)
        sums_late, packed, grad_in, other_in = leave(
            both_in,
            normed_one_low,
            grad_q,
            grads_k,
            grads_v,
            grad_hidden,
            first_gain,
            query_weight,
            key_weight,
            value_weight,
            sums,
            LATE,
            1,
        )
        grad_inputs = in_order(grad_in[:local_len], other_in)
    else:

        def join(partial):
            far = lax.ppermute(partial[tokens_here:], "seq", beside)
            return (partial[:tokens_here].astype(jnp.float32) + far.astype(jnp.float32)).astype(low)

        def reduced(partial):
            piece = lax.psum_scatter(partial, ("dp", "seq"), scatter_dimension=0, tiled=True)
            return lax.all_gather(piece, "seq", axis=0, tiled=True).astype(jnp.float32)

        grad_q, grad_k, grad_v = attend_back(*back_args)
        grads = (grad_q, join(grad_k), join(grad_v))
        weights = (query_weight, key_weight, value_weight)
        _, norm_one_back = jax.vjp(
            norm_apply, both_in.astype(jnp.float32), first_gain, first_shift
        )
        grad_in_norm, grad_first_gain, grad_first_shift = norm_one_back(
            sum(dot(grad, weight, NT) for grad, weight in zip(grads, weights))
        )
        late = [jnp.sum(item, axis=0, dtype=jnp.float32) for item in (grads[0], grads[2])]
        packed = jnp.concatenate([sums, jnp.stack([grad_first_gain, grad_first_shift, *late])])
        packed = lax.psum(packed, ("dp", "seq"))
        result = give_back(stream)
        grad_inputs = give_back((grad_hidden + grad_in_norm).astype(low))
        sums_early = [reduced(item) for item in grads_early]
        sums_late = [reduced(dot(normed_one_low, grad, TN).astype(low)) for grad in grads]
    summed_outer, summed_inner, summed_output = sums_early
    summed_query, summed_key, summed_value = sums_late
    inner_rows = inner_weight.shape[1] // width
    grad_inner_bias = packed[:inner_rows].reshape(-1)
    tail = packed[inner_rows:]
    denominator = tail[3, 0] * width
    stream_scale = jnp.sqrt(jnp.sum(tail[0]) / denominator)
    attention_scale = jnp.sqrt(jnp.sum(tail[1]) / denominator)
    feedforward_scale = jnp.sqrt(jnp.sum(tail[2]) / denominator)
    return (
        result,
        grad_inputs,
        tail[8],
        tail[9],
        summed_query,
        tail[10],
        summed_key,
        summed_value,
        tail[11],
        summed_output,
        tail[4],
        tail[5],
        tail[6],
        summed_inner,
        grad_inner_bias,
        summed_outer,
        tail[7],
        stream_scale,
        attention_scale,
        feedforward_scale,
    )


def solution(mesh):
    return jax.shard_map(
        local,
        mesh=mesh,
        in_specs=(
            P("dp", "seq", None),
            P("dp"),
            P(),
            P(),
            P(),
            P(),
            P(),
            P(),
            P(),
            P(),
            P(),
            P(),
            P(),
            P(),
            P(),
            P(),
            P(),
            P("dp", "seq", None),
        ),
        out_specs=(
            P("dp", "seq", None),
            P("dp", "seq", None),
            P(),
            P(),
            P("dp", None),
            P(),
            P("dp", None),
            P("dp", None),
            P(),
            P("dp", None),
            P(),
            P(),
            P(),
            P("dp", None),
            P(),
            P("dp", None),
            P(),
            P(),
            P(),
            P(),
        ),
        check_vma=False,
    )
```
